128 devices in a mesh: row: 16 (over x, z_hi, core), col: 8 (over y, z_lo).
Axes of the slice: x: 4, y: 4, z: 4 (z_hi: 2, z_lo: 2; z = z_hi * 2 + z_lo), core: 2. Of those that a mesh axis runs over, the one named last changes fastest.
Arguments:
- tile_values: bfloat16 [256, 8, 4, 128, 128], P(('row', 'col')), may hold values from 0 to 1
- tile_columns: int32 [256, 8, 4], P(('row', 'col')), may hold values from -1 to 255, as said below
- owner_map: int32 [256], replicated, may hold values from 0 to 255, as said below
- section_rows: int32 [2], replicated, may hold values from 0 to 15, as said below
Outputs:
- inflated: bfloat16 [32768, 12288], P('row', 'col')
The draws below stay inside these ranges and needn't reach their ends.
Inputs may be any that keep to these rules, and one draw needn't show every extreme that they name: `tile_columns`: in each tile row and block-column b, the first 1 to 4 slots name distinct tile columns within b * 32 to b * 32 + 31 and the remaining slots hold -1; some tile row uses all 4 slots. A permutation of the tile rows; of the tile rows t in each aligned group of 16, exactly 1 have owner_map[t] in each block-row's range of 16 positions. `section_rows`: distinct block-rows; the last block-row is always one of them.
All inputs are finite; a program needn't handle non-finite values.
Results may differ from the reference program's by a relative error of at most 0.001.
Values may be sent and summed in bfloat16 or wider, within the bound.
A program may use at most 128 MiB of HBM per device.

```python
import jax
import jax.numpy as jnp
from jax import lax

TILE = 128
KB = 4
SLAB = 12
SECTIONS = 2
TILES = 256
BLOCK_ROWS = 16
BLOCK_COLS = 32
SHARE = 1
N_ROW = 16
N_COL = 8


def draw_tile_columns(key, part):
    first_key, second_key = jax.random.split(key)
    row_keys = jax.random.split(first_key, TILES * N_COL)
    picks = jax.vmap(lambda one_key: jax.random.permutation(one_key, BLOCK_COLS)[:KB])(row_keys)
    picks = picks.reshape(TILES, N_COL, KB).astype(jnp.int32)
    offsets = (jnp.arange(N_COL, dtype=jnp.int32) * BLOCK_COLS)[None, :, None]
    counts = jax.random.randint(second_key, (TILES, N_COL), 1, KB + 1).astype(jnp.int32)
    counts = counts.at[0, 0].set(KB)
    slot_number = jnp.arange(KB, dtype=jnp.int32)[None, None, :]
    return jnp.where(slot_number < counts[..., None], picks + offsets, -1).astype(jnp.int32)


def draw_owner_map(key, part):
    first_key, second_key = jax.random.split(key)
    blocks = TILES // BLOCK_ROWS
    position = jnp.arange(TILES, dtype=jnp.int32)
    base = jnp.tile(jnp.repeat(jnp.arange(blocks, dtype=jnp.int32), SHARE), blocks)
    shuffle = jax.random.permutation(first_key, TILES).astype(jnp.int32)
    within = jnp.argsort(position // BLOCK_ROWS * TILES + shuffle)
    group_of = base[within]
    by_group = jnp.argsort(group_of * TILES + position).astype(jnp.int32)
    shuffle_two = jax.random.permutation(second_key, TILES).astype(jnp.int32)
    sources = jnp.argsort(position // BLOCK_ROWS * TILES + shuffle_two)
    return jnp.zeros((TILES,), jnp.int32).at[sources].set(by_group)


def draw_section_rows(key, part):
    first_key, second_key = jax.random.split(key)
    block_count = TILES // BLOCK_ROWS
    others = jax.random.permutation(first_key, block_count - 1)[:SECTIONS - 1].astype(jnp.int32)
    chosen = jnp.concatenate([jnp.full((1,), block_count - 1, jnp.int32), others])
    return jax.random.permutation(second_key, chosen).astype(jnp.int32)


def level_of(rng, extent, shards, least, largest):
    factor_of, own = 1.0, jax.random.fold_in(rng, 6)
    for dim, blocks in shards:
        draws = jnp.exp(jax.random.uniform(jax.random.fold_in(own, dim), (blocks,), jnp.float32, least / len(shards), largest / len(shards)))
        factor_of = factor_of * jnp.repeat(draws, extent[dim] // blocks).reshape([-1 if axis == dim else 1 for axis in range(len(extent))])
    return factor_of


def setup_inputs(seed: int = 0) -> dict:
    streams_of = jax.random.split(jax.random.key(seed), 5)
    return {
        "tile_values": jnp.clip(1.0 * jax.random.uniform(streams_of[0], (TILES, N_COL, KB, TILE, TILE), jnp.float32) ** level_of(streams_of[0], (TILES, N_COL, KB, TILE, TILE), ((0, 128),), -0.2, 0.2), 0.0, 1.0).astype(jnp.bfloat16),
        "tile_columns": draw_tile_columns(jax.random.fold_in(streams_of[4], 71), 0),
        "owner_map": draw_owner_map(jax.random.fold_in(streams_of[4], 71), 0),
        "section_rows": draw_section_rows(jax.random.fold_in(streams_of[4], 71), 0),
    }


def densify(values_in, columns_in, first_col):
    relative = columns_in - first_col
    picker = (relative[..., None] == jnp.arange(SLAB, dtype=jnp.int32)).astype(jnp.float32)
    spread = jnp.einsum("nkab,nkj->najb", values_in.astype(jnp.float32), picker)
    return spread.astype(jnp.bfloat16).reshape(values_in.shape[0], TILE, SLAB * TILE)


def reference(tile_values, tile_columns, owner_map, section_rows):
    tile_count = owner_map.shape[0]
    rows_block = tile_count // N_ROW
    cols_block = tile_count // N_COL
    inverse = jnp.argsort(owner_map).astype(jnp.int32)
    grid_values = tile_values[inverse]
    grid_columns = tile_columns[inverse]
    slot_values = []
    slot_targets = []
    for section in range(SECTIONS):
        section_row = section_rows[section]
        source_col = (section_row * N_COL // N_ROW).astype(jnp.int32)
        panel_vals = jnp.take(grid_values, source_col, axis=1)
        panel_cols = jnp.take(grid_columns, source_col, axis=1)
        relative = panel_cols - section_row * rows_block
        inside = (relative >= 0) & (relative < rows_block)
        slot_targets.append(jnp.where(inside, panel_cols, 0).astype(jnp.int32))
        slot_values.append(panel_vals * inside[..., None, None].astype(jnp.bfloat16))
    all_values = jnp.concatenate(slot_values, axis=1)
    all_targets = jnp.concatenate(slot_targets, axis=1)
    pieces = []
    for block_col in range(N_COL):
        slab_dense = densify(grid_values[:, block_col], grid_columns[:, block_col], block_col * cols_block)

        def one_row(row_item):
            tiles, where_from = row_item
            picked = slab_dense[where_from]
            return jnp.einsum("kab,kbn->an", tiles.astype(jnp.float32), picked.astype(jnp.float32))

        expanded = lax.map(one_row, (all_values, all_targets))
        squares = (expanded * expanded).reshape(tile_count * TILE, SLAB * TILE)
        column_total = jnp.sum(squares, axis=0)
        factor = (tile_count * TILE) / (column_total + 1e-6)
        pieces.append((squares * factor).astype(jnp.bfloat16))
    return jnp.concatenate(pieces, axis=1)
```

```python
import functools

import jax
import jax.numpy as jnp
from jax import lax
from jax.experimental import pallas as pl
from jax.experimental.pallas import tpu as pltpu
from jax.sharding import PartitionSpec as P

TILE = 128
KB = 4
SLAB = 12
SECTIONS = 2
ROWS = 16
COLS = 8
BLOCK_COLS = 32
STRIP = TILE // COLS
ENTRIES = SECTIONS * KB
PANEL = SECTIONS * ROWS
FAST = (5, 64, 6)
FULL = (8, 128, 8)
MESH = pl.DeviceIdType.MESH
VMEM = pl.BlockSpec(memory_space=pltpu.VMEM)
SMEM = pl.BlockSpec(memory_space=pltpu.SMEM)
ANY = pl.BlockSpec(memory_space=pl.ANY)
BIG = 60 << 20


def params(**kw):
    return pltpu.CompilerParams(vmem_limit_bytes=BIG, **kw)


def prep_kernel(cap, owner, sections, cols, where, send_row, row_from, panel_from, picks):
    r, c = where[0], where[1]
    sec0, sec1 = sections[0], sections[1]

    def per_group(g, _):
        def per_row(j, _):
            block = owner[g * ROWS + j] // ROWS

            @pl.when(block == r)
            def _():
                row_from[g] = j

            @pl.when(block == sec0)
            def _():
                panel_from[g] = j

            @pl.when(block == sec1)
            def _():
                panel_from[ROWS + g] = j

            return 0

        return lax.fori_loop(0, ROWS, per_row, 0)

    lax.fori_loop(0, ROWS, per_group, 0)

    def per_own(j, _):
        send_row[owner[r * ROWS + j] // ROWS] = j
        return 0

    lax.fori_loop(0, ROWS, per_own, 0)
    wanted = []
    for i in range(2):
        block = owner[r * ROWS + c * 2 + i] // ROWS
        wanted.append((block == sec0) | (block == sec1))

    def per_block(b, _):
        for m in range(cap):
            picks[b * cap + m] = 0
        count = jnp.int32(0)
        for i in range(2):
            for k in range(KB):
                rel = cols[i * BLOCK_COLS + b * KB + k] - b * BLOCK_COLS
                take = wanted[i] & (rel >= 0) & (rel < SLAB)

                @pl.when(take & (count < cap))
                def _():
                    picks[b * cap + count] = i * KB + k

                count = count + take.astype(jnp.int32)
        return 0

    lax.fori_loop(0, COLS, per_block, 0)


def prep(cap, owner, sections, cols, where):
    i32 = jnp.int32
    return pl.pallas_call(
        functools.partial(prep_kernel, cap),
        out_shape=(
            jax.ShapeDtypeStruct((ROWS,), i32),
            jax.ShapeDtypeStruct((ROWS,), i32),
            jax.ShapeDtypeStruct((2 * ROWS,), i32),
            jax.ShapeDtypeStruct((COLS * cap,), i32),
        ),
        in_specs=[SMEM] * 4,
        out_specs=(SMEM,) * 4,
    )(owner, sections, cols, where)


def spread_kernel(
    cap, tv, idx, sections, send_row, picks,
    strips, cand, lists,
    left_out, left_in, right_out, row_out,
    s_idx, r_idx, s_left, r_left, s_right, r_right, s_list, r_list, s_row, r_row,
):
    r, c = lax.axis_index("row"), lax.axis_index("col")
    barrier = pltpu.get_barrier_semaphore()
    for d in range(1, COLS):
        pl.semaphore_signal(barrier, inc=1, device_id={"col": (c + d) % COLS}, device_id_type=MESH)
    for d in range(1, ROWS):
        pl.semaphore_signal(barrier, inc=1, device_id={"row": (r + d) % ROWS}, device_id_type=MESH)
    for i in range(2):
        for s in range(SECTIONS):
            source = sections[s] // 2
            for k in range(KB):
                for h in range(COLS):
                    left_out[h, i * ENTRIES + s * KB + k] = tv[
                        i, source * KB + k, h * STRIP : (h + 1) * STRIP, :
                    ]

    def pack(b, _):
        for m in range(cap):
            e = picks[b * cap + m]
            right_out[b, m] = tv[e // KB, b * KB + e % KB]
        return 0

    lax.fori_loop(0, COLS, pack, 0)
    lists[r, c] = idx[...]
    left_in[c] = left_out[c]
    cand[c] = right_out[c]
    pl.semaphore_wait(barrier, COLS - 1 + ROWS - 1)

    idx_copies, left_copies, right_copies = [], [], []
    for d in range(1, COLS):
        to = (c + d) % COLS
        copy = pltpu.make_async_remote_copy(
            idx, lists.at[r, c], s_idx.at[d], r_idx.at[d], device_id={"col": to}, device_id_type=MESH
        )
        copy.start()
        idx_copies.append(copy)
    for d in range(1, COLS):
        to = (c + d) % COLS
        copy = pltpu.make_async_remote_copy(
            left_out.at[to], left_in.at[c], s_left.at[d], r_left.at[d],
            device_id={"col": to}, device_id_type=MESH,
        )
        copy.start()
        left_copies.append(copy)
    for d in range(1, COLS):
        to = (c + d) % COLS
        copy = pltpu.make_async_remote_copy(
            right_out.at[to], cand.at[c], s_right.at[d], r_right.at[d],
            device_id={"col": to}, device_id_type=MESH,
        )
        copy.start()
        right_copies.append(copy)
    for copy in idx_copies:
        copy.wait_recv()
    list_copies = []
    for d in range(1, ROWS):
        to = (r + d) % ROWS
        copy = pltpu.make_async_remote_copy(
            lists.at[r], lists.at[r], s_list.at[d], r_list.at[d],
            device_id={"row": to}, device_id_type=MESH,
        )
        copy.start()
        list_copies.append(copy)
    for copy in left_copies:
        copy.wait_recv()

    def reorder(t, _):
        j = send_row[t]
        for e in range(ENTRIES):
            row_out[t, e] = left_in[j // 2, (j % 2) * ENTRIES + e]
        return 0

    lax.fori_loop(0, ROWS, reorder, 0)
    strips[r] = row_out[r]
    row_copies = []
    for d in range(1, ROWS):
        to = (r + d) % ROWS
        copy = pltpu.make_async_remote_copy(
            row_out.at[to], strips.at[r], s_row.at[d], r_row.at[d],
            device_id={"row": to}, device_id_type=MESH,
        )
        copy.start()
        row_copies.append(copy)
    for copy in list_copies + row_copies + right_copies:
        copy.wait_recv()
    for copy in idx_copies + left_copies + right_copies + list_copies + row_copies:
        copy.wait_send()


def spread(cap, collective_id, tv, idx, sections, send_row, picks):
    bf = jnp.bfloat16
    dma = pltpu.SemaphoreType.DMA
    return pl.pallas_call(
        functools.partial(spread_kernel, cap),
        out_shape=(
            jax.ShapeDtypeStruct((ROWS, ENTRIES, STRIP, TILE), bf),
            jax.ShapeDtypeStruct((COLS, cap, TILE, TILE), bf),
            jax.ShapeDtypeStruct((ROWS, COLS, 1, TILE), jnp.int32),
        ),
        in_specs=[VMEM, VMEM, SMEM, SMEM, SMEM],
        out_specs=(VMEM, VMEM, VMEM),
        scratch_shapes=[
            pltpu.VMEM((COLS, 2 * ENTRIES, STRIP, TILE), bf),
            pltpu.VMEM((COLS, 2 * ENTRIES, STRIP, TILE), bf),
            pltpu.VMEM((COLS, cap, TILE, TILE), bf),
            pltpu.VMEM((ROWS, ENTRIES, STRIP, TILE), bf),
        ]
        + [dma((COLS,))] * 6
        + [dma((ROWS,))] * 4,
        compiler_params=params(collective_id=collective_id, has_side_effects=True),
    )(tv, idx, sections, send_row, picks)


def lists_kernel(
    caps, lists, owner, sections, where, row_from, panel_from,
    keep_left, row_left, inner_left, keep_right, start, count, col_right, totals,
):
    cap, cap_left, cap_group = caps
    r, c = where[0], where[1]
    for m in range(cap_group):
        keep_right[m] = 0

    def clear(m, _):
        keep_left[m] = 0
        return 0

    lax.fori_loop(0, cap_left, clear, 0)

    def left(g, n):
        j = row_from[g]
        line = g * COLS + j // 2
        base = (j % 2) * BLOCK_COLS
        p = owner[g * ROWS + j] - r * ROWS
        for s in range(SECTIONS):
            sec = sections[s]
            for k in range(KB):
                rel = lists[line, base + (sec // 2) * KB + k] - sec * ROWS
                take = (rel >= 0) & (rel < ROWS)

                @pl.when(take)
                def _():
                    keep_left[n] = g * ENTRIES + s * KB + k
                    row_left[n] = p
                    inner_left[n] = s * ROWS + rel

                n = n + take.astype(jnp.int32)
        return n

    totals[0] = lax.fori_loop(0, ROWS, left, jnp.int32(0))

    def right(g, _):
        a, b = panel_from[g], panel_from[ROWS + g]
        swap = b < a
        n = jnp.int32(0)
        used = jnp.int32(0)
        for order in range(2):
            s = (swap if order == 0 else jnp.logical_not(swap)).astype(jnp.int32)
            j = jnp.where(s == 0, a, b)
            other = jnp.where(s == 0, b, a)
            if order == 1:
                used = jnp.where(j // 2 == other // 2, used, 0)
            sec = sections[s]
            q = s * ROWS + owner[g * ROWS + j] - sec * ROWS
            line = g * COLS + j // 2
            base = (j % 2) * BLOCK_COLS + c * KB
            start[q] = g * cap_group + n
            first = n
            for k in range(KB):
                rel = lists[line, base + k] - c * BLOCK_COLS
                take = (rel >= 0) & (rel < SLAB)

                @pl.when(take)
                def _():
                    col_right[g * cap_group + n] = rel

                @pl.when(take & (g == r))
                def _():
                    keep_right[n] = (j // 2) * cap + used

                n = n + take.astype(jnp.int32)
                used = used + take.astype(jnp.int32)
            count[q] = n - first
        return 0

    lax.fori_loop(0, ROWS, right, 0)


def make_lists(caps, lists, owner, sections, where, row_from, panel_from):
    cap, cap_left, cap_group = caps
    sizes = (cap_left, cap_left, cap_left, cap_group, PANEL, PANEL, ROWS * cap_group, 1)
    return pl.pallas_call(
        functools.partial(lists_kernel, caps),
        out_shape=tuple(jax.ShapeDtypeStruct((n,), jnp.int32) for n in sizes),
        in_specs=[SMEM] * 6,
        out_specs=(SMEM,) * len(sizes),
    )(lists, owner, sections, where, row_from, panel_from)


def gather_kernel(caps, strips, cand, keep_left, keep_right, left, right, send, recv):
    cap, cap_left, cap_group = caps
    r, c = lax.axis_index("row"), lax.axis_index("col")
    cut = cap_left * 9 // 16
    a_part, b_part = (0, cut), (cut, cap_left)
    halves = lambda part: ((part[0], (part[0] + part[1]) // 2), ((part[0] + part[1]) // 2, part[1]))
    g_part = (0, cap_group)
    zp = {"col": c + 1 - 2 * (c % 2)}
    yn, yb = {"col": (c + 2) % COLS}, {"col": (c + COLS - 2) % COLS}
    core = {"row": r + 1 - 2 * (r % 2)}
    zh = {"row": (r // 4) * 4 + (r + 2) % 4}
    xn, xb = {"row": (r + 4) % ROWS}, {"row": (r + ROWS - 4) % ROWS}
    barrier = pltpu.get_barrier_semaphore()
    for peer in (zp, yn, yb, core, zh, xn, xb):
        pl.semaphore_signal(barrier, inc=1, device_id=peer, device_id_type=MESH)

    def pack_left(m, _):
        e = keep_left[m]
        left[c, m] = strips[e // ENTRIES, e % ENTRIES]
        return 0

    lax.fori_loop(0, cap_left, pack_left, 0)

    def pack_right(m, _):
        e = keep_right[m]
        right[r, m] = cand[e // cap, e % cap]
        return 0

    lax.fori_loop(0, cap_group, pack_right, 0)
    pl.semaphore_wait(barrier, 7)

    started = []

    def go(buf, origin, part, to):
        n = len(started)
        piece = buf.at[origin, pl.ds(part[0], part[1] - part[0])]
        copy = pltpu.make_async_remote_copy(
            piece, piece, send.at[n], recv.at[n], device_id=to, device_id_type=MESH
        )
        copy.start()
        started.append(copy)
        return copy

    cz = c + 1 - 2 * (c % 2)
    c_m, c_p, c_o = (c + COLS - 2) % COLS, (c + 2) % COLS, (c + 4) % COLS
    z_m, z_p, z_o = (cz + COLS - 2) % COLS, (cz + 2) % COLS, (cz + 4) % COLS
    rz = (r // 4) * 4 + (r + 2) % 4
    r_m, r_p, r_o = (r + ROWS - 4) % ROWS, (r + 4) % ROWS, (r + 8) % ROWS
    q_m, q_p, q_o = (rz + ROWS - 4) % ROWS, (rz + 4) % ROWS, (rz + 8) % ROWS
    a1, a2 = halves(a_part)
    b1, b2 = halves(b_part)
    g1, g2 = halves(g_part)

    k1 = go(left, c, a_part, zp)
    k21 = go(right, r, g_part, zh)
    k10 = go(left, c, b_part, yn)
    k11 = go(left, c, b_part, yb)
    k22 = go(right, r, g_part, xn)
    k23 = go(right, r, g_part, xb)
    k2 = go(left, c, a_part, yn)
    k3 = go(left, c, a_part, yb)
    k12 = go(left, c, b_part, zp)
    k20 = go(right, r, g_part, core)
    done = []

    def arrived(copy):
        copy.wait_recv()
        done.append(copy)

    arrived(k10)
    k13 = go(left, c_m, b1, yn)
    k14 = go(left, c_m, b_part, zp)
    arrived(k11)
    k15 = go(left, c_p, b2, yb)
    k16 = go(left, c_p, b_part, zp)
    arrived(k1)
    k4 = go(left, cz, a_part, yn)
    k5 = go(left, cz, a_part, yb)
    arrived(k21)
    k24 = go(right, rz, g_part, xn)
    k25 = go(right, rz, g_part, xb)
    k26 = go(right, rz, g_part, core)
    arrived(k22)
    k27 = go(right, r_m, g1, xn)
    k28 = go(right, r_m, g_part, core)
    arrived(k23)
    k29 = go(right, r_p, g2, xb)
    k30 = go(right, r_p, g_part, core)
    arrived(k2)
    k6 = go(left, c_m, a1, yn)
    arrived(k3)
    k7 = go(left, c_p, a2, yb)
    arrived(k13)
    k17 = go(left, c_o, b1, zp)
    arrived(k15)
    k18 = go(left, c_o, b2, zp)
    arrived(k24)
    k31 = go(right, q_m, g1, xn)
    k32 = go(right, q_m, g_part, core)
    arrived(k25)
    k33 = go(right, q_p, g2, xb)
    k34 = go(right, q_p, g_part, core)
    arrived(k4)
    k8 = go(left, z_m, a1, yn)
    arrived(k5)
    k9 = go(left, z_p, a2, yb)
    arrived(k27)
    k35 = go(right, r_o, g1, core)
    arrived(k29)
    k36 = go(right, r_o, g2, core)
    arrived(k31)
    k37 = go(right, q_o, g1, core)
    arrived(k33)
    k38 = go(right, q_o, g2, core)
    for copy in started:
        if not any(copy is other for other in done):
            copy.wait_recv()
    for copy in started:
        copy.wait_send()


COPIES = 37


def gather(caps, collective_id, strips, cand, keep_left, keep_right):
    cap, cap_left, cap_group = caps
    bf = jnp.bfloat16
    return pl.pallas_call(
        functools.partial(gather_kernel, caps),
        out_shape=(
            jax.ShapeDtypeStruct((COLS, cap_left, STRIP, TILE), bf),
            jax.ShapeDtypeStruct((ROWS, cap_group, TILE, TILE), bf),
        ),
        in_specs=[VMEM, VMEM, SMEM, SMEM],
        out_specs=(VMEM, VMEM),
        scratch_shapes=[pltpu.SemaphoreType.DMA((COPIES,))] * 2,
        compiler_params=params(collective_id=collective_id, has_side_effects=True),
    )(strips, cand, keep_left, keep_right)


OUT_TILES = ROWS * SLAB
UNROLL = 4


def product_kernel(
    caps, left, right, row_left, inner_left, start, count, col_right, totals,
    squares, slot_of, sums,
    acc, job_left, job_right, job_slot, job_first, out_of, part, sem,
):
    cap, cap_left, cap_group = caps

    def clear(o, _):
        slot_of[o] = -1
        return 0

    lax.fori_loop(0, OUT_TILES, clear, 0)

    def per_left(m, carry):
        p, q = row_left[m], inner_left[m]
        base = start[q]

        def per_right(t, carry):
            n, touched = carry
            o = p * SLAB + col_right[base + t]
            old = slot_of[o]
            fresh = old < 0
            slot = jnp.where(fresh, touched, old)
            job_left[n] = m
            job_right[n] = base + t
            job_slot[n] = slot
            job_first[n] = fresh.astype(jnp.int32)
            slot_of[o] = slot
            out_of[slot] = o
            return n + 1, touched + fresh.astype(jnp.int32)

        return lax.fori_loop(0, count[q], per_right, carry)

    n, touched = lax.fori_loop(0, totals[0], per_left, (jnp.int32(0), jnp.int32(0)))
    for u in range(UNROLL):
        job_left[n + u] = 0
        job_right[n + u] = 0
        job_slot[n + u] = OUT_TILES
        job_first[n + u] = 1

    def multiply(g, _):
        results = []
        for u in range(UNROLL):
            a = left[:, job_left[g * UNROLL + u]].reshape(TILE, TILE)
            e = job_right[g * UNROLL + u]
            b = right[e // cap_group, e % cap_group]
            results.append(jnp.dot(a, b, preferred_element_type=jnp.float32))
        for u in range(UNROLL):
            slot = job_slot[g * UNROLL + u]
            keep = (1 - job_first[g * UNROLL + u]).astype(jnp.float32)
            old = acc[slot]
            acc[slot] = results[u] + jnp.where(keep > 0, old, 0.0)
        return 0

    lax.fori_loop(0, (n + UNROLL - 1) // UNROLL, multiply, 0)
    part[...] = jnp.zeros_like(part)

    def finish(slot, _):
        value = acc[slot]
        value = value * value
        acc[slot] = value
        pltpu.make_async_copy(acc.at[slot], squares.at[slot], sem).start()
        col = out_of[slot] % SLAB
        part[col] += value.reshape(TILE // 8, 8, TILE).sum(axis=0)
        return 0

    lax.fori_loop(0, touched, finish, 0)
    sums[...] = part[...].sum(axis=1)

    def drain(slot, _):
        pltpu.make_async_copy(acc.at[slot], squares.at[slot], sem).wait()
        return 0

    lax.fori_loop(0, touched, drain, 0)


def products(caps, left, right, row_left, inner_left, start, count, col_right, totals):
    cap, cap_left, cap_group = caps
    jobs = cap_left * KB + UNROLL
    f32, i32 = jnp.float32, jnp.int32
    return pl.pallas_call(
        functools.partial(product_kernel, caps),
        out_shape=(
            jax.ShapeDtypeStruct((OUT_TILES, TILE, TILE), f32),
            jax.ShapeDtypeStruct((OUT_TILES,), i32),
            jax.ShapeDtypeStruct((ROWS, TILE), f32),
        ),
        in_specs=[VMEM, VMEM] + [SMEM] * 6,
        out_specs=(ANY, SMEM, VMEM),
        scratch_shapes=[pltpu.VMEM((OUT_TILES + 1, TILE, TILE), f32)]
        + [pltpu.SMEM((jobs,), i32)] * 4
        + [pltpu.SMEM((OUT_TILES,), i32), pltpu.VMEM((ROWS, 8, TILE), f32), pltpu.SemaphoreType.DMA],
        compiler_params=params(),
    )(left, right, row_left, inner_left, start, count, col_right, totals)


def total_kernel(mine, out, parts, send, recv):
    r = lax.axis_index("row")
    barrier = pltpu.get_barrier_semaphore()
    for d in range(1, ROWS):
        pl.semaphore_signal(barrier, inc=1, device_id={"row": (r + d) % ROWS}, device_id_type=MESH)
    parts[r] = mine[...]
    pl.semaphore_wait(barrier, ROWS - 1)
    copies = []
    for d in range(1, ROWS):
        copy = pltpu.make_async_remote_copy(
            mine, parts.at[r], send.at[d], recv.at[d],
            device_id={"row": (r + d) % ROWS}, device_id_type=MESH,
        )
        copy.start()
        copies.append(copy)
    for copy in copies:
        copy.wait_recv()
    out[...] = parts[...].sum(axis=0)
    for copy in copies:
        copy.wait_send()


def total(collective_id, mine):
    return pl.pallas_call(
        total_kernel,
        out_shape=jax.ShapeDtypeStruct((ROWS, TILE), jnp.float32),
        in_specs=[VMEM],
        out_specs=VMEM,
        scratch_shapes=[
            pltpu.VMEM((ROWS, ROWS, TILE), jnp.float32),
            pltpu.SemaphoreType.DMA((ROWS,)),
            pltpu.SemaphoreType.DMA((ROWS,)),
        ],
        compiler_params=params(collective_id=collective_id, has_side_effects=True),
    )(mine)


def write_kernel(squares, slot_of, totals, out, tiles, block, factor, in_sem, out_sem):
    count = float(ROWS * ROWS * TILE)
    factor[...] = count / (totals[...] + 1e-06)

    def fetch(o, _):
        slot = slot_of[o]

        @pl.when(slot >= 0)
        def _():
            pltpu.make_async_copy(squares.at[slot], tiles.at[o], in_sem).start()

        return 0

    lax.fori_loop(0, OUT_TILES, fetch, 0)

    def got(o, _):
        @pl.when(slot_of[o] >= 0)
        def _():
            pltpu.make_async_copy(squares.at[0], tiles.at[o], in_sem).wait()

        return 0

    lax.fori_loop(0, OUT_TILES, got, 0)

    def per_row(p, _):
        for col in range(SLAB):
            slot = slot_of[p * SLAB + col]

            @pl.when(slot >= 0)
            def _():
                value = tiles[p * SLAB + col] * factor[col : col + 1, :]
                block[p, :, col * TILE : (col + 1) * TILE] = value.astype(jnp.bfloat16)

            @pl.when(slot < 0)
            def _():
                block[p, :, col * TILE : (col + 1) * TILE] = jnp.zeros((TILE, TILE), jnp.bfloat16)

        pltpu.make_async_copy(block.at[p], out.at[pl.ds(p * TILE, TILE)], out_sem).start()
        return 0

    lax.fori_loop(0, ROWS, per_row, 0)

    def drain(p, _):
        pltpu.make_async_copy(block.at[p], out.at[pl.ds(p * TILE, TILE)], out_sem).wait()
        return 0

    lax.fori_loop(0, ROWS, drain, 0)


def write(squares, slot_of, totals):
    return pl.pallas_call(
        write_kernel,
        out_shape=jax.ShapeDtypeStruct((ROWS * TILE, SLAB * TILE), jnp.bfloat16),
        in_specs=[ANY, SMEM, VMEM],
        out_specs=ANY,
        scratch_shapes=[
            pltpu.VMEM((OUT_TILES, TILE, TILE), jnp.float32),
            pltpu.VMEM((ROWS, TILE, SLAB * TILE), jnp.bfloat16),
            pltpu.VMEM((ROWS, TILE), jnp.float32),
            pltpu.SemaphoreType.DMA,
            pltpu.SemaphoreType.DMA,
        ],
        compiler_params=params(),
    )(squares, slot_of, totals)


def overflow(lists, owner, sections):
    tiles = owner.shape[0]
    cols = lists[:, :, 0, : 2 * BLOCK_COLS].reshape(tiles, COLS, KB)
    block = owner // ROWS
    panel = (block == sections[0]) | (block == sections[1])
    rel = cols - (jnp.arange(COLS, dtype=jnp.int32) * BLOCK_COLS)[None, :, None]
    slab = ((rel >= 0) & (rel < SLAB) & panel[:, None, None]).astype(jnp.int32).sum(axis=2)
    pairs = slab.reshape(tiles // 2, 2, COLS).sum(axis=1)
    groups = slab.reshape(ROWS, ROWS, COLS).sum(axis=1)
    inner = jnp.zeros((tiles,), jnp.int32)
    for s in range(SECTIONS):
        off = cols - sections[s] * ROWS
        inner = inner + ((off >= 0) & (off < ROWS)).astype(jnp.int32).sum(axis=(1, 2))
    mine = (block[:, None] == jnp.arange(ROWS, dtype=jnp.int32)[None, :]).astype(jnp.int32)
    rows = (mine * inner[:, None]).sum(axis=0)
    return (pairs.max() > FAST[0]) | (rows.max() > FAST[1]) | (groups.max() > FAST[2])


def per_device(tile_values, tile_columns, owner_map, section_rows):
    where = jnp.stack([lax.axis_index("row"), lax.axis_index("col")]).astype(jnp.int32)
    flat = tile_columns.reshape(-1)
    idx = jnp.pad(flat, (0, TILE - flat.shape[0])).reshape(1, TILE)
    tv = tile_values.reshape(2, COLS * KB, TILE, TILE)

    def first(caps, collective_id):
        send_row, row_from, panel_from, picks = prep(caps[0], owner_map, section_rows, flat, where)
        strips, cand, lists = spread(caps[0], collective_id, tv, idx, section_rows, send_row, picks)
        return strips, cand, lists, row_from, panel_from

    def rest(caps, ids, strips, cand, lists, row_from, panel_from):
        made = make_lists(
            caps, lists.reshape(ROWS * COLS, TILE), owner_map, section_rows, where, row_from, panel_from
        )
        keep_left, row_left, inner_left, keep_right, start, count, col_right, totals = made
        left, right = gather(caps, ids[0], strips, cand, keep_left, keep_right)
        squares, slot_of, sums = products(
            caps, left, right, row_left, inner_left, start, count, col_right, totals
        )
        return write(squares, slot_of, total(ids[1], sums))

    got = first(FAST, 0)
    flag = overflow(got[2], owner_map, section_rows)
    return lax.cond(
        flag,
        lambda *_: rest(FULL, (4, 5), *first(FULL, 3)),
        lambda *args: rest(FAST, (1, 2), *args),
        *got,
    )


def solution(mesh):
    both = ("row", "col")
    in_specs = (P(both, None, None, None, None), P(both, None, None), P(), P())
    return jax.shard_map(
        per_device, mesh=mesh, in_specs=in_specs, out_specs=P("row", "col"), check_vma=False
    )
```

```python
import functools

import jax
import jax.numpy as jnp
from jax import lax
from jax.experimental import pallas as pl
from jax.experimental.pallas import tpu as pltpu
from jax.sharding import PartitionSpec as P

TILE = 128
KB = 4
SLAB = 12
SECTIONS = 2
ROWS = 16
COLS = 8
BLOCK_COLS = 32
STRIP = TILE // COLS
ENTRIES = SECTIONS * KB
PANEL = SECTIONS * ROWS
FAST = (8, 56, 10, 16)
FULL = (16, 128, 16, 32)
MESH = pl.DeviceIdType.MESH
VMEM = pl.BlockSpec(memory_space=pltpu.VMEM)
SMEM = pl.BlockSpec(memory_space=pltpu.SMEM)
ANY = pl.BlockSpec(memory_space=pl.ANY)


def params(mib, **kw):
    return pltpu.CompilerParams(vmem_limit_bytes=mib << 20, **kw)


def prep_kernel(cap, owner, sections, cols, send_row, row_from, panel_from, picks, inverse):
    r, c = lax.axis_index("row"), lax.axis_index("col")

    def invert(g, _):
        for j in range(ROWS):
            inverse[owner[g * ROWS + j]] = g * ROWS + j
        return 0

    lax.fori_loop(0, ROWS, invert, 0)
    secs = [sections[0], sections[1]]
    for j in range(ROWS):
        send_row[owner[r * ROWS + j] >> 4] = j
        t = inverse[r * ROWS + j]
        row_from[t >> 4] = t & 15
        for s in range(SECTIONS):
            t = inverse[secs[s] * ROWS + j]
            panel_from[s * ROWS + (t >> 4)] = t & 15
    wanted = []
    for i in range(2):
        block = owner[r * ROWS + c * 2 + i] >> 4
        wanted.append((block == secs[0]) | (block == secs[1]))
    room = cap + 1

    def per_y(yd, _):
        for m in range(room):
            picks[yd * room + m] = 0
        count = jnp.int32(0)
        for i in range(2):
            for z in range(2):
                b = yd * 2 + z
                for k in range(KB):
                    rel = cols[i * BLOCK_COLS + b * KB + k] - b * BLOCK_COLS
                    take = wanted[i] & (rel >= 0) & (rel < SLAB)
                    picks[yd * room + count] = i * BLOCK_COLS + b * KB + k
                    count = jnp.minimum(count + take.astype(jnp.int32), cap)
        return 0

    lax.fori_loop(0, 4, per_y, 0)


def prep(cap, owner, sections, cols):
    i32 = jnp.int32
    return pl.pallas_call(
        functools.partial(prep_kernel, cap),
        out_shape=(
            jax.ShapeDtypeStruct((ROWS,), i32),
            jax.ShapeDtypeStruct((ROWS,), i32),
            jax.ShapeDtypeStruct((2 * ROWS,), i32),
            jax.ShapeDtypeStruct((4 * (cap + 1),), i32),
        ),
        in_specs=[SMEM] * 3,
        out_specs=(SMEM,) * 4,
        scratch_shapes=[pltpu.SMEM((ROWS * ROWS,), i32)],
    )(owner, sections, cols)


def iota(dim):
    return lax.broadcasted_iota(jnp.int32, (TILE, TILE), dim)


def picked(mask):
    return jnp.where(mask, 1.0, 0.0).astype(jnp.bfloat16)


def mm(a, b, dims=((1,), (0,))):
    return lax.dot_general(a, b, (dims, ((), ())), preferred_element_type=jnp.float32)


def counts_over(lists, owner, sections):
    cols = lists[...].reshape(TILE, TILE)
    line, lane = iota(0), iota(1)
    blocks = []
    for i in range(2):
        total = jnp.zeros((TILE, TILE), jnp.float32)
        for h in range(2):
            row = jnp.broadcast_to((owner[h : h + 1, :] >> 4).astype(jnp.float32), (TILE, TILE))
            choose = picked(lane + h * TILE == 2 * line + i)
            total = total + mm(choose, row.astype(jnp.bfloat16), ((1,), (1,)))
        blocks.append(total.astype(jnp.int32))
    mine = jnp.where(lane < BLOCK_COLS, blocks[0], blocks[1])
    sec0, sec1 = sections[0], sections[1]
    real = lane < 2 * BLOCK_COLS
    b = (lane & (BLOCK_COLS - 1)) >> 2
    rel = cols - b * BLOCK_COLS
    slab = picked(real & (rel >= 0) & (rel < SLAB) & ((mine == sec0) | (mine == sec1)))
    inner0 = (cols >= sec0 * ROWS) & (cols < sec0 * ROWS + ROWS)
    inner1 = (cols >= sec1 * ROWS) & (cols < sec1 * ROWS + ROWS)
    inner = picked(real & (inner0 | inner1))
    lane_b = (line & (BLOCK_COLS - 1)) >> 2
    to_y = picked((line < 2 * BLOCK_COLS) & ((lane_b >> 1) == lane))
    to_b = picked((line < 2 * BLOCK_COLS) & (lane_b == lane))
    per_y = mm(slab, to_y)
    per_b = mm(slab, to_b).astype(jnp.bfloat16)
    same_pair = picked(((line >> 4) == (lane >> 4)) & ((line & 1) == (lane & 1)))
    same_x = picked((line >> 5) == (lane >> 5))
    per_pair = mm(same_pair, per_b)
    per_x = mm(same_x, per_b)
    rows = jnp.zeros((TILE, TILE), jnp.float32)
    for i in range(2):
        own = picked((line >= i * BLOCK_COLS) & (line < (i + 1) * BLOCK_COLS))
        number = mm(inner, own).astype(jnp.bfloat16)
        rows = rows + mm(picked(blocks[i] == lane), number, ((0,), (0,)))
    over = per_y - FAST[0]
    over = jnp.maximum(over, rows - FAST[1])
    over = jnp.maximum(over, per_pair - FAST[2])
    over = jnp.maximum(over, per_x - FAST[3])
    return over


def spread_kernel(
    cap, tv, idx, owner, sections, send_row, picks,
    strips, cand, lists, over,
    left_out, left_in, right_out, row_out,
    s_idx, r_idx, s_left, r_left, s_right, r_right, s_core, r_core, s_list, r_list, s_row, r_row,
):
    r, c = lax.axis_index("row"), lax.axis_index("col")
    core, y, z = r % 2, c // 2, c % 2
    barrier = pltpu.get_barrier_semaphore()
    for d in range(1, COLS):
        pl.semaphore_signal(barrier, inc=1, device_id={"col": (c + d) % COLS}, device_id_type=MESH)
    for d in range(1, ROWS):
        pl.semaphore_signal(barrier, inc=1, device_id={"row": (r + d) % ROWS}, device_id_type=MESH)
    for i in range(2):
        for s in range(SECTIONS):
            source = sections[s] // 2
            for k in range(KB):
                for h in range(COLS):
                    left_out[h, i * ENTRIES + s * KB + k] = tv[
                        i * BLOCK_COLS + source * KB + k, h * STRIP : (h + 1) * STRIP, :
                    ]

    def pack(yd, _):
        for m in range(cap):
            right_out[yd, m] = tv[picks[yd * (cap + 1) + m]]
        return 0

    lax.fori_loop(0, 4, pack, 0)
    lists[r, c] = idx[...]
    left_in[c] = left_out[c]
    cand[core, y] = right_out[y]
    pl.semaphore_wait(barrier, COLS - 1 + ROWS - 1)

    idx_copies, left_copies, right_copies, core_copies = [], [], [], []
    for d in range(1, COLS):
        to = (c + d) % COLS
        copy = pltpu.make_async_remote_copy(
            idx, lists.at[r, c], s_idx.at[d], r_idx.at[d], device_id={"col": to}, device_id_type=MESH
        )
        copy.start()
        idx_copies.append(copy)
    for d in range(1, COLS):
        to = (c + d) % COLS
        copy = pltpu.make_async_remote_copy(
            left_out.at[to], left_in.at[c], s_left.at[d], r_left.at[d],
            device_id={"col": to}, device_id_type=MESH,
        )
        copy.start()
        left_copies.append(copy)
    for d in (2, 1, 3):
        to = (y + d) % 4
        copy = pltpu.make_async_remote_copy(
            right_out.at[to], cand.at[core, y], s_right.at[d], r_right.at[d],
            device_id={"col": to * 2 + z}, device_id_type=MESH,
        )
        copy.start()
        right_copies.append((d, copy))

    def to_core(src, origin, d):
        copy = pltpu.make_async_remote_copy(
            src, cand.at[core, origin], s_core.at[d], r_core.at[d],
            device_id={"row": r + 1 - 2 * core}, device_id_type=MESH,
        )
        copy.start()
        core_copies.append(copy)

    to_core(right_out.at[y], y, 0)
    for copy in idx_copies:
        copy.wait_recv()
    list_copies = []
    for d in range(1, ROWS):
        to = (r + d) % ROWS
        copy = pltpu.make_async_remote_copy(
            lists.at[r], lists.at[r], s_list.at[d], r_list.at[d],
            device_id={"row": to}, device_id_type=MESH,
        )
        copy.start()
        list_copies.append(copy)
    for copy in left_copies:
        copy.wait_recv()

    def reorder(t, _):
        j = send_row[t]
        for e in range(ENTRIES):
            row_out[t, e] = left_in[j // 2, (j % 2) * ENTRIES + e]
        return 0

    lax.fori_loop(0, ROWS, reorder, 0)
    strips[r] = row_out[r]
    row_copies = []
    for d in range(1, ROWS):
        to = (r + d) % ROWS
        copy = pltpu.make_async_remote_copy(
            row_out.at[to], strips.at[r], s_row.at[d], r_row.at[d],
            device_id={"row": to}, device_id_type=MESH,
        )
        copy.start()
        row_copies.append(copy)
    for copy in list_copies:
        copy.wait_recv()
    over[...] = counts_over(lists, owner, sections)
    for d, copy in right_copies:
        copy.wait_recv()
        origin = (y + 4 - d) % 4
        to_core(cand.at[core, origin], origin, d)
    for copy in row_copies + core_copies:
        copy.wait_recv()
    sent = [copy for _, copy in right_copies]
    for copy in idx_copies + left_copies + sent + core_copies + list_copies + row_copies:
        copy.wait_send()


def spread(cap, collective_id, tv, idx, owner, sections, send_row, picks):
    bf = jnp.bfloat16
    dma = pltpu.SemaphoreType.DMA
    return pl.pallas_call(
        functools.partial(spread_kernel, cap),
        out_shape=(
            jax.ShapeDtypeStruct((ROWS, ENTRIES, STRIP, TILE), bf),
            jax.ShapeDtypeStruct((2, 4, cap, TILE, TILE), bf),
            jax.ShapeDtypeStruct((ROWS, COLS, 1, TILE), jnp.int32),
            jax.ShapeDtypeStruct((TILE, TILE), jnp.float32),
        ),
        in_specs=[VMEM, VMEM, VMEM, SMEM, SMEM, SMEM],
        out_specs=(VMEM,) * 4,
        scratch_shapes=[
            pltpu.VMEM((COLS, 2 * ENTRIES, STRIP, TILE), bf),
            pltpu.VMEM((COLS, 2 * ENTRIES, STRIP, TILE), bf),
            pltpu.VMEM((4, cap, TILE, TILE), bf),
            pltpu.VMEM((ROWS, ENTRIES, STRIP, TILE), bf),
        ]
        + [dma((COLS,))] * 8
        + [dma((ROWS,))] * 4,
        compiler_params=params(20, collective_id=collective_id, has_side_effects=True),
    )(tv, idx, owner, sections, send_row, picks)


def lists_kernel(
    caps, lists, owner, sections, row_from, panel_from,
    keep_left, row_left, inner_left, here, there, keep, start, count, col_right, totals,
):
    cap_y, cap_left, cap_pair, cap_x = caps
    r, c = lax.axis_index("row"), lax.axis_index("col")
    x, zh = r >> 2, (r >> 1) & 1
    y, zl = c >> 1, c & 1
    secs = [sections[0], sections[1]]
    for m in range(cap_pair):
        here[m] = 0
        there[m] = 0
    for m in range(cap_x):
        keep[m] = 0

    def clear(m, _):
        for u in range(8):
            keep_left[m * 8 + u] = 0
        return 0

    lax.fori_loop(0, cap_left // 8, clear, 0)

    def left(g, n):
        j = row_from[g]
        line = g * COLS + (j >> 1)
        base = (j & 1) * BLOCK_COLS
        p = owner[g * ROWS + j] - r * ROWS
        for s in range(SECTIONS):
            for k in range(KB):
                rel = lists[line, base + (secs[s] >> 1) * KB + k] - secs[s] * ROWS
                keep_left[n] = g * ENTRIES + s * KB + k
                row_left[n] = p
                inner_left[n] = s * ROWS + rel
                n = n + ((rel >= 0) & (rel < ROWS)).astype(jnp.int32)
        return n

    totals[0] = lax.fori_loop(0, ROWS, left, jnp.int32(0))

    def ordered(g):
        a, b = panel_from[g], panel_from[ROWS + g]
        swap = (b < a).astype(jnp.int32)
        return ((swap, jnp.minimum(a, b)), (1 - swap, jnp.maximum(a, b)))

    def pairs(k2, carry):
        n_here, n_there = carry
        g = x * 4 + zh * 2 + k2
        used = jnp.int32(0)
        before = jnp.int32(-1)
        for s, j in ordered(g):
            source = j >> 1
            used = jnp.where(source == before, used, 0)
            before = source
            line = g * COLS + source
            base = (j & 1) * BLOCK_COLS
            near = (source & 1) == zl
            spot = k2 * 4 * cap_y + (source >> 1) * cap_y
            for z in range(2):
                mine = zl == z
                for k in range(KB):
                    b = y * 2 + z
                    rel = lists[line, base + b * KB + k] - b * BLOCK_COLS
                    ok = (rel >= 0) & (rel < SLAB)
                    take_here = (ok & near & mine).astype(jnp.int32)
                    take_there = (ok & near & jnp.logical_not(mine)).astype(jnp.int32)
                    at = jnp.minimum(spot + used, 8 * cap_y - 1)
                    here[n_here] = at
                    there[n_there] = at
                    n_here = n_here + take_here
                    n_there = n_there + take_there
                    used = used + ok.astype(jnp.int32)
        return n_here, n_there

    lax.fori_loop(0, 2, pairs, (jnp.int32(0), jnp.int32(0)))

    def per_x(xs, _):
        def per_zh(zs, n):
            def per_core(k2, carry):
                n, seen0, seen1 = carry
                g = xs * 4 + zs * 2 + k2
                for s, j in ordered(g):
                    source = j >> 1
                    sec = jnp.where(s == 0, secs[0], secs[1])
                    q = s * ROWS + owner[g * ROWS + j] - sec * ROWS
                    line = g * COLS + source
                    base = (j & 1) * BLOCK_COLS + c * KB
                    odd = source & 1
                    first = n
                    for k in range(KB):
                        rel = lists[line, base + k] - c * BLOCK_COLS
                        take = ((rel >= 0) & (rel < SLAB)).astype(jnp.int32)
                        seen = jnp.where(odd == 0, seen0, seen1)
                        at = jnp.minimum((zs * 2 + odd) * cap_pair + seen, 4 * cap_pair - 1)
                        col_right[xs * (cap_x + 1) + n] = rel
                        keep[jnp.where(xs == x, n, cap_x)] = at
                        n = n + take
                        seen0 = seen0 + take * (1 - odd)
                        seen1 = seen1 + take * odd
                    start[q] = xs * (cap_x + 1) + first
                    count[q] = n - first
                return n, seen0, seen1

            return lax.fori_loop(0, 2, per_core, (n, jnp.int32(0), jnp.int32(0)))[0]

        lax.fori_loop(0, 2, per_zh, jnp.int32(0))
        return 0

    lax.fori_loop(0, 4, per_x, 0)


def make_lists(caps, lists, owner, sections, row_from, panel_from):
    cap_y, cap_left, cap_pair, cap_x = caps
    more = cap_left + 8
    sizes = (more, more, more, cap_pair + 8, cap_pair + 8, cap_x + 8)
    sizes = sizes + (PANEL, PANEL, 4 * (cap_x + 1), 1)
    return pl.pallas_call(
        functools.partial(lists_kernel, caps),
        out_shape=tuple(jax.ShapeDtypeStruct((n,), jnp.int32) for n in sizes),
        in_specs=[SMEM] * 5,
        out_specs=(SMEM,) * len(sizes),
    )(lists, owner, sections, row_from, panel_from)


def gather_kernel(caps, strips, cand, keep_left, here, there, keep, left, right, held, other, send, recv):
    cap_y, cap_left, cap_pair, cap_x = caps
    r, c = lax.axis_index("row"), lax.axis_index("col")
    k = r % 2
    x, y = r // 4, c // 2
    me = ((r // 2) % 2) * 2 + c % 2
    cz = c + 1 - 2 * (c % 2)
    rz = (r // 4) * 4 + (r + 2) % 4
    cut = cap_left * 11 // 14
    zp, zh, zx = {"col": cz}, {"row": rz}, {"row": rz, "col": cz}
    yn, yb = {"col": (c + 2) % COLS}, {"col": (c + COLS - 2) % COLS}
    core = {"row": r + 1 - 2 * k}
    xn, xb = {"row": (r + 4) % ROWS}, {"row": (r + ROWS - 4) % ROWS}
    barrier = pltpu.get_barrier_semaphore()
    for peer in (zp, zh, zx, yn, yb, core, xn, xb):
        pl.semaphore_signal(barrier, inc=1, device_id=peer, device_id_type=MESH)
    half, part = cap_pair // 2, cap_x // 2

    for m in range(half):
        e = there[k * half + m]
        other[m] = cand[e // (4 * cap_y), (e // cap_y) % 4, e % cap_y]
    for m in range(cap_pair):
        e = here[m]
        held[me, m // half, m % half] = cand[e // (4 * cap_y), (e // cap_y) % 4, e % cap_y]

    def pack_left(m, _):
        for u in range(4):
            e = keep_left[m * 4 + u]
            left[c, m * 4 + u] = strips[e // ENTRIES, e % ENTRIES]
        return 0

    lax.fori_loop(0, cap_left // 4, pack_left, 0)
    pl.semaphore_wait(barrier, 8)

    started, done = [], []

    def push(src, dst, to):
        n = len(started)
        copy = pltpu.make_async_remote_copy(
            src, dst, send.at[n], recv.at[n], device_id=to, device_id_type=MESH
        )
        copy.start()
        started.append(copy)
        return copy

    def go(origin, a, b, to):
        piece = left.at[origin, pl.ds(a, b - a)]
        return push(piece, piece, to)

    def gx(origin, a, b, to):
        piece = right.at[origin, k, pl.ds(a, b - a)]
        return push(piece, piece, to)

    def arrived(copy):
        copy.wait_recv()
        done.append(copy)

    end = cap_left
    a_mid, b_mid = cut // 2, (cut + end) // 2
    c_m, c_p, c_o = (c + COLS - 2) % COLS, (c + 2) % COLS, (c + 4) % COLS
    z_m, z_p = (cz + COLS - 2) % COLS, (cz + 2) % COLS
    x_m, x_p, x_o = (x + 3) % 4, (x + 1) % 4, (x + 2) % 4
    z_of_p, z_of_h = (me // 2) * 2 + (me + 1) % 2, (me + 2) % 4
    z_of_x = (z_of_p + 2) % 4

    s1 = push(other, held.at[me, k], zp)
    s2 = push(other, held.at[me, k], zx)
    s3 = push(held.at[me, k], held.at[me, k], zh)
    k1 = go(c, 0, cut, zp)
    k2 = go(c, 0, cut, yn)
    k3 = go(c, 0, cut, yb)
    k10 = go(c, cut, end, yn)
    k11 = go(c, cut, end, yb)
    k12 = go(c, cut, end, zp)
    arrived(s1)
    t1 = push(held.at[z_of_p, k], held.at[z_of_p, k], core)
    arrived(s2)
    t2 = push(held.at[z_of_x, k], held.at[z_of_x, k], core)
    arrived(s3)
    t3 = push(held.at[z_of_h, k], held.at[z_of_h, k], core)
    arrived(k2)
    k6 = go(c_m, 0, a_mid, yn)
    arrived(k3)
    k7 = go(c_p, a_mid, cut, yb)
    arrived(k1)
    k4 = go(cz, 0, cut, yn)
    k5 = go(cz, 0, cut, yb)
    arrived(t1)
    arrived(t2)
    arrived(t3)
    for m in range(cap_x):
        e = keep[m]
        right[x, m // part, m % part] = held[e // cap_pair, (e // half) % 2, e % half]
    u1 = gx(x, 0, part, xn)
    u2 = gx(x, 0, part, xb)
    arrived(k10)
    k13 = go(c_m, cut, b_mid, yn)
    k14 = go(c_m, cut, end, zp)
    arrived(k11)
    k15 = go(c_p, b_mid, end, yb)
    k16 = go(c_p, cut, end, zp)
    arrived(u1)
    u3 = gx(x_m, 0, part // 2, xn)
    u4 = gx(x_m, 0, part, core)
    arrived(u2)
    u5 = gx(x_p, part // 2, part, xb)
    u6 = gx(x_p, 0, part, core)
    arrived(k4)
    k8 = go(z_m, 0, a_mid, yn)
    arrived(k5)
    k9 = go(z_p, a_mid, cut, yb)
    arrived(k13)
    k17 = go(c_o, cut, b_mid, zp)
    arrived(k15)
    k18 = go(c_o, b_mid, end, zp)
    arrived(u3)
    u7 = gx(x_o, 0, part // 2, core)
    arrived(u5)
    u8 = gx(x_o, part // 2, part, core)
    for copy in started:
        if not any(copy is seen for seen in done):
            copy.wait_recv()
    for copy in started:
        copy.wait_send()


COPIES = 32


def gather(caps, collective_id, strips, cand, keep_left, here, there, keep):
    cap_y, cap_left, cap_pair, cap_x = caps
    bf = jnp.bfloat16
    return pl.pallas_call(
        functools.partial(gather_kernel, caps),
        out_shape=(
            jax.ShapeDtypeStruct((COLS, cap_left, STRIP, TILE), bf),
            jax.ShapeDtypeStruct((4, 2, cap_x // 2, TILE, TILE), bf),
        ),
        in_specs=[VMEM, VMEM] + [SMEM] * 4,
        out_specs=(VMEM, VMEM),
        scratch_shapes=[
            pltpu.VMEM((4, 2, cap_pair // 2, TILE, TILE), bf),
            pltpu.VMEM((cap_pair // 2, TILE, TILE), bf),
        ]
        + [pltpu.SemaphoreType.DMA((COPIES,))] * 2,
        compiler_params=params(24, collective_id=collective_id, has_side_effects=True),
    )(strips, cand, keep_left, here, there, keep)


OUT_TILES = ROWS * SLAB
UNROLL = 4


def product_kernel(
    caps, left, right, row_left, inner_left, start, count, col_right, totals,
    squares, blank, out_of, touched_out, sums,
    acc, zeros, job_left, job_right, job_slot, job_first, slot_of, part, sem, zero_sem,
):
    cap_y, cap_left, cap_pair, cap_x = caps
    zeros[...] = jnp.zeros_like(zeros)
    for p in range(ROWS):
        pltpu.make_async_copy(zeros, blank.at[pl.ds(p * TILE, TILE)], zero_sem.at[p]).start()

    def clear(o, _):
        for u in range(16):
            slot_of[o * 16 + u] = -1
        return 0

    lax.fori_loop(0, OUT_TILES // 16, clear, 0)

    def per_left(m, carry):
        p, q = row_left[m], inner_left[m]
        place = start[q]

        def per_right(t, carry):
            n, touched = carry
            at = place + t
            xs = at // (cap_x + 1)
            o = p * SLAB + col_right[at]
            old = slot_of[o]
            fresh = old < 0
            slot = jnp.where(fresh, touched, old)
            job_left[n] = m
            job_right[n] = at - xs
            job_slot[n] = slot
            job_first[n] = fresh.astype(jnp.int32)
            slot_of[o] = slot
            out_of[slot] = o
            return n + 1, touched + fresh.astype(jnp.int32)

        return lax.fori_loop(0, count[q], per_right, carry)

    n, touched = lax.fori_loop(0, totals[0], per_left, (jnp.int32(0), jnp.int32(0)))
    touched_out[0] = touched
    for u in range(UNROLL):
        job_left[n + u] = 0
        job_right[n + u] = 0
        job_slot[n + u] = OUT_TILES
        job_first[n + u] = 1
    part_x = cap_x // 2

    def multiply(g, _):
        results = []
        for u in range(UNROLL):
            a = left[:, job_left[g * UNROLL + u]].reshape(TILE, TILE)
            e = job_right[g * UNROLL + u]
            b = right[e // cap_x, (e // part_x) % 2, e % part_x]
            results.append(jnp.dot(a, b, preferred_element_type=jnp.float32))
        for u in range(UNROLL):
            slot = job_slot[g * UNROLL + u]
            keep = (1 - job_first[g * UNROLL + u]).astype(jnp.float32)
            old = acc[slot]
            acc[slot] = results[u] + jnp.where(keep > 0, old, 0.0)
        return 0

    lax.fori_loop(0, (n + UNROLL - 1) // UNROLL, multiply, 0)
    part[...] = jnp.zeros_like(part)

    def finish(slot, _):
        value = acc[slot]
        value = value * value
        acc[slot] = value
        pltpu.make_async_copy(acc.at[slot], squares.at[slot], sem).start()
        col = lax.rem(out_of[slot], SLAB)
        part[col] += value.reshape(TILE // 8, 8, TILE).sum(axis=0)
        return 0

    lax.fori_loop(0, touched, finish, 0)
    sums[...] = part[...].sum(axis=1)

    def drain(slot, _):
        pltpu.make_async_copy(acc.at[slot], squares.at[slot], sem).wait()
        return 0

    lax.fori_loop(0, touched, drain, 0)
    for p in range(ROWS):
        pltpu.make_async_copy(zeros, blank.at[pl.ds(p * TILE, TILE)], zero_sem.at[p]).wait()


def products(caps, left, right, row_left, inner_left, start, count, col_right, totals):
    cap_y, cap_left, cap_pair, cap_x = caps
    jobs = cap_left * KB + UNROLL
    f32, i32 = jnp.float32, jnp.int32
    return pl.pallas_call(
        functools.partial(product_kernel, caps),
        out_shape=(
            jax.ShapeDtypeStruct((OUT_TILES, TILE, TILE), f32),
            jax.ShapeDtypeStruct((ROWS * TILE, SLAB * TILE), jnp.bfloat16),
            jax.ShapeDtypeStruct((OUT_TILES,), i32),
            jax.ShapeDtypeStruct((1,), i32),
            jax.ShapeDtypeStruct((ROWS, TILE), f32),
        ),
        in_specs=[VMEM, VMEM] + [SMEM] * 6,
        out_specs=(ANY, ANY, SMEM, SMEM, VMEM),
        scratch_shapes=[
            pltpu.VMEM((OUT_TILES + 1, TILE, TILE), f32),
            pltpu.VMEM((TILE, SLAB * TILE), jnp.bfloat16),
        ]
        + [pltpu.SMEM((jobs,), i32)] * 4
        + [
            pltpu.SMEM((OUT_TILES,), i32),
            pltpu.VMEM((ROWS, 8, TILE), f32),
            pltpu.SemaphoreType.DMA,
            pltpu.SemaphoreType.DMA((ROWS,)),
        ],
        compiler_params=params(30),
    )(left, right, row_left, inner_left, start, count, col_right, totals)


def total_kernel(mine, out, parts, send, recv):
    r = lax.axis_index("row")
    barrier = pltpu.get_barrier_semaphore()
    for d in range(1, ROWS):
        pl.semaphore_signal(barrier, inc=1, device_id={"row": (r + d) % ROWS}, device_id_type=MESH)
    parts[r] = mine[...]
    pl.semaphore_wait(barrier, ROWS - 1)
    copies = []
    for d in range(1, ROWS):
        copy = pltpu.make_async_remote_copy(
            mine, parts.at[r], send.at[d], recv.at[d],
            device_id={"row": (r + d) % ROWS}, device_id_type=MESH,
        )
        copy.start()
        copies.append(copy)
    for copy in copies:
        copy.wait_recv()
    out[...] = parts[...].sum(axis=0)
    for copy in copies:
        copy.wait_send()


def total(collective_id, mine):
    return pl.pallas_call(
        total_kernel,
        out_shape=jax.ShapeDtypeStruct((ROWS, TILE), jnp.float32),
        in_specs=[VMEM],
        out_specs=VMEM,
        scratch_shapes=[
            pltpu.VMEM((ROWS, ROWS, TILE), jnp.float32),
            pltpu.SemaphoreType.DMA((ROWS,)),
            pltpu.SemaphoreType.DMA((ROWS,)),
        ],
        compiler_params=params(4, collective_id=collective_id, has_side_effects=True),
    )(mine)


def write_kernel(squares, blank, out_of, touched_in, totals, out, tiles, block, factor, in_sem, out_sem):
    touched = touched_in[0]

    def fetch(slot, _):
        pltpu.make_async_copy(squares.at[slot], tiles.at[slot], in_sem.at[slot]).start()
        return 0

    lax.fori_loop(0, touched, fetch, 0)
    count = float(ROWS * ROWS * TILE)
    factor[...] = count / (totals[...] + 1e-06)

    def place(slot):
        o = out_of[slot]
        p = o // SLAB
        col = o - p * SLAB
        row = pl.ds(pl.multiple_of(p * TILE, TILE), TILE)
        lanes = pl.ds(pl.multiple_of(col * TILE, TILE), TILE)
        copy = pltpu.make_async_copy(block.at[slot], out.at[row, lanes], out_sem)
        return col, copy

    def scale(slot, _):
        pltpu.make_async_copy(squares.at[slot], tiles.at[slot], in_sem.at[slot]).wait()
        col, copy = place(slot)
        block[slot] = (tiles[slot] * factor[pl.ds(col, 1), :]).astype(jnp.bfloat16)
        copy.start()
        return 0

    lax.fori_loop(0, touched, scale, 0)

    def drain(slot, _):
        place(slot)[1].wait()
        return 0

    lax.fori_loop(0, touched, drain, 0)


def write(squares, blank, out_of, touched, totals):
    return pl.pallas_call(
        write_kernel,
        out_shape=jax.ShapeDtypeStruct((ROWS * TILE, SLAB * TILE), jnp.bfloat16),
        in_specs=[ANY, ANY, SMEM, SMEM, VMEM],
        out_specs=ANY,
        input_output_aliases={1: 0},
        scratch_shapes=[
            pltpu.VMEM((OUT_TILES, TILE, TILE), jnp.float32),
            pltpu.VMEM((OUT_TILES, TILE, TILE), jnp.bfloat16),
            pltpu.VMEM((ROWS, TILE), jnp.float32),
            pltpu.SemaphoreType.DMA((OUT_TILES,)),
            pltpu.SemaphoreType.DMA,
        ],
        compiler_params=params(24),
    )(squares, blank, out_of, touched, totals)


def per_device(tile_values, tile_columns, owner_map, section_rows):
    flat = tile_columns.reshape(-1)
    idx = jnp.pad(flat, (0, TILE - flat.shape[0])).reshape(1, TILE)
    tv = tile_values.reshape(2 * COLS * KB, TILE, TILE)
    owner_rows = owner_map.reshape(2, TILE)

    def first(caps, collective_id):
        send_row, row_from, panel_from, picks = prep(caps[0], owner_map, section_rows, flat)
        got = spread(caps[0], collective_id, tv, idx, owner_rows, section_rows, send_row, picks)
        return *got, row_from, panel_from

    def rest(caps, ids, strips, cand, lists, over, row_from, panel_from):
        made = make_lists(
            caps, lists.reshape(ROWS * COLS, TILE), owner_map, section_rows, row_from, panel_from
        )
        keep_left, row_left, inner_left, here, there, keep, start, count, col_right, totals = made
        left, right = gather(caps, ids[0], strips, cand, keep_left, here, there, keep)
        squares, blank, out_of, touched, sums = products(
            caps, left, right, row_left, inner_left, start, count, col_right, totals
        )
        return write(squares, blank, out_of, touched, total(ids[1], sums))

    got = first(FAST, 0)
    return lax.cond(
        jnp.max(got[3]) > 0,
        lambda *_: rest(FULL, (4, 5), *first(FULL, 3)),
        lambda *args: rest(FAST, (1, 2), *args),
        *got,
    )


def solution(mesh):
    both = ("row", "col")
    in_specs = (P(both, None, None, None, None), P(both, None, None), P(), P())
    return jax.shard_map(
        per_device, mesh=mesh, in_specs=in_specs, out_specs=P("row", "col"), check_vma=False
    )
```

```python
import functools

import jax
import jax.numpy as jnp
from jax import lax
from jax.experimental import pallas as pl
from jax.experimental.pallas import tpu as pltpu
from jax.sharding import PartitionSpec as P

TILE = 128
KB = 4
SLAB = 12
SECTIONS = 2
ROWS = 16
COLS = 8
BLOCK_COLS = 32
STRIP = TILE // COLS
ENTRIES = SECTIONS * KB
PANEL = SECTIONS * ROWS
FAST = (8, 56, 10, 16, 80)
FULL = (16, 128, 16, 32, 512)
MESH = pl.DeviceIdType.MESH
VMEM = pl.BlockSpec(memory_space=pltpu.VMEM)
SMEM = pl.BlockSpec(memory_space=pltpu.SMEM)
ANY = pl.BlockSpec(memory_space=pl.ANY)


def params(mib, **kw):
    return pltpu.CompilerParams(vmem_limit_bytes=mib << 20, **kw)


SEND, ROW_FROM, PANEL_FROM, PICKS = 0, ROWS, 2 * ROWS, 4 * ROWS


def prep_kernel(cap, owner, sections, cols, plan, inverse):
    r, c = lax.axis_index("row"), lax.axis_index("col")

    def invert(g, _):
        for j in range(ROWS):
            inverse[owner[g * ROWS + j]] = g * ROWS + j
        return 0

    lax.fori_loop(0, ROWS, invert, 0)
    secs = [sections[0], sections[1]]
    for j in range(ROWS):
        plan[SEND + (owner[r * ROWS + j] >> 4)] = j
        t = inverse[r * ROWS + j]
        plan[ROW_FROM + (t >> 4)] = t & 15
        for s in range(SECTIONS):
            t = inverse[secs[s] * ROWS + j]
            plan[PANEL_FROM + s * ROWS + (t >> 4)] = t & 15
    wanted = []
    for i in range(2):
        block = owner[r * ROWS + c * 2 + i] >> 4
        wanted.append((block == secs[0]) | (block == secs[1]))
    room = cap + 1

    def per_y(yd, _):
        for m in range(room):
            plan[PICKS + yd * room + m] = 0
        count = jnp.int32(0)
        for i in range(2):
            for z in range(2):
                b = yd * 2 + z
                for k in range(KB):
                    rel = cols[i * BLOCK_COLS + b * KB + k] - b * BLOCK_COLS
                    take = wanted[i] & (rel >= 0) & (rel < SLAB)
                    plan[PICKS + yd * room + count] = i * BLOCK_COLS + b * KB + k
                    count = jnp.minimum(count + take.astype(jnp.int32), cap)
        return 0

    lax.fori_loop(0, 4, per_y, 0)


def prep(cap, owner, sections, cols):
    return pl.pallas_call(
        functools.partial(prep_kernel, cap),
        out_shape=jax.ShapeDtypeStruct((PICKS + 4 * (cap + 1),), jnp.int32),
        in_specs=[SMEM] * 3,
        out_specs=SMEM,
        scratch_shapes=[pltpu.SMEM((ROWS * ROWS,), jnp.int32)],
    )(owner, sections, cols)


def iota(dim):
    return lax.broadcasted_iota(jnp.int32, (TILE, TILE), dim)


def picked(mask):
    return jnp.where(mask, 1.0, 0.0).astype(jnp.bfloat16)


def mm(a, b, dims=((1,), (0,))):
    return lax.dot_general(a, b, (dims, ((), ())), preferred_element_type=jnp.float32)


def counts_over(lists, owner, sections):
    cols = lists[...].reshape(TILE, TILE)
    line, lane = iota(0), iota(1)
    blocks, places = [], []
    for i in range(2):
        total = jnp.zeros((TILE, TILE), jnp.float32)
        for h in range(2):
            row = jnp.broadcast_to(owner[h : h + 1, :].astype(jnp.float32), (TILE, TILE))
            choose = picked(lane + h * TILE == 2 * line + i)
            total = total + mm(choose, row.astype(jnp.bfloat16), ((1,), (1,)))
        places.append(total.astype(jnp.int32))
        blocks.append(places[i] >> 4)
    mine = jnp.where(lane < BLOCK_COLS, blocks[0], blocks[1])
    sec0, sec1 = sections[0], sections[1]
    real = lane < 2 * BLOCK_COLS
    b = (lane & (BLOCK_COLS - 1)) >> 2
    rel = cols - b * BLOCK_COLS
    slab = picked(real & (rel >= 0) & (rel < SLAB) & ((mine == sec0) | (mine == sec1)))
    inner0 = (cols >= sec0 * ROWS) & (cols < sec0 * ROWS + ROWS)
    inner1 = (cols >= sec1 * ROWS) & (cols < sec1 * ROWS + ROWS)
    inner = picked(real & (inner0 | inner1))
    lane_b = (line & (BLOCK_COLS - 1)) >> 2
    to_y = picked((line < 2 * BLOCK_COLS) & ((lane_b >> 1) == lane))
    to_b = picked((line < 2 * BLOCK_COLS) & (lane_b == lane))
    per_y = mm(slab, to_y)
    per_b = mm(slab, to_b).astype(jnp.bfloat16)
    same_pair = picked(((line >> 4) == (lane >> 4)) & ((line & 1) == (lane & 1)))
    same_x = picked((line >> 5) == (lane >> 5))
    per_pair = mm(same_pair, per_b)
    per_x = mm(same_x, per_b)
    rows = jnp.zeros((TILE, TILE), jnp.float32)
    section = lane >> 4
    target = jnp.where(section == 0, sec0, sec1) * ROWS + (lane & (ROWS - 1))
    target = jnp.where(section < SECTIONS, target, 2 * TILE + 1)
    panel_tiles = jnp.zeros((TILE, TILE), jnp.float32)
    for i in range(2):
        own = (line >= i * BLOCK_COLS) & (line < (i + 1) * BLOCK_COLS)
        number = mm(inner, picked(own)).astype(jnp.bfloat16)
        rows = rows + mm(picked(blocks[i] == lane), number, ((0,), (0,)))
        mine_b = mm(slab, picked(own & (lane_b == lane))).astype(jnp.bfloat16)
        panel_tiles = panel_tiles + mm(picked(places[i] == target), mine_b, ((0,), (0,)))
    panel_tiles = panel_tiles.astype(jnp.bfloat16)
    jobs = jnp.zeros((TILE, TILE), jnp.float32)
    source = jnp.where((lane >> 2) % SECTIONS == 0, sec0, sec1) >> 1
    wanted = (lane // ENTRIES) * BLOCK_COLS + source * KB + lane % KB
    shifted = jnp.where(real, cols + 1, 0).astype(jnp.float32).astype(jnp.bfloat16)
    chosen = mm(shifted, picked((lane < 2 * ENTRIES) & (line == wanted))).astype(jnp.int32) - 1
    for i in range(2):
        hits = jnp.zeros((TILE, TILE), jnp.float32)
        for e in range(ENTRIES):
            at = chosen[:, i * ENTRIES + e : i * ENTRIES + e + 1]
            hit = (at == target) & (section == e // KB)
            hits = hits + jnp.where(hit, 1.0, 0.0)
        number = mm(hits.astype(jnp.bfloat16), panel_tiles).astype(jnp.bfloat16)
        jobs = jobs + mm(picked(blocks[i] == lane), number, ((0,), (0,)))
    over = per_y - FAST[0]
    over = jnp.maximum(over, rows - FAST[1])
    over = jnp.maximum(over, per_pair - FAST[2])
    over = jnp.maximum(over, per_x - FAST[3])
    over = jnp.maximum(over, jobs - FAST[4])
    return over


def spread_kernel(
    cap, tv, idx, owner, sections, plan,
    strips, cand, lists, over,
    left_out, left_in, right_out, row_out,
    s_idx, r_idx, s_left, r_left, s_right, r_right, s_core, r_core, s_list, r_list, s_row, r_row,
):
    r, c = lax.axis_index("row"), lax.axis_index("col")
    core, y, z = r % 2, c // 2, c % 2
    barrier = pltpu.get_barrier_semaphore()
    for d in range(1, COLS):
        pl.semaphore_signal(barrier, inc=1, device_id={"col": (c + d) % COLS}, device_id_type=MESH)
    for d in range(1, ROWS):
        pl.semaphore_signal(barrier, inc=1, device_id={"row": (r + d) % ROWS}, device_id_type=MESH)
    for i in range(2):
        for s in range(SECTIONS):
            source = sections[s] // 2
            for k in range(KB):
                for h in range(COLS):
                    left_out[h, i * ENTRIES + s * KB + k] = tv[
                        i * BLOCK_COLS + source * KB + k, h * STRIP : (h + 1) * STRIP, :
                    ]

    def pack(yd, _):
        for m in range(cap):
            right_out[yd, m] = tv[plan[PICKS + yd * (cap + 1) + m]]
        return 0

    lax.fori_loop(0, 4, pack, 0)
    lists[r, c] = idx[...]
    left_in[c] = left_out[c]
    cand[core, y] = right_out[y]
    pl.semaphore_wait(barrier, COLS - 1 + ROWS - 1)

    idx_copies, left_copies, right_copies, core_copies = [], [], [], []
    for d in range(1, COLS):
        to = (c + d) % COLS
        copy = pltpu.make_async_remote_copy(
            idx, lists.at[r, c], s_idx.at[d], r_idx.at[d], device_id={"col": to}, device_id_type=MESH
        )
        copy.start()
        idx_copies.append(copy)
    for d in range(1, COLS):
        to = (c + d) % COLS
        copy = pltpu.make_async_remote_copy(
            left_out.at[to], left_in.at[c], s_left.at[d], r_left.at[d],
            device_id={"col": to}, device_id_type=MESH,
        )
        copy.start()
        left_copies.append(copy)
    for d in (2, 1, 3):
        to = (y + d) % 4
        copy = pltpu.make_async_remote_copy(
            right_out.at[to], cand.at[core, y], s_right.at[d], r_right.at[d],
            device_id={"col": to * 2 + z}, device_id_type=MESH,
        )
        copy.start()
        right_copies.append((d, copy))

    def to_core(src, origin, d):
        copy = pltpu.make_async_remote_copy(
            src, cand.at[core, origin], s_core.at[d], r_core.at[d],
            device_id={"row": r + 1 - 2 * core}, device_id_type=MESH,
        )
        copy.start()
        core_copies.append(copy)

    to_core(right_out.at[y], y, 0)
    for copy in idx_copies:
        copy.wait_recv()
    list_copies = []
    for d in range(1, ROWS):
        to = (r + d) % ROWS
        copy = pltpu.make_async_remote_copy(
            lists.at[r], lists.at[r], s_list.at[d], r_list.at[d],
            device_id={"row": to}, device_id_type=MESH,
        )
        copy.start()
        list_copies.append(copy)
    for copy in left_copies:
        copy.wait_recv()

    def reorder(t, _):
        j = plan[SEND + t]
        for e in range(ENTRIES):
            row_out[t, e] = left_in[j // 2, (j % 2) * ENTRIES + e]
        return 0

    lax.fori_loop(0, ROWS, reorder, 0)
    strips[r] = row_out[r]
    row_copies = []
    for d in range(1, ROWS):
        to = (r + d) % ROWS
        copy = pltpu.make_async_remote_copy(
            row_out.at[to], strips.at[r], s_row.at[d], r_row.at[d],
            device_id={"row": to}, device_id_type=MESH,
        )
        copy.start()
        row_copies.append(copy)
    for copy in list_copies:
        copy.wait_recv()
    over[...] = counts_over(lists, owner, sections)
    for d, copy in right_copies:
        copy.wait_recv()
        origin = (y + 4 - d) % 4
        to_core(cand.at[core, origin], origin, d)
    for copy in row_copies + core_copies:
        copy.wait_recv()
    sent = [copy for _, copy in right_copies]
    for copy in idx_copies + left_copies + sent + core_copies + list_copies + row_copies:
        copy.wait_send()


def spread(cap, collective_id, tv, idx, owner, sections, plan):
    bf = jnp.bfloat16
    dma = pltpu.SemaphoreType.DMA
    return pl.pallas_call(
        functools.partial(spread_kernel, cap),
        out_shape=(
            jax.ShapeDtypeStruct((ROWS, ENTRIES, STRIP, TILE), bf),
            jax.ShapeDtypeStruct((2, 4, cap, TILE, TILE), bf),
            jax.ShapeDtypeStruct((ROWS, COLS, 1, TILE), jnp.int32),
            jax.ShapeDtypeStruct((TILE, TILE), jnp.float32),
        ),
        in_specs=[VMEM, VMEM, VMEM, SMEM, SMEM],
        out_specs=(VMEM,) * 4,
        scratch_shapes=[
            pltpu.VMEM((COLS, 2 * ENTRIES, STRIP, TILE), bf),
            pltpu.VMEM((COLS, 2 * ENTRIES, STRIP, TILE), bf),
            pltpu.VMEM((4, cap, TILE, TILE), bf),
            pltpu.VMEM((ROWS, ENTRIES, STRIP, TILE), bf),
        ]
        + [dma((COLS,))] * 8
        + [dma((ROWS,))] * 4,
        compiler_params=params(20, collective_id=collective_id, has_side_effects=True),
    )(tv, idx, owner, sections, plan)


OUT_TILES = ROWS * SLAB
UNUSED = ROWS - 1


def places(caps):
    cap_y, cap_left, cap_pair, cap_x, jobs = caps
    sizes = (
        ("left", cap_left + 8), ("here", cap_pair + 8), ("there", cap_pair + 8), ("keep", cap_x + 8),
        ("job_left", jobs + 8), ("job_right", jobs + 8), ("job_last", jobs + 8), ("job_col", jobs + 8),
        ("out", OUT_TILES), ("slot", OUT_TILES), ("touched", 8),
    )
    at, found = 0, {}
    for name, size in sizes:
        found[name] = at
        at += size
    return found, at


class Part:
    def __init__(self, ref, base):
        self.ref, self.base = ref, base

    def __getitem__(self, i):
        return self.ref[self.base + i]

    def __setitem__(self, i, value):
        self.ref[self.base + i] = value


def lists_kernel(
    caps, lists, owner, sections, plan, made, blank,
    zeros, row_left, inner_left, start, count, col_right, zero_sem,
):
    cap_y, cap_left, cap_pair, cap_x, jobs = caps
    zeros[...] = jnp.zeros_like(zeros)
    for p in range(ROWS):
        pltpu.make_async_copy(zeros, blank.at[pl.ds(p * TILE, TILE)], zero_sem.at[p]).start()
    part = {name: Part(made, base) for name, base in places(caps)[0].items()}
    keep_left, here, there, keep = part["left"], part["here"], part["there"], part["keep"]
    job_left, job_right = part["job_left"], part["job_right"]
    job_last, job_col = part["job_last"], part["job_col"]
    out_of, slot_of = part["out"], part["slot"]
    row_from, panel_from = Part(plan, ROW_FROM), Part(plan, PANEL_FROM)
    r, c = lax.axis_index("row"), lax.axis_index("col")
    x, zh = r >> 2, (r >> 1) & 1
    y, zl = c >> 1, c & 1
    secs = [sections[0], sections[1]]
    for m in range(cap_pair):
        here[m] = 0
        there[m] = 0
    for m in range(cap_x):
        keep[m] = 0

    def clear(m, _):
        for u in range(8):
            keep_left[m * 8 + u] = 0
        return 0

    lax.fori_loop(0, cap_left // 8, clear, 0)

    def left(g, n):
        j = row_from[g]
        line = g * COLS + (j >> 1)
        base = (j & 1) * BLOCK_COLS
        p = owner[g * ROWS + j] - r * ROWS
        for s in range(SECTIONS):
            for k in range(KB):
                rel = lists[line, base + (secs[s] >> 1) * KB + k] - secs[s] * ROWS
                keep_left[n] = g * ENTRIES + s * KB + k
                row_left[n] = p
                inner_left[n] = s * ROWS + rel
                n = n + ((rel >= 0) & (rel < ROWS)).astype(jnp.int32)
        return n

    left_count = lax.fori_loop(0, ROWS, left, jnp.int32(0))

    def ordered(g):
        a, b = panel_from[g], panel_from[ROWS + g]
        swap = (b < a).astype(jnp.int32)
        return ((swap, jnp.minimum(a, b)), (1 - swap, jnp.maximum(a, b)))

    def pairs(k2, carry):
        n_here, n_there = carry
        g = x * 4 + zh * 2 + k2
        used = jnp.int32(0)
        before = jnp.int32(-1)
        for s, j in ordered(g):
            source = j >> 1
            used = jnp.where(source == before, used, 0)
            before = source
            line = g * COLS + source
            base = (j & 1) * BLOCK_COLS
            near = (source & 1) == zl
            spot = k2 * 4 * cap_y + (source >> 1) * cap_y
            for z in range(2):
                mine = zl == z
                for k in range(KB):
                    b = y * 2 + z
                    rel = lists[line, base + b * KB + k] - b * BLOCK_COLS
                    ok = (rel >= 0) & (rel < SLAB)
                    take_here = (ok & near & mine).astype(jnp.int32)
                    take_there = (ok & near & jnp.logical_not(mine)).astype(jnp.int32)
                    at = jnp.minimum(spot + used, 8 * cap_y - 1)
                    here[n_here] = at
                    there[n_there] = at
                    n_here = n_here + take_here
                    n_there = n_there + take_there
                    used = used + ok.astype(jnp.int32)
        return n_here, n_there

    lax.fori_loop(0, 2, pairs, (jnp.int32(0), jnp.int32(0)))

    def per_x(xs, _):
        def per_zh(zs, n):
            def per_core(k2, carry):
                n, seen0, seen1 = carry
                g = xs * 4 + zs * 2 + k2
                for s, j in ordered(g):
                    source = j >> 1
                    sec = jnp.where(s == 0, secs[0], secs[1])
                    q = s * ROWS + owner[g * ROWS + j] - sec * ROWS
                    line = g * COLS + source
                    base = (j & 1) * BLOCK_COLS + c * KB
                    odd = source & 1
                    first = n
                    for k in range(KB):
                        rel = lists[line, base + k] - c * BLOCK_COLS
                        take = ((rel >= 0) & (rel < SLAB)).astype(jnp.int32)
                        seen = jnp.where(odd == 0, seen0, seen1)
                        at = jnp.minimum((zs * 2 + odd) * cap_pair + seen, 4 * cap_pair - 1)
                        col_right[xs * (cap_x + 1) + n] = rel
                        keep[jnp.where(xs == x, n, cap_x)] = at
                        n = n + take
                        seen0 = seen0 + take * (1 - odd)
                        seen1 = seen1 + take * odd
                    start[q] = xs * (cap_x + 1) + first
                    count[q] = n - first
                return n, seen0, seen1

            return lax.fori_loop(0, 2, per_core, (n, jnp.int32(0), jnp.int32(0)))[0]

        lax.fori_loop(0, 2, per_zh, jnp.int32(0))
        return 0

    lax.fori_loop(0, 4, per_x, 0)

    def no_slot(o, _):
        for u in range(16):
            slot_of[o * 16 + u] = -1
        return 0

    lax.fori_loop(0, OUT_TILES // 16, no_slot, 0)

    def no_job(n, _):
        for u in range(8):
            job_left[n * 8 + u] = 0
            job_right[n * 8 + u] = 0
            job_last[n * 8 + u] = -1
            job_col[n * 8 + u] = UNUSED
        return 0

    lax.fori_loop(0, jobs // 8, no_job, 0)

    def per_left(m, carry):
        first = row_left[m] * SLAB
        q = inner_left[m]
        begin = start[q]

        def per_right(t, carry):
            n, touched = carry
            at = begin + t
            col = col_right[at]
            o = first + col
            last = slot_of[o]
            fresh = last < 0
            job_left[n] = m
            job_right[n] = at - at // (cap_x + 1)
            job_last[n] = last
            job_col[n] = col
            job_col[jnp.where(fresh, jobs + 1, last)] = UNUSED
            slot_of[o] = n
            out_of[jnp.where(fresh, touched, OUT_TILES - 1)] = jnp.where(
                fresh, o, out_of[OUT_TILES - 1]
            )
            return n + 1, touched + fresh.astype(jnp.int32)

        return lax.fori_loop(0, count[q], per_right, carry)

    _, touched = lax.fori_loop(0, left_count, per_left, (jnp.int32(0), jnp.int32(0)))
    part["touched"][0] = touched
    for p in range(ROWS):
        pltpu.make_async_copy(zeros, blank.at[pl.ds(p * TILE, TILE)], zero_sem.at[p]).wait()


def make_lists(caps, lists, owner, sections, plan):
    cap_y, cap_left, cap_pair, cap_x, jobs = caps
    smem = lambda n: pltpu.SMEM((n,), jnp.int32)
    return pl.pallas_call(
        functools.partial(lists_kernel, caps),
        out_shape=(
            jax.ShapeDtypeStruct((places(caps)[1],), jnp.int32),
            jax.ShapeDtypeStruct((ROWS * TILE, SLAB * TILE), jnp.bfloat16),
        ),
        in_specs=[SMEM] * 4,
        out_specs=(SMEM, ANY),
        scratch_shapes=[
            pltpu.VMEM((TILE, SLAB * TILE), jnp.bfloat16),
            smem(cap_left + 8), smem(cap_left + 8), smem(PANEL), smem(PANEL), smem(4 * (cap_x + 1)),
            pltpu.SemaphoreType.DMA((ROWS,)),
        ],
        compiler_params=params(4),
    )(lists, owner, sections, plan)


UNROLL = 8


def multiply_kernel(
    caps, strips, cand, plan, sums, totals,
    left, right, held, other, rows, parts, send, recv, total_send, total_recv,
):
    cap_y, cap_left, cap_pair, cap_x, jobs = caps
    part_of = {name: Part(plan, base) for name, base in places(caps)[0].items()}
    keep_left, here, there, keep = (part_of[n] for n in ("left", "here", "there", "keep"))
    r, c = lax.axis_index("row"), lax.axis_index("col")
    k = r % 2
    x, y = r // 4, c // 2
    me = ((r // 2) % 2) * 2 + c % 2
    cz = c + 1 - 2 * (c % 2)
    rz = (r // 4) * 4 + (r + 2) % 4
    cut = cap_left * 11 // 14
    zp, zh, zx = {"col": cz}, {"row": rz}, {"row": rz, "col": cz}
    yn, yb = {"col": (c + 2) % COLS}, {"col": (c + COLS - 2) % COLS}
    core = {"row": r + 1 - 2 * k}
    xn, xb = {"row": (r + 4) % ROWS}, {"row": (r + ROWS - 4) % ROWS}
    barrier = pltpu.get_barrier_semaphore()
    for peer in (zp, zx, yn, yb):
        pl.semaphore_signal(barrier, inc=1, device_id=peer, device_id_type=MESH)
    for d in range(1, ROWS):
        pl.semaphore_signal(barrier, inc=1, device_id={"row": (r + d) % ROWS}, device_id_type=MESH)
    half, part = cap_pair // 2, cap_x // 2

    for m in range(half):
        e = there[k * half + m]
        other[m] = cand[e // (4 * cap_y), (e // cap_y) % 4, e % cap_y]
    for m in range(cap_pair):
        e = here[m]
        held[me, m // half, m % half] = cand[e // (4 * cap_y), (e // cap_y) % 4, e % cap_y]

    def pack_left(m, _):
        for u in range(4):
            e = keep_left[m * 4 + u]
            left[c, m * 4 + u] = strips[e // ENTRIES, e % ENTRIES]
        return 0

    lax.fori_loop(0, cap_left // 4, pack_left, 0)
    pl.semaphore_wait(barrier, 4 + ROWS - 1)

    started, done = [], []

    def push(src, dst, to):
        n = len(started)
        copy = pltpu.make_async_remote_copy(
            src, dst, send.at[n], recv.at[n], device_id=to, device_id_type=MESH
        )
        copy.start()
        started.append(copy)
        return copy

    def go(origin, a, b, to):
        piece = left.at[origin, pl.ds(a, b - a)]
        return push(piece, piece, to)

    def gx(origin, a, b, to):
        piece = right.at[origin, k, pl.ds(a, b - a)]
        return push(piece, piece, to)

    def arrived(copy):
        copy.wait_recv()
        done.append(copy)

    end = cap_left
    a_mid, b_mid = cut // 2, (cut + end) // 2
    c_m, c_p, c_o = (c + COLS - 2) % COLS, (c + 2) % COLS, (c + 4) % COLS
    z_m, z_p = (cz + COLS - 2) % COLS, (cz + 2) % COLS
    x_m, x_p, x_o = (x + 3) % 4, (x + 1) % 4, (x + 2) % 4
    z_of_p, z_of_h = (me // 2) * 2 + (me + 1) % 2, (me + 2) % 4
    z_of_x = (z_of_p + 2) % 4

    s1 = push(other, held.at[me, k], zp)
    s2 = push(other, held.at[me, k], zx)
    s3 = push(held.at[me, k], held.at[me, k], zh)
    k1 = go(c, 0, cut, zp)
    k2 = go(c, 0, cut, yn)
    k3 = go(c, 0, cut, yb)
    k10 = go(c, cut, end, yn)
    k11 = go(c, cut, end, yb)
    k12 = go(c, cut, end, zp)
    arrived(s1)
    t1 = push(held.at[z_of_p, k], held.at[z_of_p, k], core)
    arrived(s2)
    t2 = push(held.at[z_of_x, k], held.at[z_of_x, k], core)
    arrived(s3)
    t3 = push(held.at[z_of_h, k], held.at[z_of_h, k], core)
    arrived(k2)
    k6 = go(c_m, 0, a_mid, yn)
    arrived(k3)
    k7 = go(c_p, a_mid, cut, yb)
    arrived(k1)
    k4 = go(cz, 0, cut, yn)
    k5 = go(cz, 0, cut, yb)
    arrived(t1)
    arrived(t2)
    arrived(t3)
    for m in range(cap_x):
        e = keep[m]
        right[x, m // part, m % part] = held[e // cap_pair, (e // half) % 2, e % half]
    u1 = gx(x, 0, part, xn)
    u2 = gx(x, 0, part, xb)
    arrived(k10)
    k13 = go(c_m, cut, b_mid, yn)
    k14 = go(c_m, cut, end, zp)
    arrived(k11)
    k15 = go(c_p, b_mid, end, yb)
    k16 = go(c_p, cut, end, zp)
    arrived(u1)
    u3 = gx(x_m, 0, part // 2, xn)
    u4 = gx(x_m, 0, part, core)
    arrived(u2)
    u5 = gx(x_p, part // 2, part, xb)
    u6 = gx(x_p, 0, part, core)
    arrived(k4)
    k8 = go(z_m, 0, a_mid, yn)
    arrived(k5)
    k9 = go(z_p, a_mid, cut, yb)
    arrived(k13)
    k17 = go(c_o, cut, b_mid, zp)
    arrived(k15)
    k18 = go(c_o, b_mid, end, zp)
    arrived(u3)
    u7 = gx(x_o, 0, part // 2, core)
    arrived(u5)
    u8 = gx(x_o, part // 2, part, core)
    for copy in started:
        if not any(copy is seen for seen in done):
            copy.wait_recv()
    for copy in started:
        copy.wait_send()

    job_left, job_right = part_of["job_left"], part_of["job_right"]
    job_last, job_col = part_of["job_last"], part_of["job_col"]
    rows[...] = jnp.zeros_like(rows)
    line = lax.broadcasted_iota(jnp.int32, (ROWS, TILE), 0)

    def multiply(g, _):
        results = []
        for u in range(UNROLL):
            n = g * UNROLL + u
            a = left[:, job_left[n]].reshape(TILE, TILE)
            e = job_right[n]
            b = right[e // cap_x, (e // part) % 2, e % part]
            results.append(jnp.dot(a, b, preferred_element_type=jnp.float32))
        added = jnp.zeros((ROWS, TILE), jnp.float32)
        for u in range(UNROLL):
            n = g * UNROLL + u
            last = job_last[n]
            old = sums[jnp.maximum(last, 0)]
            value = results[u] + jnp.where(last >= 0, old, 0.0)
            sums[n] = value
            square = (value * value).reshape(TILE // 8, 8, TILE).sum(axis=0)
            square = square.sum(axis=0, keepdims=True)
            added = added + jnp.where(line == job_col[n], square, 0.0)
        rows[...] += added
        return 0

    lax.fori_loop(0, jobs // UNROLL, multiply, 0)
    parts[r] = rows[...]
    copies = []
    for d in range(1, ROWS):
        copy = pltpu.make_async_remote_copy(
            rows, parts.at[r], total_send.at[d], total_recv.at[d],
            device_id={"row": (r + d) % ROWS}, device_id_type=MESH,
        )
        copy.start()
        copies.append(copy)
    for copy in copies:
        copy.wait_recv()
    totals[...] = parts[...].sum(axis=0)
    for copy in copies:
        copy.wait_send()


COPIES = 32


def multiply(caps, collective_id, strips, cand, plan):
    cap_y, cap_left, cap_pair, cap_x, jobs = caps
    bf, f32 = jnp.bfloat16, jnp.float32
    dma = pltpu.SemaphoreType.DMA
    mib = 24 + jobs * TILE * TILE * 4 // (1 << 20)
    return pl.pallas_call(
        functools.partial(multiply_kernel, caps),
        out_shape=(
            jax.ShapeDtypeStruct((jobs, TILE, TILE), f32),
            jax.ShapeDtypeStruct((ROWS, TILE), f32),
        ),
        in_specs=[VMEM, VMEM, SMEM],
        out_specs=(VMEM, VMEM),
        scratch_shapes=[
            pltpu.VMEM((COLS, cap_left, STRIP, TILE), bf),
            pltpu.VMEM((4, 2, cap_x // 2, TILE, TILE), bf),
            pltpu.VMEM((4, 2, cap_pair // 2, TILE, TILE), bf),
            pltpu.VMEM((cap_pair // 2, TILE, TILE), bf),
            pltpu.VMEM((ROWS, TILE), f32),
            pltpu.VMEM((ROWS, ROWS, TILE), f32),
        ]
        + [dma((COPIES,))] * 2
        + [dma((ROWS,))] * 2,
        compiler_params=params(mib, collective_id=collective_id, has_side_effects=True),
    )(strips, cand, plan)


def write_kernel(at, sums, blank, plan, totals, out, block, factor, out_sem):
    touched = plan[at["touched"]]
    count = float(ROWS * ROWS * TILE)
    factor[...] = count / (totals[...] + 1e-06)

    def place(i):
        o = plan[at["out"] + i]
        p = o // SLAB
        col = o - p * SLAB
        row = pl.ds(pl.multiple_of(p * TILE, TILE), TILE)
        lanes = pl.ds(pl.multiple_of(col * TILE, TILE), TILE)
        return o, col, pltpu.make_async_copy(block.at[i], out.at[row, lanes], out_sem)

    def scale(i, _):
        o, col, copy = place(i)
        value = sums[plan[at["slot"] + o]]
        block[i] = (value * value * factor[pl.ds(col, 1), :]).astype(jnp.bfloat16)
        copy.start()
        return 0

    lax.fori_loop(0, touched, scale, 0)

    def drain(i, _):
        place(i)[2].wait()
        return 0

    lax.fori_loop(0, touched, drain, 0)


def write(caps, sums, blank, plan, totals):
    jobs = caps[4]
    mib = 10 + jobs * TILE * TILE * 4 // (1 << 20)
    return pl.pallas_call(
        functools.partial(write_kernel, places(caps)[0]),
        out_shape=jax.ShapeDtypeStruct((ROWS * TILE, SLAB * TILE), jnp.bfloat16),
        in_specs=[VMEM, ANY, SMEM, VMEM],
        out_specs=ANY,
        input_output_aliases={1: 0},
        scratch_shapes=[
            pltpu.VMEM((OUT_TILES, TILE, TILE), jnp.bfloat16),
            pltpu.VMEM((ROWS, TILE), jnp.float32),
            pltpu.SemaphoreType.DMA,
        ],
        compiler_params=params(mib),
    )(sums, blank, plan, totals)


def per_device(tile_values, tile_columns, owner_map, section_rows):
    flat = tile_columns.reshape(-1)
    idx = jnp.pad(flat, (0, TILE - flat.shape[0])).reshape(1, TILE)
    tv = tile_values.reshape(2 * COLS * KB, TILE, TILE)
    owner_rows = owner_map.reshape(2, TILE)

    def first(caps, collective_id):
        plan = prep(caps[0], owner_map, section_rows, flat)
        return *spread(caps[0], collective_id, tv, idx, owner_rows, section_rows, plan), plan

    def rest(caps, collective_id, strips, cand, lists, over, plan):
        made, blank = make_lists(
            caps, lists.reshape(ROWS * COLS, TILE), owner_map, section_rows, plan
        )
        sums, totals = multiply(caps, collective_id, strips, cand, made)
        return write(caps, sums, blank, made, totals)

    got = first(FAST, 0)
    return lax.cond(
        jnp.max(got[3]) > 0,
        lambda *_: rest(FULL, 3, *first(FULL, 2)),
        lambda *args: rest(FAST, 1, *args),
        *got,
    )


def solution(mesh):
    both = ("row", "col")
    in_specs = (P(both, None, None, None, None), P(both, None, None), P(), P())
    return jax.shard_map(
        per_device, mesh=mesh, in_specs=in_specs, out_specs=P("row", "col"), check_vma=False
    )
```

```python
import functools

import jax
import jax.numpy as jnp
from jax import lax
from jax.experimental import pallas as pl
from jax.experimental.pallas import tpu as pltpu
from jax.sharding import PartitionSpec as P

TILE = 128
KB = 4
SLAB = 12
SECTIONS = 2
ROWS = 16
COLS = 8
BLOCK_COLS = 32
STRIP = TILE // COLS
ENTRIES = SECTIONS * KB
PANEL = SECTIONS * ROWS
FAST = (8, 56, 10, 16, 80)
FULL = (16, 128, 16, 32, 512)
MESH = pl.DeviceIdType.MESH
VMEM = pl.BlockSpec(memory_space=pltpu.VMEM)
SMEM = pl.BlockSpec(memory_space=pltpu.SMEM)
ANY = pl.BlockSpec(memory_space=pl.ANY)


def params(mib, **kw):
    return pltpu.CompilerParams(vmem_limit_bytes=mib << 20, **kw)


SEND, ROW_FROM, PANEL_FROM, PICKS = 0, ROWS, 2 * ROWS, 4 * ROWS


def prep_kernel(cap, owner, sections, cols, plan, inverse):
    r, c = lax.axis_index("row"), lax.axis_index("col")

    def invert(g, _):
        for j in range(ROWS):
            inverse[owner[g * ROWS + j]] = g * ROWS + j
        return 0

    lax.fori_loop(0, ROWS, invert, 0)
    secs = [sections[0], sections[1]]
    for j in range(ROWS):
        plan[SEND + (owner[r * ROWS + j] >> 4)] = j
        t = inverse[r * ROWS + j]
        plan[ROW_FROM + (t >> 4)] = t & 15
        for s in range(SECTIONS):
            t = inverse[secs[s] * ROWS + j]
            plan[PANEL_FROM + s * ROWS + (t >> 4)] = t & 15
    wanted = []
    for i in range(2):
        block = owner[r * ROWS + c * 2 + i] >> 4
        wanted.append((block == secs[0]) | (block == secs[1]))
    room = cap + 1

    def per_y(yd, _):
        for m in range(room):
            plan[PICKS + yd * room + m] = 0
        count = jnp.int32(0)
        for i in range(2):
            for z in range(2):
                b = yd * 2 + z
                for k in range(KB):
                    rel = cols[i * BLOCK_COLS + b * KB + k] - b * BLOCK_COLS
                    take = wanted[i] & (rel >= 0) & (rel < SLAB)
                    plan[PICKS + yd * room + count] = i * BLOCK_COLS + b * KB + k
                    count = jnp.minimum(count + take.astype(jnp.int32), cap)
        return 0

    lax.fori_loop(0, 4, per_y, 0)


def prep(cap, owner, sections, cols):
    return pl.pallas_call(
        functools.partial(prep_kernel, cap),
        out_shape=jax.ShapeDtypeStruct((PICKS + 4 * (cap + 1),), jnp.int32),
        in_specs=[SMEM] * 3,
        out_specs=SMEM,
        scratch_shapes=[pltpu.SMEM((ROWS * ROWS,), jnp.int32)],
    )(owner, sections, cols)


def iota(dim):
    return lax.broadcasted_iota(jnp.int32, (TILE, TILE), dim)


def picked(mask):
    return jnp.where(mask, 1.0, 0.0).astype(jnp.bfloat16)


def mm(a, b, dims=((1,), (0,))):
    return lax.dot_general(a, b, (dims, ((), ())), preferred_element_type=jnp.float32)


ROW_LEFT, ROW_HERE, ROW_THERE, ROW_KEEP = 0, 1, 2, 3
ROW_JOB, ROW_TILE, ROW_LAST, ROW_COL, ROW_OUT = 4, 5, 6, 7, 8


def vector_plan(caps, lists, owner, sections, r, c):
    cap_y, cap_left, cap_pair, cap_x, most_jobs = caps
    f32, bf, i32 = jnp.float32, jnp.bfloat16, jnp.int32
    cols = lists[...].reshape(TILE, TILE)
    line, lane = iota(0), iota(1)
    before = picked(line < lane)
    after = picked(lane < line)
    ones = jnp.ones((TILE, TILE), bf)
    same = picked(line == lane)
    nn, tn, nt = ((1,), (0,)), ((0,), (0,)), ((1,), (1,))
    small = lambda v: v.astype(f32).astype(bf)
    whole = lambda v: v.astype(i32)
    places_, blocks = [], []
    for i in range(2):
        total = jnp.zeros((TILE, TILE), f32)
        for h in range(2):
            row = jnp.broadcast_to(owner[h : h + 1, :].astype(f32), (TILE, TILE))
            total = total + mm(picked(lane + h * TILE == 2 * line + i), row.astype(bf), nt)
        places_.append(whole(total))
        blocks.append(places_[i] >> 4)
    mine = jnp.where(lane < BLOCK_COLS, blocks[0], blocks[1])
    sec0, sec1 = sections[0], sections[1]
    real = lane < 2 * BLOCK_COLS
    b = (lane & (BLOCK_COLS - 1)) >> 2
    rel = cols - b * BLOCK_COLS
    slab_mask = real & (rel >= 0) & (rel < SLAB) & ((mine == sec0) | (mine == sec1))
    slab = picked(slab_mask)
    shifted = small(jnp.where(real, cols + 1, 0))
    lane_b = (line & (BLOCK_COLS - 1)) >> 2
    row_real = line < 2 * BLOCK_COLS

    per_y = mm(slab, picked(row_real & ((lane_b >> 1) == lane)))
    per_b = small(mm(slab, picked(row_real & (lane_b == lane))))
    per_pair = mm(picked(((line >> 4) == (lane >> 4)) & ((line & 1) == (lane & 1))), per_b)
    per_x = mm(picked((line >> 5) == (lane >> 5)), per_b)
    section = lane >> 4
    target = jnp.where(section == 0, sec0, sec1) * ROWS + (lane & (ROWS - 1))
    target = jnp.where(section < SECTIONS, target, 2 * TILE + 1)
    source = jnp.where((lane >> 2) % SECTIONS == 0, sec0, sec1) >> 1
    chosen, panel_tiles = [], jnp.zeros((TILE, TILE), f32)
    for i in range(2):
        wanted = i * BLOCK_COLS + source * KB + lane % KB
        chosen.append(mm(shifted, picked((lane < ENTRIES) & (line == wanted))))
        own = (line >= i * BLOCK_COLS) & (line < (i + 1) * BLOCK_COLS)
        mine_b = small(mm(slab, picked(own & (lane_b == lane))))
        panel_tiles = panel_tiles + mm(picked(places_[i] == target), mine_b, tn)
    panel_tiles = small(panel_tiles)
    rows = jnp.zeros((TILE, TILE), f32)
    jobs = jnp.zeros((TILE, TILE), f32)
    for i in range(2):
        hits = jnp.zeros((TILE, TILE), f32)
        for e in range(ENTRIES):
            at = whole(chosen[i][:, e : e + 1]) - 1
            hits = hits + jnp.where((at == target) & (section == e // KB), 1.0, 0.0)
        hits = small(hits)
        block = picked(blocks[i] == lane)
        rows = rows + mm(block, small(mm(hits, ones)), tn)
        jobs = jobs + mm(block, small(mm(hits, panel_tiles)), tn)
    over = jnp.maximum(per_y - cap_y, rows - cap_left)
    over = jnp.maximum(over, jnp.maximum(per_pair - cap_pair, per_x - cap_x))
    over = jnp.maximum(over, jobs - most_jobs)

    got = jnp.zeros((TILE, TILE), f32)
    place = jnp.zeros((TILE, TILE), f32)
    for i in range(2):
        group = picked(((line >> 3) == lane) & (blocks[i] == r))
        got = got + mm(group, small(chosen[i]), tn)
        place = place + mm(group, small(places_[i]), tn)
    line16 = lax.broadcasted_iota(i32, (ROWS, TILE), 0)
    lane16 = lax.broadcasted_iota(i32, (ROWS, TILE), 1)
    got, place = whole(got[:ROWS]) - 1, whole(place[:ROWS]) - r * ROWS
    inner = got - jnp.where(lane16 < KB, sec0, sec1) * ROWS
    ok = (lane16 < ENTRIES) & (inner >= 0) & (inner < ROWS)
    inner = inner + (lane16 >> 2) * ROWS
    flags = picked(ok)
    spare = jnp.zeros((TILE - ROWS, TILE), bf)
    padded = jnp.concatenate([flags, spare], axis=0)
    rank = mm(padded, before) + mm(after, small(mm(padded, ones)))
    rank = jnp.where(ok, whole(rank[:ROWS]), -1)
    zero16 = jnp.zeros((ROWS, TILE), i32)
    code, left_p, left_q = zero16, zero16, zero16
    for e in range(ENTRIES):
        hit = rank[:, e : e + 1] == lane16
        code = code + jnp.where(hit, line16 * ENTRIES + e, 0)
        left_p = left_p + jnp.where(hit, place[:, e : e + 1], 0)
        left_q = left_q + jnp.where(hit, inner[:, e : e + 1] + 1, 0)
    code = code.sum(axis=0, keepdims=True)
    left_p = left_p.sum(axis=0, keepdims=True)
    left_q = left_q.sum(axis=0, keepdims=True)

    def lanes_of(column):
        wanted = (lane >> 2) * BLOCK_COLS + column * KB + lane % KB
        return picked((lane < 2 * KB) & (line == wanted))

    x, zh, y, zl = r // 4, (r // 2) % 2, c // 2, c % 2
    to_here, to_there = lanes_of(c), lanes_of(c + 1 - 2 * zl)
    of_y = slab_mask & ((b >> 1) == y)
    used = small(mm(picked(of_y), before))
    spot = ((line >> 3) & 1) * (4 * cap_y) + ((line & 7) >> 1) * cap_y
    eligible = ((line >> 4) == x * 2 + zh) & ((line & 1) == zl)

    def packed_row(key, values):
        sums = [jnp.zeros((TILE, TILE), i32) for _ in values]
        for u in range(2 * KB):
            hit = key[:, u : u + 1] == lane
            for n, value in enumerate(values):
                sums[n] = sums[n] + jnp.where(hit, value(u), 0)
        return [v.sum(axis=0, keepdims=True) for v in sums]

    def from_y(choose):
        flag = (mm(slab, choose) > 0.5) & eligible
        number = picked(flag)
        order = whole(mm(number, before) + mm(after, small(mm(number, ones))))
        at = spot + whole(mm(used, choose))
        key = jnp.where(flag, order, -1)
        return packed_row(key, [lambda u: at[:, u : u + 1]])[0]

    here, there = from_y(to_here), from_y(to_there)

    flag = mm(slab, to_here) > 0.5
    number = picked(flag)
    ahead = mm(number, before)
    rest = small(mm(number, ones))
    in_x = whole(ahead + mm(picked((lane < line) & ((line >> 5) == (lane >> 5))), rest))
    same_pair = (lane < line) & ((line >> 4) == (lane >> 4)) & ((line & 1) == (lane & 1))
    in_pair = whole(ahead + mm(picked(same_pair), rest))
    at = (((line >> 4) & 1) * 2 + (line & 1)) * cap_pair + in_pair
    key = jnp.where(flag & ((line >> 5) == x), in_x, -1)
    keep = packed_row(key, [lambda u: at[:, u : u + 1]])[0]
    key = jnp.where(flag, (line >> 5) * cap_x + in_x, -1)
    grid_col = whole(mm(shifted, to_here)) - 1 - c * BLOCK_COLS
    panel_of = []
    for i in range(2):
        q = jnp.where(blocks[i] == sec0, places_[i] - sec0 * ROWS, places_[i] - sec1 * ROWS + ROWS)
        panel_of.append(q + 1)
    right_q, right_col = packed_row(
        key, [lambda u: panel_of[u // KB], lambda u: grid_col[:, u : u + 1]]
    )

    wide = lambda row: jnp.broadcast_to(row, (TILE, TILE))
    left_q_down = whole(mm(same, small(wide(left_q)), nt))
    pair = picked((left_q_down == wide(right_q)) & (left_q_down > 0))
    number = small(mm(pair, ones))
    begin_row = whole(mm(number, before, tn))
    number_row = whole(mm(number, same, tn))
    job_of = picked((line >= begin_row) & (line < begin_row + number_row))
    begin = mm(job_of, small(mm(after, number)))
    turn = mm(job_of, small(mm(pair, before)))
    choice = (mm(job_of, pair) > 0.5) & (whole(turn) == line - whole(begin))
    choice = picked(choice)
    line8 = lax.broadcasted_iota(i32, (ROWS, TILE), 0)
    stack = jnp.where(line8 == 0, lane16, jnp.where(line8 == 1, jnp.broadcast_to(left_p, (ROWS, TILE)), 0))
    by_left = whole(mm(small(stack), job_of, nt))
    stack = jnp.where(line8 == 0, lane16, jnp.where(line8 == 1, jnp.broadcast_to(right_col, (ROWS, TILE)), 1))
    by_right = whole(mm(small(stack), choice, nt))
    job_left, job_p = by_left[0:1], by_left[1:2]
    job_tile, job_col, valid = by_right[0:1], by_right[1:2], by_right[2:3] > 0
    out = jnp.where(valid, job_p * SLAB + job_col, 255)
    out_row = wide(out)
    out_down = whole(mm(same, small(out_row), nt))
    alike = out_down == out_row
    last = jnp.where(alike & (line < lane), line, -1).max(axis=0, keepdims=True)
    later = jnp.where(alike & (line > lane), 1, 0).max(axis=0, keepdims=True)
    final = valid & (later == 0)
    made = [
        jnp.clip(code, 0, ROWS * ENTRIES - 1),
        jnp.clip(here, 0, 8 * cap_y - 1),
        jnp.clip(there, 0, 8 * cap_y - 1),
        jnp.clip(keep, 0, 4 * cap_pair - 1),
        jnp.clip(job_left, 0, cap_left - 1),
        jnp.clip(job_tile, 0, 4 * cap_x - 1),
        jnp.where(valid, jnp.clip(last, -1, most_jobs - 1), -1),
        jnp.where(final, job_col, UNUSED),
        jnp.where(final, jnp.clip(out, 0, OUT_TILES - 1), -1),
    ]
    plan = jnp.zeros((ROWS, TILE), i32)
    for n, row in enumerate(made):
        plan = jnp.where(line16 == n, jnp.broadcast_to(row, (ROWS, TILE)), plan)
    return plan, over


def spread_part(
    cap, tv, idx, sections, plan,
    strips, cand, lists,
    left_out, left_in, right_out, row_out,
    s_idx, r_idx, s_left, r_left, s_right, r_right, s_core, r_core, s_list, r_list, s_row, r_row,
    meet, on_lists, on_strips,
):
    r, c = lax.axis_index("row"), lax.axis_index("col")
    core, y, z = r % 2, c // 2, c % 2
    for i in range(2):
        for s in range(SECTIONS):
            source = sections[s] // 2
            for k in range(KB):
                for h in range(COLS):
                    left_out[h, i * ENTRIES + s * KB + k] = tv[
                        i * BLOCK_COLS + source * KB + k, h * STRIP : (h + 1) * STRIP, :
                    ]

    def pack(yd, _):
        for m in range(cap):
            right_out[yd, m] = tv[plan[PICKS + yd * (cap + 1) + m]]
        return 0

    lax.fori_loop(0, 4, pack, 0)
    lists[r, c] = idx[...]
    left_in[c] = left_out[c]
    cand[core, y] = right_out[y]
    meet()

    idx_copies, left_copies, right_copies, core_copies = [], [], [], []
    for d in range(1, COLS):
        to = (c + d) % COLS
        copy = pltpu.make_async_remote_copy(
            idx, lists.at[r, c], s_idx.at[d], r_idx.at[d], device_id={"col": to}, device_id_type=MESH
        )
        copy.start()
        idx_copies.append(copy)
    for d in range(1, COLS):
        to = (c + d) % COLS
        copy = pltpu.make_async_remote_copy(
            left_out.at[to], left_in.at[c], s_left.at[d], r_left.at[d],
            device_id={"col": to}, device_id_type=MESH,
        )
        copy.start()
        left_copies.append(copy)
    for d in (2, 1, 3):
        to = (y + d) % 4
        copy = pltpu.make_async_remote_copy(
            right_out.at[to], cand.at[core, y], s_right.at[d], r_right.at[d],
            device_id={"col": to * 2 + z}, device_id_type=MESH,
        )
        copy.start()
        right_copies.append((d, copy))

    def to_core(src, origin, d):
        copy = pltpu.make_async_remote_copy(
            src, cand.at[core, origin], s_core.at[d], r_core.at[d],
            device_id={"row": r + 1 - 2 * core}, device_id_type=MESH,
        )
        copy.start()
        core_copies.append(copy)

    to_core(right_out.at[y], y, 0)
    for copy in idx_copies:
        copy.wait_recv()
    list_copies = []
    for d in range(1, ROWS):
        to = (r + d) % ROWS
        copy = pltpu.make_async_remote_copy(
            lists.at[r], lists.at[r], s_list.at[d], r_list.at[d],
            device_id={"row": to}, device_id_type=MESH,
        )
        copy.start()
        list_copies.append(copy)
    for copy in left_copies:
        copy.wait_recv()

    def reorder(t, _):
        j = plan[SEND + t]
        for e in range(ENTRIES):
            row_out[t, e] = left_in[j // 2, (j % 2) * ENTRIES + e]
        return 0

    lax.fori_loop(0, ROWS, reorder, 0)
    strips[r] = row_out[r]
    row_copies = []
    for d in range(1, ROWS):
        to = (r + d) % ROWS
        copy = pltpu.make_async_remote_copy(
            row_out.at[to], strips.at[r], s_row.at[d], r_row.at[d],
            device_id={"row": to}, device_id_type=MESH,
        )
        copy.start()
        row_copies.append(copy)
    for copy in list_copies:
        copy.wait_recv()
    on_lists()
    for copy in row_copies:
        copy.wait_recv()
    on_strips()
    for d, copy in right_copies:
        copy.wait_recv()
        origin = (y + 4 - d) % 4
        to_core(cand.at[core, origin], origin, d)
    for copy in core_copies:
        copy.wait_recv()
    sent = [copy for _, copy in right_copies]
    return idx_copies + left_copies + sent + core_copies + list_copies + row_copies


def greet(r, c):
    barrier = pltpu.get_barrier_semaphore()
    for d in range(1, COLS):
        pl.semaphore_signal(barrier, inc=1, device_id={"col": (c + d) % COLS}, device_id_type=MESH)
    for d in range(1, ROWS):
        pl.semaphore_signal(barrier, inc=1, device_id={"row": (r + d) % ROWS}, device_id_type=MESH)
    across = {"row": (r // 4) * 4 + (r + 2) % 4, "col": c + 1 - 2 * (c % 2)}
    pl.semaphore_signal(barrier, inc=1, device_id=across, device_id_type=MESH)


def meet():
    pl.semaphore_wait(pltpu.get_barrier_semaphore(), COLS - 1 + ROWS - 1 + 1)


def spread_kernel(cap, tv, idx, sections, plan, strips, cand, lists, *scratch):
    greet(lax.axis_index("row"), lax.axis_index("col"))
    nothing = lambda: None
    started = spread_part(
        cap, tv, idx, sections, plan, strips, cand, lists, *scratch, meet, nothing, nothing
    )
    for copy in started:
        copy.wait_send()


def spread_scratch(cap):
    bf = jnp.bfloat16
    dma = pltpu.SemaphoreType.DMA
    return (
        [
            pltpu.VMEM((COLS, 2 * ENTRIES, STRIP, TILE), bf),
            pltpu.VMEM((COLS, 2 * ENTRIES, STRIP, TILE), bf),
            pltpu.VMEM((4, cap, TILE, TILE), bf),
            pltpu.VMEM((ROWS, ENTRIES, STRIP, TILE), bf),
        ]
        + [dma((COLS,))] * 8
        + [dma((ROWS,))] * 4
    )


def spread(cap, collective_id, tv, idx, sections, plan):
    bf = jnp.bfloat16
    return pl.pallas_call(
        functools.partial(spread_kernel, cap),
        out_shape=(
            jax.ShapeDtypeStruct((ROWS, ENTRIES, STRIP, TILE), bf),
            jax.ShapeDtypeStruct((2, 4, cap, TILE, TILE), bf),
            jax.ShapeDtypeStruct((ROWS, COLS, 1, TILE), jnp.int32),
        ),
        in_specs=[VMEM, VMEM, SMEM, SMEM],
        out_specs=(VMEM,) * 3,
        scratch_shapes=spread_scratch(cap),
        compiler_params=params(20, collective_id=collective_id, has_side_effects=True),
    )(tv, idx, sections, plan)


OUT_TILES = ROWS * SLAB
UNUSED = ROWS - 1


def places(caps):
    cap_y, cap_left, cap_pair, cap_x, jobs = caps
    sizes = (
        ("left", cap_left + 8), ("here", cap_pair + 8), ("there", cap_pair + 8), ("keep", cap_x + 8),
        ("job_left", jobs + 8), ("job_right", jobs + 8), ("job_last", jobs + 8), ("job_col", jobs + 8),
        ("out", OUT_TILES), ("slot", OUT_TILES), ("touched", 8),
    )
    at, found = 0, {}
    for name, size in sizes:
        found[name] = at
        at += size
    return found, at


class Part:
    def __init__(self, ref, base):
        self.ref, self.base = ref, base

    def __getitem__(self, i):
        return self.ref[self.base + i]

    def __setitem__(self, i, value):
        self.ref[self.base + i] = value


def lists_kernel(
    caps, lists, owner, sections, plan, made, blank,
    zeros, row_left, inner_left, start, count, col_right, zero_sem,
):
    cap_y, cap_left, cap_pair, cap_x, jobs = caps
    zeros[...] = jnp.zeros_like(zeros)
    for p in range(ROWS):
        pltpu.make_async_copy(zeros, blank.at[pl.ds(p * TILE, TILE)], zero_sem.at[p]).start()
    part = {name: Part(made, base) for name, base in places(caps)[0].items()}
    keep_left, here, there, keep = part["left"], part["here"], part["there"], part["keep"]
    job_left, job_right = part["job_left"], part["job_right"]
    job_last, job_col = part["job_last"], part["job_col"]
    out_of, slot_of = part["out"], part["slot"]
    row_from, panel_from = Part(plan, ROW_FROM), Part(plan, PANEL_FROM)
    r, c = lax.axis_index("row"), lax.axis_index("col")
    x, zh = r >> 2, (r >> 1) & 1
    y, zl = c >> 1, c & 1
    secs = [sections[0], sections[1]]
    for m in range(cap_pair):
        here[m] = 0
        there[m] = 0
    for m in range(cap_x):
        keep[m] = 0

    def clear(m, _):
        for u in range(8):
            keep_left[m * 8 + u] = 0
        return 0

    lax.fori_loop(0, cap_left // 8, clear, 0)

    def left(g, n):
        j = row_from[g]
        line = g * COLS + (j >> 1)
        base = (j & 1) * BLOCK_COLS
        p = owner[g * ROWS + j] - r * ROWS
        for s in range(SECTIONS):
            for k in range(KB):
                rel = lists[line, base + (secs[s] >> 1) * KB + k] - secs[s] * ROWS
                keep_left[n] = g * ENTRIES + s * KB + k
                row_left[n] = p
                inner_left[n] = s * ROWS + rel
                n = n + ((rel >= 0) & (rel < ROWS)).astype(jnp.int32)
        return n

    left_count = lax.fori_loop(0, ROWS, left, jnp.int32(0))

    def ordered(g):
        a, b = panel_from[g], panel_from[ROWS + g]
        swap = (b < a).astype(jnp.int32)
        return ((swap, jnp.minimum(a, b)), (1 - swap, jnp.maximum(a, b)))

    def pairs(k2, carry):
        n_here, n_there = carry
        g = x * 4 + zh * 2 + k2
        used = jnp.int32(0)
        before = jnp.int32(-1)
        for s, j in ordered(g):
            source = j >> 1
            used = jnp.where(source == before, used, 0)
            before = source
            line = g * COLS + source
            base = (j & 1) * BLOCK_COLS
            near = (source & 1) == zl
            spot = k2 * 4 * cap_y + (source >> 1) * cap_y
            for z in range(2):
                mine = zl == z
                for k in range(KB):
                    b = y * 2 + z
                    rel = lists[line, base + b * KB + k] - b * BLOCK_COLS
                    ok = (rel >= 0) & (rel < SLAB)
                    take_here = (ok & near & mine).astype(jnp.int32)
                    take_there = (ok & near & jnp.logical_not(mine)).astype(jnp.int32)
                    at = jnp.minimum(spot + used, 8 * cap_y - 1)
                    here[n_here] = at
                    there[n_there] = at
                    n_here = n_here + take_here
                    n_there = n_there + take_there
                    used = used + ok.astype(jnp.int32)
        return n_here, n_there

    lax.fori_loop(0, 2, pairs, (jnp.int32(0), jnp.int32(0)))

    def per_x(xs, _):
        def per_zh(zs, n):
            def per_core(k2, carry):
                n, seen0, seen1 = carry
                g = xs * 4 + zs * 2 + k2
                for s, j in ordered(g):
                    source = j >> 1
                    sec = jnp.where(s == 0, secs[0], secs[1])
                    q = s * ROWS + owner[g * ROWS + j] - sec * ROWS
                    line = g * COLS + source
                    base = (j & 1) * BLOCK_COLS + c * KB
                    odd = source & 1
                    first = n
                    for k in range(KB):
                        rel = lists[line, base + k] - c * BLOCK_COLS
                        take = ((rel >= 0) & (rel < SLAB)).astype(jnp.int32)
                        seen = jnp.where(odd == 0, seen0, seen1)
                        at = jnp.minimum((zs * 2 + odd) * cap_pair + seen, 4 * cap_pair - 1)
                        col_right[xs * (cap_x + 1) + n] = rel
                        keep[jnp.where(xs == x, n, cap_x)] = at
                        n = n + take
                        seen0 = seen0 + take * (1 - odd)
                        seen1 = seen1 + take * odd
                    start[q] = xs * (cap_x + 1) + first
                    count[q] = n - first
                return n, seen0, seen1

            return lax.fori_loop(0, 2, per_core, (n, jnp.int32(0), jnp.int32(0)))[0]

        lax.fori_loop(0, 2, per_zh, jnp.int32(0))
        return 0

    lax.fori_loop(0, 4, per_x, 0)

    def no_slot(o, _):
        for u in range(16):
            slot_of[o * 16 + u] = -1
        return 0

    lax.fori_loop(0, OUT_TILES // 16, no_slot, 0)

    def no_job(n, _):
        for u in range(8):
            job_left[n * 8 + u] = 0
            job_right[n * 8 + u] = 0
            job_last[n * 8 + u] = -1
            job_col[n * 8 + u] = UNUSED
        return 0

    lax.fori_loop(0, jobs // 8, no_job, 0)

    def per_left(m, carry):
        first = row_left[m] * SLAB
        q = inner_left[m]
        begin = start[q]

        def per_right(t, carry):
            n, touched = carry
            at = begin + t
            col = col_right[at]
            o = first + col
            last = slot_of[o]
            fresh = last < 0
            job_left[n] = m
            job_right[n] = at - at // (cap_x + 1)
            job_last[n] = last
            job_col[n] = col
            job_col[jnp.where(fresh, jobs + 1, last)] = UNUSED
            slot_of[o] = n
            out_of[jnp.where(fresh, touched, OUT_TILES - 1)] = jnp.where(
                fresh, o, out_of[OUT_TILES - 1]
            )
            return n + 1, touched + fresh.astype(jnp.int32)

        return lax.fori_loop(0, count[q], per_right, carry)

    _, touched = lax.fori_loop(0, left_count, per_left, (jnp.int32(0), jnp.int32(0)))
    part["touched"][0] = touched
    for p in range(ROWS):
        pltpu.make_async_copy(zeros, blank.at[pl.ds(p * TILE, TILE)], zero_sem.at[p]).wait()


def make_lists(caps, lists, owner, sections, plan):
    cap_y, cap_left, cap_pair, cap_x, jobs = caps
    smem = lambda n: pltpu.SMEM((n,), jnp.int32)
    return pl.pallas_call(
        functools.partial(lists_kernel, caps),
        out_shape=(
            jax.ShapeDtypeStruct((places(caps)[1],), jnp.int32),
            jax.ShapeDtypeStruct((ROWS * TILE, SLAB * TILE), jnp.bfloat16),
        ),
        in_specs=[SMEM] * 4,
        out_specs=(SMEM, ANY),
        scratch_shapes=[
            pltpu.VMEM((TILE, SLAB * TILE), jnp.bfloat16),
            smem(cap_left + 8), smem(cap_left + 8), smem(PANEL), smem(PANEL), smem(4 * (cap_x + 1)),
            pltpu.SemaphoreType.DMA((ROWS,)),
        ],
        compiler_params=params(4),
    )(lists, owner, sections, plan)


UNROLL = 8


def gather_part(caps, keep_left, here, there, keep, strips, cand, left, right, held, other, send, recv):
    cap_y, cap_left, cap_pair, cap_x, jobs = caps
    r, c = lax.axis_index("row"), lax.axis_index("col")
    k = r % 2
    x, y = r // 4, c // 2
    me = ((r // 2) % 2) * 2 + c % 2
    cz = c + 1 - 2 * (c % 2)
    rz = (r // 4) * 4 + (r + 2) % 4
    cut = cap_left * 11 // 14
    zp, zh, zx = {"col": cz}, {"row": rz}, {"row": rz, "col": cz}
    yn, yb = {"col": (c + 2) % COLS}, {"col": (c + COLS - 2) % COLS}
    core = {"row": r + 1 - 2 * k}
    xn, xb = {"row": (r + 4) % ROWS}, {"row": (r + ROWS - 4) % ROWS}
    half, part = cap_pair // 2, cap_x // 2

    def pack_left(m, _):
        for u in range(4):
            e = keep_left[m * 4 + u]
            left[c, m * 4 + u] = strips[e // ENTRIES, e % ENTRIES]
        return 0

    lax.fori_loop(0, cap_left // 4, pack_left, 0)

    started, done = [], []

    def push(src, dst, to):
        n = len(started)
        copy = pltpu.make_async_remote_copy(
            src, dst, send.at[n], recv.at[n], device_id=to, device_id_type=MESH
        )
        copy.start()
        started.append(copy)
        return copy

    def go(origin, a, b, to):
        piece = left.at[origin, pl.ds(a, b - a)]
        return push(piece, piece, to)

    def gx(origin, a, b, to):
        piece = right.at[origin, k, pl.ds(a, b - a)]
        return push(piece, piece, to)

    def arrived(copy):
        copy.wait_recv()
        done.append(copy)

    end = cap_left
    a_mid, b_mid = cut // 2, (cut + end) // 2
    c_m, c_p, c_o = (c + COLS - 2) % COLS, (c + 2) % COLS, (c + 4) % COLS
    z_m, z_p = (cz + COLS - 2) % COLS, (cz + 2) % COLS
    x_m, x_p, x_o = (x + 3) % 4, (x + 1) % 4, (x + 2) % 4
    z_of_p, z_of_h = (me // 2) * 2 + (me + 1) % 2, (me + 2) % 4
    z_of_x = (z_of_p + 2) % 4

    k1 = go(c, 0, cut, zp)
    k2 = go(c, 0, cut, yn)
    k3 = go(c, 0, cut, yb)
    k10 = go(c, cut, end, yn)
    k11 = go(c, cut, end, yb)
    k12 = go(c, cut, end, zp)
    yield
    for m in range(half):
        e = there[k * half + m]
        other[m] = cand[e // (4 * cap_y), (e // cap_y) % 4, e % cap_y]
    for m in range(cap_pair):
        e = here[m]
        held[me, m // half, m % half] = cand[e // (4 * cap_y), (e // cap_y) % 4, e % cap_y]

    s1 = push(other, held.at[me, k], zp)
    s2 = push(other, held.at[me, k], zx)
    s3 = push(held.at[me, k], held.at[me, k], zh)
    arrived(s1)
    t1 = push(held.at[z_of_p, k], held.at[z_of_p, k], core)
    arrived(s2)
    t2 = push(held.at[z_of_x, k], held.at[z_of_x, k], core)
    arrived(s3)
    t3 = push(held.at[z_of_h, k], held.at[z_of_h, k], core)
    arrived(k2)
    k6 = go(c_m, 0, a_mid, yn)
    arrived(k3)
    k7 = go(c_p, a_mid, cut, yb)
    arrived(k1)
    k4 = go(cz, 0, cut, yn)
    k5 = go(cz, 0, cut, yb)
    arrived(t1)
    arrived(t2)
    arrived(t3)
    for m in range(cap_x):
        e = keep[m]
        right[x, m // part, m % part] = held[e // cap_pair, (e // half) % 2, e % half]
    u1 = gx(x, 0, part, xn)
    u2 = gx(x, 0, part, xb)
    arrived(k10)
    k13 = go(c_m, cut, b_mid, yn)
    k14 = go(c_m, cut, end, zp)
    arrived(k11)
    k15 = go(c_p, b_mid, end, yb)
    k16 = go(c_p, cut, end, zp)
    arrived(u1)
    u3 = gx(x_m, 0, part // 2, xn)
    u4 = gx(x_m, 0, part, core)
    arrived(u2)
    u5 = gx(x_p, part // 2, part, xb)
    u6 = gx(x_p, 0, part, core)
    arrived(k4)
    k8 = go(z_m, 0, a_mid, yn)
    arrived(k5)
    k9 = go(z_p, a_mid, cut, yb)
    arrived(k13)
    k17 = go(c_o, cut, b_mid, zp)
    arrived(k15)
    k18 = go(c_o, b_mid, end, zp)
    arrived(u3)
    u7 = gx(x_o, 0, part // 2, core)
    arrived(u5)
    u8 = gx(x_o, part // 2, part, core)
    for copy in started:
        if not any(copy is seen for seen in done):
            copy.wait_recv()
    yield started


def product_part(
    caps, job_left, job_right, job_last, job_col, left, right, sums, totals, rows, parts,
    total_send, total_recv,
):
    cap_y, cap_left, cap_pair, cap_x, jobs = caps
    r = lax.axis_index("row")
    part = cap_x // 2
    rows[...] = jnp.zeros_like(rows)
    line = lax.broadcasted_iota(jnp.int32, (ROWS, TILE), 0)

    def multiply(g, _):
        results = []
        for u in range(UNROLL):
            n = g * UNROLL + u
            a = left[:, job_left[n]].reshape(TILE, TILE)
            e = job_right[n]
            b = right[e // cap_x, (e // part) % 2, e % part]
            results.append(jnp.dot(a, b, preferred_element_type=jnp.float32))
        added = jnp.zeros((ROWS, TILE), jnp.float32)
        for u in range(UNROLL):
            n = g * UNROLL + u
            last = job_last[n]
            old = sums[jnp.maximum(last, 0)]
            value = results[u] + jnp.where(last >= 0, old, 0.0)
            sums[n] = value
            square = (value * value).reshape(TILE // 8, 8, TILE).sum(axis=0)
            square = square.sum(axis=0, keepdims=True)
            added = added + jnp.where(line == job_col[n], square, 0.0)
        rows[...] += added
        return 0

    lax.fori_loop(0, jobs // UNROLL, multiply, 0)
    parts[r] = rows[...]
    copies = []
    for d in range(1, ROWS):
        copy = pltpu.make_async_remote_copy(
            rows, parts.at[r], total_send.at[d], total_recv.at[d],
            device_id={"row": (r + d) % ROWS}, device_id_type=MESH,
        )
        copy.start()
        copies.append(copy)
    for copy in copies:
        copy.wait_recv()
    totals[...] = parts[...].sum(axis=0)
    return copies


def multiply_kernel(
    caps, strips, cand, plan, sums, totals,
    left, right, held, other, rows, parts, send, recv, total_send, total_recv,
):
    greet(lax.axis_index("row"), lax.axis_index("col"))
    found = {name: Part(plan, base) for name, base in places(caps)[0].items()}
    meet()
    steps = gather_part(
        caps, found["left"], found["here"], found["there"], found["keep"],
        strips, cand, left, right, held, other, send, recv,
    )
    next(steps)
    started = next(steps)
    started += product_part(
        caps, found["job_left"], found["job_right"], found["job_last"], found["job_col"],
        left, right, sums, totals, rows, parts, total_send, total_recv,
    )
    for copy in started:
        copy.wait_send()


COPIES = 32


def multiply_scratch(caps):
    cap_y, cap_left, cap_pair, cap_x, jobs = caps
    bf, f32 = jnp.bfloat16, jnp.float32
    dma = pltpu.SemaphoreType.DMA
    return (
        [
            pltpu.VMEM((COLS, cap_left, STRIP, TILE), bf),
            pltpu.VMEM((4, 2, cap_x // 2, TILE, TILE), bf),
            pltpu.VMEM((4, 2, cap_pair // 2, TILE, TILE), bf),
            pltpu.VMEM((cap_pair // 2, TILE, TILE), bf),
            pltpu.VMEM((ROWS, TILE), f32),
            pltpu.VMEM((ROWS, ROWS, TILE), f32),
        ]
        + [dma((COPIES,))] * 2
        + [dma((ROWS,))] * 2
    )


def multiply(caps, collective_id, strips, cand, plan):
    jobs, f32 = caps[4], jnp.float32
    mib = 24 + jobs * TILE * TILE * 4 // (1 << 20)
    return pl.pallas_call(
        functools.partial(multiply_kernel, caps),
        out_shape=(
            jax.ShapeDtypeStruct((jobs, TILE, TILE), f32),
            jax.ShapeDtypeStruct((ROWS, TILE), f32),
        ),
        in_specs=[VMEM, VMEM, SMEM],
        out_specs=(VMEM, VMEM),
        scratch_shapes=multiply_scratch(caps),
        compiler_params=params(mib, collective_id=collective_id, has_side_effects=True),
    )(strips, cand, plan)


class Row:
    def __init__(self, ref, row):
        self.ref, self.row = ref, row

    def __getitem__(self, i):
        return self.ref[self.row, i]


def whole_kernel(
    caps, tv, idx, owner, sections, plan,
    sums, totals, blank, made, over,
    strips, cand, lists, zeros, scalars, zero_sem, plan_sem, *scratch,
):
    r, c = lax.axis_index("row"), lax.axis_index("col")
    greet(r, c)
    zeros[...] = jnp.zeros_like(zeros)
    clears = [
        pltpu.make_async_copy(zeros, blank.at[pl.ds(p * TILE, TILE)], zero_sem.at[p])
        for p in range(ROWS)
    ]
    first, second = scratch[:16], scratch[16:]
    left, right, held, other, rows, parts, send, recv, total_send, total_recv = second
    row = lambda n: Row(scalars, n)
    steps = gather_part(
        caps, row(ROW_LEFT), row(ROW_HERE), row(ROW_THERE), row(ROW_KEEP),
        strips, cand, left, right, held, other, send, recv,
    )

    def on_lists():
        found, excess = vector_plan(caps, lists, owner, sections, r, c)
        made[...] = found
        over[...] = excess
        move = pltpu.make_async_copy(made, scalars, plan_sem)
        move.start()
        for copy in clears:
            copy.start()
        move.wait()

    started = spread_part(
        caps[0], tv, idx, sections, plan, strips, cand, lists, *first,
        meet, on_lists, lambda: next(steps),
    )
    started = started + next(steps)
    started += product_part(
        caps, row(ROW_JOB), row(ROW_TILE), row(ROW_LAST), row(ROW_COL),
        left, right, sums, totals, rows, parts, total_send, total_recv,
    )
    for copy in started:
        copy.wait_send()
    for copy in clears:
        copy.wait()


def whole(caps, collective_id, tv, idx, owner, sections, plan):
    bf, f32, i32 = jnp.bfloat16, jnp.float32, jnp.int32
    dma = pltpu.SemaphoreType.DMA
    return pl.pallas_call(
        functools.partial(whole_kernel, caps),
        out_shape=(
            jax.ShapeDtypeStruct((caps[4], TILE, TILE), f32),
            jax.ShapeDtypeStruct((ROWS, TILE), f32),
            jax.ShapeDtypeStruct((ROWS * TILE, SLAB * TILE), bf),
            jax.ShapeDtypeStruct((ROWS, TILE), i32),
            jax.ShapeDtypeStruct((TILE, TILE), f32),
        ),
        in_specs=[VMEM, VMEM, VMEM, SMEM, SMEM],
        out_specs=(VMEM, VMEM, ANY, VMEM, VMEM),
        scratch_shapes=[
            pltpu.VMEM((ROWS, ENTRIES, STRIP, TILE), bf),
            pltpu.VMEM((2, 4, caps[0], TILE, TILE), bf),
            pltpu.VMEM((ROWS, COLS, 1, TILE), i32),
            pltpu.VMEM((TILE, SLAB * TILE), bf),
            pltpu.SMEM((ROWS, TILE), i32),
            dma((ROWS,)),
            dma,
        ]
        + spread_scratch(caps[0])
        + multiply_scratch(caps),
        compiler_params=params(40, collective_id=collective_id, has_side_effects=True),
    )(tv, idx, owner, sections, plan)


def write_listed_kernel(jobs, sums, blank, plan, totals, out, block, factor, out_sem):
    count = float(ROWS * ROWS * TILE)
    factor[...] = count / (totals[...] + 1e-06)

    def place(n):
        o = plan[ROW_OUT, n]
        p = jnp.maximum(o, 0) // SLAB
        col = jnp.maximum(o, 0) - p * SLAB
        row = pl.ds(pl.multiple_of(p * TILE, TILE), TILE)
        lanes = pl.ds(pl.multiple_of(col * TILE, TILE), TILE)
        return o, col, pltpu.make_async_copy(block.at[n], out.at[row, lanes], out_sem)

    def scale(n, _):
        o, col, copy = place(n)

        @pl.when(o >= 0)
        def _():
            value = sums[n]
            block[n] = (value * value * factor[pl.ds(col, 1), :]).astype(jnp.bfloat16)
            copy.start()

        return 0

    lax.fori_loop(0, jobs, scale, 0)

    def drain(n, _):
        o, _, copy = place(n)

        @pl.when(o >= 0)
        def _():
            copy.wait()

        return 0

    lax.fori_loop(0, jobs, drain, 0)


def write_listed(jobs, sums, blank, plan, totals):
    return pl.pallas_call(
        functools.partial(write_listed_kernel, jobs),
        out_shape=jax.ShapeDtypeStruct((ROWS * TILE, SLAB * TILE), jnp.bfloat16),
        in_specs=[VMEM, ANY, SMEM, VMEM],
        out_specs=ANY,
        input_output_aliases={1: 0},
        scratch_shapes=[
            pltpu.VMEM((jobs, TILE, TILE), jnp.bfloat16),
            pltpu.VMEM((ROWS, TILE), jnp.float32),
            pltpu.SemaphoreType.DMA,
        ],
        compiler_params=params(12),
    )(sums, blank, plan, totals)


def write_kernel(at, sums, blank, plan, totals, out, block, factor, out_sem):
    touched = plan[at["touched"]]
    count = float(ROWS * ROWS * TILE)
    factor[...] = count / (totals[...] + 1e-06)

    def place(i):
        o = plan[at["out"] + i]
        p = o // SLAB
        col = o - p * SLAB
        row = pl.ds(pl.multiple_of(p * TILE, TILE), TILE)
        lanes = pl.ds(pl.multiple_of(col * TILE, TILE), TILE)
        return o, col, pltpu.make_async_copy(block.at[i], out.at[row, lanes], out_sem)

    def scale(i, _):
        o, col, copy = place(i)
        value = sums[plan[at["slot"] + o]]
        block[i] = (value * value * factor[pl.ds(col, 1), :]).astype(jnp.bfloat16)
        copy.start()
        return 0

    lax.fori_loop(0, touched, scale, 0)

    def drain(i, _):
        place(i)[2].wait()
        return 0

    lax.fori_loop(0, touched, drain, 0)


def write(caps, sums, blank, plan, totals):
    jobs = caps[4]
    mib = 10 + jobs * TILE * TILE * 4 // (1 << 20)
    return pl.pallas_call(
        functools.partial(write_kernel, places(caps)[0]),
        out_shape=jax.ShapeDtypeStruct((ROWS * TILE, SLAB * TILE), jnp.bfloat16),
        in_specs=[VMEM, ANY, SMEM, VMEM],
        out_specs=ANY,
        input_output_aliases={1: 0},
        scratch_shapes=[
            pltpu.VMEM((OUT_TILES, TILE, TILE), jnp.bfloat16),
            pltpu.VMEM((ROWS, TILE), jnp.float32),
            pltpu.SemaphoreType.DMA,
        ],
        compiler_params=params(mib),
    )(sums, blank, plan, totals)


def per_device(tile_values, tile_columns, owner_map, section_rows):
    flat = tile_columns.reshape(-1)
    idx = jnp.pad(flat, (0, TILE - flat.shape[0])).reshape(1, TILE)
    tv = tile_values.reshape(2 * COLS * KB, TILE, TILE)
    owner_rows = owner_map.reshape(2, TILE)

    def full():
        plan = prep(FULL[0], owner_map, section_rows, flat)
        strips, cand, lists = spread(FULL[0], 2, tv, idx, section_rows, plan)
        made, blank = make_lists(
            FULL, lists.reshape(ROWS * COLS, TILE), owner_map, section_rows, plan
        )
        sums, totals = multiply(FULL, 3, strips, cand, made)
        return write(FULL, sums, blank, made, totals)

    plan = prep(FAST[0], owner_map, section_rows, flat)
    *got, over = whole(FAST, 0, tv, idx, owner_rows, section_rows, plan)

    def packed(sums, totals, blank, made):
        return write_listed(FAST[4], sums, blank, made, totals)

    return lax.cond(jnp.max(over) > 0, lambda *_: full(), packed, *got)


def solution(mesh):
    both = ("row", "col")
    in_specs = (P(both, None, None, None, None), P(both, None, None), P(), P())
    return jax.shard_map(
        per_device, mesh=mesh, in_specs=in_specs, out_specs=P("row", "col"), check_vma=False
    )
```

```python
import functools

import jax
import jax.numpy as jnp
from jax import lax
from jax.experimental import pallas as pl
from jax.experimental.pallas import tpu as pltpu
from jax.sharding import PartitionSpec as P

TILE = 128
KB = 4
SLAB = 12
SECTIONS = 2
ROWS = 16
COLS = 8
BLOCK_COLS = 32
STRIP = TILE // COLS
ENTRIES = SECTIONS * KB
PANEL = SECTIONS * ROWS
FAST = (8, 56, 6, 16, 80)
FULL = (16, 128, 8, 32, 512)
MESH = pl.DeviceIdType.MESH
VMEM = pl.BlockSpec(memory_space=pltpu.VMEM)
SMEM = pl.BlockSpec(memory_space=pltpu.SMEM)
ANY = pl.BlockSpec(memory_space=pl.ANY)
HBM = pl.BlockSpec(memory_space=pltpu.HBM)


def params(mib, **kw):
    return pltpu.CompilerParams(vmem_limit_bytes=mib << 20, **kw)


SEND, ROW_FROM, PANEL_FROM, PICKS = 0, ROWS, 2 * ROWS, 4 * ROWS


def prep_kernel(cap, owner, sections, cols, plan, blank, inverse, zeros, zero_sem):
    r, c = lax.axis_index("row"), lax.axis_index("col")
    zeros[...] = jnp.zeros_like(zeros)
    clears = [
        pltpu.make_async_copy(zeros, blank.at[pl.ds(p * TILE, TILE)], zero_sem.at[p])
        for p in range(ROWS)
    ]
    for copy in clears:
        copy.start()

    def invert(g, _):
        for j in range(ROWS):
            inverse[owner[g * ROWS + j]] = g * ROWS + j
        return 0

    lax.fori_loop(0, ROWS, invert, 0)
    secs = [sections[0], sections[1]]
    for j in range(ROWS):
        plan[SEND + (owner[r * ROWS + j] >> 4)] = j
        t = inverse[r * ROWS + j]
        plan[ROW_FROM + (t >> 4)] = t & 15
        for s in range(SECTIONS):
            t = inverse[secs[s] * ROWS + j]
            plan[PANEL_FROM + s * ROWS + (t >> 4)] = t & 15
    wanted = []
    for i in range(2):
        block = owner[r * ROWS + c * 2 + i] >> 4
        wanted.append((block == secs[0]) | (block == secs[1]))
    room = cap + 1

    def per_y(yd, _):
        for m in range(room):
            plan[PICKS + yd * room + m] = 0
        count = jnp.int32(0)
        for i in range(2):
            for z in range(2):
                b = yd * 2 + z
                for k in range(KB):
                    rel = cols[i * BLOCK_COLS + b * KB + k] - b * BLOCK_COLS
                    take = wanted[i] & (rel >= 0) & (rel < SLAB)
                    plan[PICKS + yd * room + count] = i * BLOCK_COLS + b * KB + k
                    count = jnp.minimum(count + take.astype(jnp.int32), cap)
        return 0

    lax.fori_loop(0, 4, per_y, 0)
    for copy in clears:
        copy.wait()


def prep(cap, owner, sections, cols):
    return pl.pallas_call(
        functools.partial(prep_kernel, cap),
        out_shape=(
            jax.ShapeDtypeStruct((PICKS + 4 * (cap + 1),), jnp.int32),
            jax.ShapeDtypeStruct((ROWS * TILE, SLAB * TILE), jnp.bfloat16),
        ),
        in_specs=[SMEM] * 3,
        out_specs=(SMEM, ANY),
        scratch_shapes=[
            pltpu.SMEM((ROWS * ROWS,), jnp.int32),
            pltpu.VMEM((TILE, SLAB * TILE), jnp.bfloat16),
            pltpu.SemaphoreType.DMA((ROWS,)),
        ],
        compiler_params=params(4),
    )(owner, sections, cols)


def iota(dim):
    return lax.broadcasted_iota(jnp.int32, (TILE, TILE), dim)


def picked(mask):
    return jnp.where(mask, 1.0, 0.0).astype(jnp.bfloat16)


def mm(a, b, dims=((1,), (0,))):
    return lax.dot_general(a, b, (dims, ((), ())), preferred_element_type=jnp.float32)


ROW_LEFT, ROW_HERE, ROW_THERE, ROW_KEEP = 0, 1, 2, 3
ROW_JOB, ROW_TILE, ROW_LAST, ROW_COL, ROW_OUT = 4, 5, 6, 7, 8


def vector_plan(caps, lists, owner, sections, r, c):
    cap_y, cap_left, cap_pair, cap_x, most_jobs = caps
    f32, bf, i32 = jnp.float32, jnp.bfloat16, jnp.int32
    cols = lists[...].reshape(TILE, TILE)
    line, lane = iota(0), iota(1)
    before = picked(line < lane)
    after = picked(lane < line)
    ones = jnp.ones((TILE, TILE), bf)
    same = picked(line == lane)
    nn, tn, nt = ((1,), (0,)), ((0,), (0,)), ((1,), (1,))
    small = lambda v: v.astype(f32).astype(bf)
    whole = lambda v: v.astype(i32)
    places_, blocks = [], []
    for i in range(2):
        total = jnp.zeros((TILE, TILE), f32)
        for h in range(2):
            row = jnp.broadcast_to(owner[h : h + 1, :].astype(f32), (TILE, TILE))
            total = total + mm(picked(lane + h * TILE == 2 * line + i), row.astype(bf), nt)
        places_.append(whole(total))
        blocks.append(places_[i] >> 4)
    mine = jnp.where(lane < BLOCK_COLS, blocks[0], blocks[1])
    sec0, sec1 = sections[0], sections[1]
    real = lane < 2 * BLOCK_COLS
    b = (lane & (BLOCK_COLS - 1)) >> 2
    rel = cols - b * BLOCK_COLS
    slab_mask = real & (rel >= 0) & (rel < SLAB) & ((mine == sec0) | (mine == sec1))
    slab = picked(slab_mask)
    shifted = small(jnp.where(real, cols + 1, 0))
    lane_b = (line & (BLOCK_COLS - 1)) >> 2
    row_real = line < 2 * BLOCK_COLS

    per_y = mm(slab, picked(row_real & ((lane_b >> 1) == lane)))
    per_b = small(mm(slab, picked(row_real & (lane_b == lane))))
    per_pair = mm(picked(((line >> 3) == (lane >> 3)) & ((line & 1) == (lane & 1))), per_b)
    per_x = mm(picked((line >> 5) == (lane >> 5)), per_b)
    section = lane >> 4
    target = jnp.where(section == 0, sec0, sec1) * ROWS + (lane & (ROWS - 1))
    target = jnp.where(section < SECTIONS, target, 2 * TILE + 1)
    source = jnp.where((lane >> 2) % SECTIONS == 0, sec0, sec1) >> 1
    chosen, panel_tiles = [], jnp.zeros((TILE, TILE), f32)
    for i in range(2):
        wanted = i * BLOCK_COLS + source * KB + lane % KB
        chosen.append(mm(shifted, picked((lane < ENTRIES) & (line == wanted))))
        own = (line >= i * BLOCK_COLS) & (line < (i + 1) * BLOCK_COLS)
        mine_b = small(mm(slab, picked(own & (lane_b == lane))))
        panel_tiles = panel_tiles + mm(picked(places_[i] == target), mine_b, tn)
    panel_tiles = small(panel_tiles)
    rows = jnp.zeros((TILE, TILE), f32)
    jobs = jnp.zeros((TILE, TILE), f32)
    for i in range(2):
        hits = jnp.zeros((TILE, TILE), f32)
        for e in range(ENTRIES):
            at = whole(chosen[i][:, e : e + 1]) - 1
            hits = hits + jnp.where((at == target) & (section == e // KB), 1.0, 0.0)
        hits = small(hits)
        block = picked(blocks[i] == lane)
        rows = rows + mm(block, small(mm(hits, ones)), tn)
        jobs = jobs + mm(block, small(mm(hits, panel_tiles)), tn)
    over = jnp.maximum(per_y - cap_y, rows - cap_left)
    over = jnp.maximum(over, jnp.maximum(per_pair - cap_pair, per_x - cap_x))
    over = jnp.maximum(over, jobs - most_jobs)

    got = jnp.zeros((TILE, TILE), f32)
    place = jnp.zeros((TILE, TILE), f32)
    for i in range(2):
        group = picked(((line >> 3) == lane) & (blocks[i] == r))
        got = got + mm(group, small(chosen[i]), tn)
        place = place + mm(group, small(places_[i]), tn)
    line16 = lax.broadcasted_iota(i32, (ROWS, TILE), 0)
    lane16 = lax.broadcasted_iota(i32, (ROWS, TILE), 1)
    got, place = whole(got[:ROWS]) - 1, whole(place[:ROWS]) - r * ROWS
    inner = got - jnp.where(lane16 < KB, sec0, sec1) * ROWS
    ok = (lane16 < ENTRIES) & (inner >= 0) & (inner < ROWS)
    inner = inner + (lane16 >> 2) * ROWS
    flags = picked(ok)
    spare = jnp.zeros((TILE - ROWS, TILE), bf)
    padded = jnp.concatenate([flags, spare], axis=0)
    rank = mm(padded, before) + mm(after, small(mm(padded, ones)))
    rank = jnp.where(ok, whole(rank[:ROWS]), -1)
    zero16 = jnp.zeros((ROWS, TILE), i32)
    code, left_p, left_q = zero16, zero16, zero16
    for e in range(ENTRIES):
        hit = rank[:, e : e + 1] == lane16
        code = code + jnp.where(hit, line16 * ENTRIES + e, 0)
        left_p = left_p + jnp.where(hit, place[:, e : e + 1], 0)
        left_q = left_q + jnp.where(hit, inner[:, e : e + 1] + 1, 0)
    code = code.sum(axis=0, keepdims=True)
    left_p = left_p.sum(axis=0, keepdims=True)
    left_q = left_q.sum(axis=0, keepdims=True)

    def lanes_of(column):
        wanted = (lane >> 2) * BLOCK_COLS + column * KB + lane % KB
        return picked((lane < 2 * KB) & (line == wanted))

    x, y, zl = r // 4, c // 2, c % 2
    to_here, to_there = lanes_of(c), lanes_of(c + 1 - 2 * zl)
    of_y = slab_mask & ((b >> 1) == y)
    used = small(mm(picked(of_y), before))
    spot = ((line & 7) >> 1) * cap_y
    eligible = ((line >> 3) == r) & ((line & 1) == zl)

    def packed_row(key, values):
        sums = [jnp.zeros((TILE, TILE), i32) for _ in values]
        for u in range(2 * KB):
            hit = key[:, u : u + 1] == lane
            for n, value in enumerate(values):
                sums[n] = sums[n] + jnp.where(hit, value(u), 0)
        return [v.sum(axis=0, keepdims=True) for v in sums]

    def from_y(choose):
        flag = (mm(slab, choose) > 0.5) & eligible
        number = picked(flag)
        order = whole(mm(number, before) + mm(after, small(mm(number, ones))))
        at = spot + whole(mm(used, choose))
        key = jnp.where(flag, order, -1)
        return packed_row(key, [lambda u: at[:, u : u + 1]])[0]

    here, there = from_y(to_here), from_y(to_there)

    flag = mm(slab, to_here) > 0.5
    number = picked(flag)
    ahead = mm(number, before)
    rest = small(mm(number, ones))
    in_x = whole(ahead + mm(picked((lane < line) & ((line >> 5) == (lane >> 5))), rest))
    same_pair = (lane < line) & ((line >> 3) == (lane >> 3)) & ((line & 1) == (lane & 1))
    in_pair = whole(ahead + mm(picked(same_pair), rest))
    at = ((((line >> 4) & 1) * 2 + (line & 1)) * 2 + ((line >> 3) & 1)) * cap_pair + in_pair
    key = jnp.where(flag & ((line >> 5) == x), in_x, -1)
    keep = packed_row(key, [lambda u: at[:, u : u + 1]])[0]
    key = jnp.where(flag, (line >> 5) * cap_x + in_x, -1)
    grid_col = whole(mm(shifted, to_here)) - 1 - c * BLOCK_COLS
    panel_of = []
    for i in range(2):
        q = jnp.where(blocks[i] == sec0, places_[i] - sec0 * ROWS, places_[i] - sec1 * ROWS + ROWS)
        panel_of.append(q + 1)
    right_q, right_col = packed_row(
        key, [lambda u: panel_of[u // KB], lambda u: grid_col[:, u : u + 1]]
    )

    wide = lambda row: jnp.broadcast_to(row, (TILE, TILE))
    left_q_down = whole(mm(same, small(wide(left_q)), nt))
    pair = picked((left_q_down == wide(right_q)) & (left_q_down > 0))
    number = small(mm(pair, ones))
    begin_row = whole(mm(number, before, tn))
    number_row = whole(mm(number, same, tn))
    job_of = picked((line >= begin_row) & (line < begin_row + number_row))
    begin = mm(job_of, small(mm(after, number)))
    turn = mm(job_of, small(mm(pair, before)))
    choice = (mm(job_of, pair) > 0.5) & (whole(turn) == line - whole(begin))
    choice = picked(choice)
    line8 = lax.broadcasted_iota(i32, (ROWS, TILE), 0)
    stack = jnp.where(line8 == 0, lane16, jnp.where(line8 == 1, jnp.broadcast_to(left_p, (ROWS, TILE)), 0))
    by_left = whole(mm(small(stack), job_of, nt))
    stack = jnp.where(line8 == 0, lane16, jnp.where(line8 == 1, jnp.broadcast_to(right_col, (ROWS, TILE)), 1))
    by_right = whole(mm(small(stack), choice, nt))
    job_left, job_p = by_left[0:1], by_left[1:2]
    job_tile, job_col, valid = by_right[0:1], by_right[1:2], by_right[2:3] > 0
    out = jnp.where(valid, job_p * SLAB + job_col, 255)
    out_row = wide(out)
    out_down = whole(mm(same, small(out_row), nt))
    alike = out_down == out_row
    last = jnp.where(alike & (line < lane), line, -1).max(axis=0, keepdims=True)
    later = jnp.where(alike & (line > lane), 1, 0).max(axis=0, keepdims=True)
    final = valid & (later == 0)
    made = [
        jnp.clip(code, 0, ROWS * ENTRIES - 1),
        jnp.clip(here, 0, 4 * cap_y - 1),
        jnp.clip(there, 0, 4 * cap_y - 1),
        jnp.clip(keep, 0, 8 * cap_pair - 1),
        jnp.clip(job_left, 0, cap_left - 1),
        jnp.clip(job_tile, 0, 4 * cap_x - 1),
        jnp.where(valid, jnp.clip(last, -1, most_jobs - 1), -1),
        jnp.where(final, job_col, UNUSED),
        jnp.where(final, jnp.clip(out, 0, OUT_TILES - 1), -1),
    ]
    plan = jnp.zeros((ROWS, TILE), i32)
    for n, row in enumerate(made):
        plan = jnp.where(line16 == n, jnp.broadcast_to(row, (ROWS, TILE)), plan)
    return plan, over


def spread_part(
    cap, tv, idx, sections, pick, sender,
    strips, cand, lists,
    left_out, left_in, right_out, row_out,
    s_idx, r_idx, s_left, r_left, s_right, r_right, s_list, r_list, s_row, r_row,
    meet, on_lists, on_right, on_strips,
):
    r, c = lax.axis_index("row"), lax.axis_index("col")
    y, z = c // 2, c % 2
    for i in range(2):
        for s in range(SECTIONS):
            source = sections[s] // 2
            for k in range(KB):
                for h in range(COLS):
                    left_out[h, i * ENTRIES + s * KB + k] = tv[
                        i * BLOCK_COLS + source * KB + k, h * STRIP : (h + 1) * STRIP, :
                    ]

    def pack(yd, _):
        for m in range(cap):
            right_out[yd, m] = tv[pick(yd, m)]
        return 0

    lax.fori_loop(0, 4, pack, 0)
    lists[r, c] = idx[...]
    left_in[c] = left_out[c]
    cand[y] = right_out[y]
    meet()

    idx_copies, left_copies, right_copies = [], [], []
    for d in range(1, COLS):
        to = (c + d) % COLS
        copy = pltpu.make_async_remote_copy(
            idx, lists.at[r, c], s_idx.at[d], r_idx.at[d], device_id={"col": to}, device_id_type=MESH
        )
        copy.start()
        idx_copies.append(copy)
    for d in range(1, COLS):
        to = (c + d) % COLS
        copy = pltpu.make_async_remote_copy(
            left_out.at[to], left_in.at[c], s_left.at[d], r_left.at[d],
            device_id={"col": to}, device_id_type=MESH,
        )
        copy.start()
        left_copies.append(copy)
    for d in (2, 1, 3):
        to = (y + d) % 4
        copy = pltpu.make_async_remote_copy(
            right_out.at[to], cand.at[y], s_right.at[d], r_right.at[d],
            device_id={"col": to * 2 + z}, device_id_type=MESH,
        )
        copy.start()
        right_copies.append(copy)
    for copy in idx_copies:
        copy.wait_recv()
    list_copies = []
    for d in range(1, ROWS):
        to = (r + d) % ROWS
        copy = pltpu.make_async_remote_copy(
            lists.at[r], lists.at[r], s_list.at[d], r_list.at[d],
            device_id={"row": to}, device_id_type=MESH,
        )
        copy.start()
        list_copies.append(copy)
    for copy in left_copies:
        copy.wait_recv()

    def reorder(t, _):
        j = sender(t)
        for e in range(ENTRIES):
            row_out[t, e] = left_in[j // 2, (j % 2) * ENTRIES + e]
        return 0

    lax.fori_loop(0, ROWS, reorder, 0)
    strips[r] = row_out[r]
    row_copies = []
    for d in range(1, ROWS):
        to = (r + d) % ROWS
        copy = pltpu.make_async_remote_copy(
            row_out.at[to], strips.at[r], s_row.at[d], r_row.at[d],
            device_id={"row": to}, device_id_type=MESH,
        )
        copy.start()
        row_copies.append(copy)
    for copy in list_copies:
        copy.wait_recv()
    on_lists()
    for copy in right_copies:
        copy.wait_recv()
    on_right()
    for copy in row_copies:
        copy.wait_recv()
    on_strips()
    return idx_copies + left_copies + right_copies + list_copies + row_copies


def greet(r, c):
    barrier = pltpu.get_barrier_semaphore()
    for d in range(1, COLS):
        pl.semaphore_signal(barrier, inc=1, device_id={"col": (c + d) % COLS}, device_id_type=MESH)
    for d in range(1, ROWS):
        pl.semaphore_signal(barrier, inc=1, device_id={"row": (r + d) % ROWS}, device_id_type=MESH)
    across = {"row": (r // 4) * 4 + (r + 2) % 4, "col": c + 1 - 2 * (c % 2)}
    pl.semaphore_signal(barrier, inc=1, device_id=across, device_id_type=MESH)


def meet():
    pl.semaphore_wait(pltpu.get_barrier_semaphore(), COLS - 1 + ROWS - 1 + 1)


def spread_kernel(cap, tv, idx, sections, plan, strips, cand, lists, *scratch):
    greet(lax.axis_index("row"), lax.axis_index("col"))
    nothing = lambda: None
    pick = lambda yd, m: plan[PICKS + yd * (cap + 1) + m]
    sender = lambda t: plan[SEND + t]
    started = spread_part(
        cap, tv, idx, sections, pick, sender, strips, cand, lists, *scratch, meet, *[nothing] * 3
    )
    for copy in started:
        copy.wait_send()


def spread_scratch(cap):
    bf = jnp.bfloat16
    dma = pltpu.SemaphoreType.DMA
    return (
        [
            pltpu.VMEM((COLS, 2 * ENTRIES, STRIP, TILE), bf),
            pltpu.VMEM((COLS, 2 * ENTRIES, STRIP, TILE), bf),
            pltpu.VMEM((4, cap, TILE, TILE), bf),
            pltpu.VMEM((ROWS, ENTRIES, STRIP, TILE), bf),
        ]
        + [dma((COLS,))] * 6
        + [dma((ROWS,))] * 4
    )


def spread(cap, collective_id, tv, idx, sections, plan):
    bf = jnp.bfloat16
    return pl.pallas_call(
        functools.partial(spread_kernel, cap),
        out_shape=(
            jax.ShapeDtypeStruct((ROWS, ENTRIES, STRIP, TILE), bf),
            jax.ShapeDtypeStruct((4, cap, TILE, TILE), bf),
            jax.ShapeDtypeStruct((ROWS, COLS, 1, TILE), jnp.int32),
        ),
        in_specs=[VMEM, VMEM, SMEM, SMEM],
        out_specs=(VMEM,) * 3,
        scratch_shapes=spread_scratch(cap),
        compiler_params=params(20, collective_id=collective_id, has_side_effects=True),
    )(tv, idx, sections, plan)


OUT_TILES = ROWS * SLAB
UNUSED = ROWS - 1


def places(caps):
    cap_y, cap_left, cap_pair, cap_x, jobs = caps
    sizes = (
        ("left", cap_left + 8), ("here", cap_pair + 8), ("there", cap_pair + 8), ("keep", cap_x + 8),
        ("job_left", jobs + 8), ("job_right", jobs + 8), ("job_last", jobs + 8), ("job_col", jobs + 8),
        ("out", OUT_TILES), ("slot", OUT_TILES), ("touched", 8),
    )
    at, found = 0, {}
    for name, size in sizes:
        found[name] = at
        at += size
    return found, at


class Part:
    def __init__(self, ref, base):
        self.ref, self.base = ref, base

    def __getitem__(self, i):
        return self.ref[self.base + i]

    def __setitem__(self, i, value):
        self.ref[self.base + i] = value


def lists_kernel(
    caps, lists, owner, sections, plan, made,
    row_left, inner_left, start, count, col_right,
):
    cap_y, cap_left, cap_pair, cap_x, jobs = caps
    part = {name: Part(made, base) for name, base in places(caps)[0].items()}
    keep_left, here, there, keep = part["left"], part["here"], part["there"], part["keep"]
    job_left, job_right = part["job_left"], part["job_right"]
    job_last, job_col = part["job_last"], part["job_col"]
    out_of, slot_of = part["out"], part["slot"]
    row_from, panel_from = Part(plan, ROW_FROM), Part(plan, PANEL_FROM)
    r, c = lax.axis_index("row"), lax.axis_index("col")
    x = r >> 2
    y, zl = c >> 1, c & 1
    secs = [sections[0], sections[1]]
    for m in range(cap_pair):
        here[m] = 0
        there[m] = 0
    for m in range(cap_x):
        keep[m] = 0

    def clear(m, _):
        for u in range(8):
            keep_left[m * 8 + u] = 0
        return 0

    lax.fori_loop(0, cap_left // 8, clear, 0)

    def left(g, n):
        j = row_from[g]
        line = g * COLS + (j >> 1)
        base = (j & 1) * BLOCK_COLS
        p = owner[g * ROWS + j] - r * ROWS
        for s in range(SECTIONS):
            for k in range(KB):
                rel = lists[line, base + (secs[s] >> 1) * KB + k] - secs[s] * ROWS
                keep_left[n] = g * ENTRIES + s * KB + k
                row_left[n] = p
                inner_left[n] = s * ROWS + rel
                n = n + ((rel >= 0) & (rel < ROWS)).astype(jnp.int32)
        return n

    left_count = lax.fori_loop(0, ROWS, left, jnp.int32(0))

    def ordered(g):
        a, b = panel_from[g], panel_from[ROWS + g]
        swap = (b < a).astype(jnp.int32)
        return ((swap, jnp.minimum(a, b)), (1 - swap, jnp.maximum(a, b)))

    n_here, n_there, used, before = jnp.int32(0), jnp.int32(0), jnp.int32(0), jnp.int32(-1)
    for s, j in ordered(r):
        source = j >> 1
        used = jnp.where(source == before, used, 0)
        before = source
        line = r * COLS + source
        base = (j & 1) * BLOCK_COLS
        near = (source & 1) == zl
        for z in range(2):
            mine = zl == z
            for k in range(KB):
                b = y * 2 + z
                rel = lists[line, base + b * KB + k] - b * BLOCK_COLS
                ok = (rel >= 0) & (rel < SLAB)
                at = jnp.minimum((source >> 1) * cap_y + used, 4 * cap_y - 1)
                here[n_here] = at
                there[n_there] = at
                n_here = n_here + (ok & near & mine).astype(jnp.int32)
                n_there = n_there + (ok & near & jnp.logical_not(mine)).astype(jnp.int32)
                used = used + ok.astype(jnp.int32)

    def per_x(xs, _):
        def per_zh(zs, n):
            def per_core(k2, carry):
                n, seen0, seen1 = carry, jnp.int32(0), jnp.int32(0)
                g = xs * 4 + zs * 2 + k2
                for s, j in ordered(g):
                    source = j >> 1
                    sec = jnp.where(s == 0, secs[0], secs[1])
                    q = s * ROWS + owner[g * ROWS + j] - sec * ROWS
                    line = g * COLS + source
                    base = (j & 1) * BLOCK_COLS + c * KB
                    odd = source & 1
                    first = n
                    for k in range(KB):
                        rel = lists[line, base + k] - c * BLOCK_COLS
                        take = ((rel >= 0) & (rel < SLAB)).astype(jnp.int32)
                        seen = jnp.where(odd == 0, seen0, seen1)
                        at = ((zs * 2 + odd) * 2 + k2) * cap_pair
                        at = jnp.minimum(at + seen, 8 * cap_pair - 1)
                        col_right[xs * (cap_x + 1) + n] = rel
                        keep[jnp.where(xs == x, n, cap_x)] = at
                        n = n + take
                        seen0 = seen0 + take * (1 - odd)
                        seen1 = seen1 + take * odd
                    start[q] = xs * (cap_x + 1) + first
                    count[q] = n - first
                return n

            return lax.fori_loop(0, 2, per_core, n)

        lax.fori_loop(0, 2, per_zh, jnp.int32(0))
        return 0

    lax.fori_loop(0, 4, per_x, 0)

    def no_slot(o, _):
        for u in range(16):
            slot_of[o * 16 + u] = -1
        return 0

    lax.fori_loop(0, OUT_TILES // 16, no_slot, 0)

    def no_job(n, _):
        for u in range(8):
            job_left[n * 8 + u] = 0
            job_right[n * 8 + u] = 0
            job_last[n * 8 + u] = -1
            job_col[n * 8 + u] = UNUSED
        return 0

    lax.fori_loop(0, jobs // 8, no_job, 0)

    def per_left(m, carry):
        first = row_left[m] * SLAB
        q = inner_left[m]
        begin = start[q]

        def per_right(t, carry):
            n, touched = carry
            at = begin + t
            col = col_right[at]
            o = first + col
            last = slot_of[o]
            fresh = last < 0
            job_left[n] = m
            job_right[n] = at - at // (cap_x + 1)
            job_last[n] = last
            job_col[n] = col
            job_col[jnp.where(fresh, jobs + 1, last)] = UNUSED
            slot_of[o] = n
            out_of[jnp.where(fresh, touched, OUT_TILES - 1)] = jnp.where(
                fresh, o, out_of[OUT_TILES - 1]
            )
            return n + 1, touched + fresh.astype(jnp.int32)

        return lax.fori_loop(0, count[q], per_right, carry)

    _, touched = lax.fori_loop(0, left_count, per_left, (jnp.int32(0), jnp.int32(0)))
    part["touched"][0] = touched


def make_lists(caps, lists, owner, sections, plan):
    cap_y, cap_left, cap_pair, cap_x, jobs = caps
    smem = lambda n: pltpu.SMEM((n,), jnp.int32)
    return pl.pallas_call(
        functools.partial(lists_kernel, caps),
        out_shape=jax.ShapeDtypeStruct((places(caps)[1],), jnp.int32),
        in_specs=[SMEM] * 4,
        out_specs=SMEM,
        scratch_shapes=[
            smem(cap_left + 8), smem(cap_left + 8), smem(PANEL), smem(PANEL), smem(4 * (cap_x + 1)),
        ],
        compiler_params=params(4),
    )(lists, owner, sections, plan)


UNROLL = 8


def gather_part(caps, keep_left, here, there, keep, strips, cand, left, right, held, other, send, recv):
    cap_y, cap_left, cap_pair, cap_x, jobs = caps
    r, c = lax.axis_index("row"), lax.axis_index("col")
    k = r % 2
    x = r // 4
    me = ((r // 2) % 2) * 2 + c % 2
    cz = c + 1 - 2 * (c % 2)
    rz = (r // 4) * 4 + (r + 2) % 4
    zp, zh, zx = {"col": cz}, {"row": rz}, {"row": rz, "col": cz}
    yn, yb = {"col": (c + 2) % COLS}, {"col": (c + COLS - 2) % COLS}
    core = {"row": r + 1 - 2 * k}
    xn, xb = {"row": (r + 4) % ROWS}, {"row": (r + ROWS - 4) % ROWS}
    part = cap_x // 2
    end = cap_left
    mid = end // 2
    c_m, c_p = (c + COLS - 2) % COLS, (c + 2) % COLS
    z_m, z_p = (cz + COLS - 2) % COLS, (cz + 2) % COLS
    x_m, x_p, x_o = (x + 3) % 4, (x + 1) % 4, (x + 2) % 4
    z_of_p, z_of_h = (me // 2) * 2 + (me + 1) % 2, (me + 2) % 4
    z_of_x = (z_of_p + 2) % 4
    started, done = [], []

    def push(src, dst, to):
        n = len(started)
        copy = pltpu.make_async_remote_copy(
            src, dst, send.at[n], recv.at[n], device_id=to, device_id_type=MESH
        )
        copy.start()
        started.append(copy)
        return copy

    def go(origin, a, b, to):
        piece = left.at[origin, pl.ds(a, b - a)]
        return push(piece, piece, to)

    def gz(origin, to):
        piece = held.at[origin, k]
        return push(piece, piece, to)

    def gx(origin, a, b, to):
        piece = right.at[origin, k, pl.ds(a, b - a)]
        return push(piece, piece, to)

    def arrived(*copies):
        for copy in copies:
            copy.wait_recv()
            done.append(copy)

    for m in range(cap_pair):
        e = there[m]
        other[m] = cand[e // cap_y, e % cap_y]
        e = here[m]
        held[me, k, m] = cand[e // cap_y, e % cap_y]
    s1 = push(other, held.at[me, k], zp)
    s2 = push(other, held.at[me, k], zx)
    s3 = gz(me, zh)
    t0 = gz(me, core)
    yield started

    def pack_left(m, _):
        for u in range(4):
            e = keep_left[m * 4 + u]
            left[c, m * 4 + u] = strips[e // ENTRIES, e % ENTRIES]
        return 0

    lax.fori_loop(0, cap_left // 4, pack_left, 0)
    k1 = go(c, 0, end, zp)
    k2 = go(c, 0, end, yn)
    k3 = go(c, 0, end, yb)
    yield started
    arrived(s1)
    t1 = gz(z_of_p, core)
    arrived(s2)
    t2 = gz(z_of_x, core)
    arrived(s3)
    t3 = gz(z_of_h, core)
    arrived(t0, t1, t2, t3)
    for m in range(cap_x):
        e = keep[m]
        right[x, m // part, m % part] = held[e // (2 * cap_pair), (e // cap_pair) % 2, e % cap_pair]
    u1 = gx(x, 0, part, xn)
    u2 = gx(x, 0, part, xb)
    arrived(k1)
    k4 = go(cz, 0, end, yn)
    k5 = go(cz, 0, end, yb)
    arrived(k2)
    k6 = go(c_m, 0, mid, yn)
    arrived(k3)
    k7 = go(c_p, mid, end, yb)
    arrived(u1)
    u3 = gx(x_m, 0, part // 2, xn)
    u4 = gx(x_m, 0, part, core)
    arrived(u2)
    u5 = gx(x_p, part // 2, part, xb)
    u6 = gx(x_p, 0, part, core)
    arrived(k4)
    k8 = go(z_m, 0, mid, yn)
    arrived(k5)
    k9 = go(z_p, mid, end, yb)
    arrived(u3)
    u7 = gx(x_o, 0, part // 2, core)
    arrived(u5)
    u8 = gx(x_o, part // 2, part, core)
    for copy in started:
        if not any(copy is seen for seen in done):
            copy.wait_recv()
    yield started


def product_part(
    caps, job_left, job_right, job_last, job_col, left, right, sums, totals, rows, parts,
    total_send, total_recv,
):
    cap_y, cap_left, cap_pair, cap_x, jobs = caps
    r = lax.axis_index("row")
    part = cap_x // 2
    rows[...] = jnp.zeros_like(rows)
    line = lax.broadcasted_iota(jnp.int32, (ROWS, TILE), 0)

    def multiply(g, _):
        results = []
        for u in range(UNROLL):
            n = g * UNROLL + u
            a = left[:, job_left[n]].reshape(TILE, TILE)
            e = job_right[n]
            b = right[e // cap_x, (e // part) % 2, e % part]
            results.append(jnp.dot(a, b, preferred_element_type=jnp.float32))
        added = jnp.zeros((ROWS, TILE), jnp.float32)
        for u in range(UNROLL):
            n = g * UNROLL + u
            last = job_last[n]
            old = sums[jnp.maximum(last, 0)]
            value = results[u] + jnp.where(last >= 0, old, 0.0)
            sums[n] = value
            square = (value * value).reshape(TILE // 8, 8, TILE).sum(axis=0)
            square = square.sum(axis=0, keepdims=True)
            added = added + jnp.where(line == job_col[n], square, 0.0)
        rows[...] += added
        return 0

    lax.fori_loop(0, jobs // UNROLL, multiply, 0)
    parts[r] = rows[...]
    copies = []
    for d in range(1, ROWS):
        copy = pltpu.make_async_remote_copy(
            rows, parts.at[r], total_send.at[d], total_recv.at[d],
            device_id={"row": (r + d) % ROWS}, device_id_type=MESH,
        )
        copy.start()
        copies.append(copy)
    for copy in copies:
        copy.wait_recv()
    totals[...] = parts[...].sum(axis=0)
    return copies


def multiply_kernel(
    caps, strips, cand, plan, sums, totals,
    left, right, held, other, rows, parts, send, recv, total_send, total_recv,
):
    greet(lax.axis_index("row"), lax.axis_index("col"))
    found = {name: Part(plan, base) for name, base in places(caps)[0].items()}
    meet()
    steps = gather_part(
        caps, found["left"], found["here"], found["there"], found["keep"],
        strips, cand, left, right, held, other, send, recv,
    )
    for _ in range(2):
        next(steps)
    started = next(steps)
    started += product_part(
        caps, found["job_left"], found["job_right"], found["job_last"], found["job_col"],
        left, right, sums, totals, rows, parts, total_send, total_recv,
    )
    for copy in started:
        copy.wait_send()


COPIES = 24


def multiply_scratch(caps):
    cap_y, cap_left, cap_pair, cap_x, jobs = caps
    bf, f32 = jnp.bfloat16, jnp.float32
    dma = pltpu.SemaphoreType.DMA
    return (
        [
            pltpu.VMEM((COLS, cap_left, STRIP, TILE), bf),
            pltpu.VMEM((4, 2, cap_x // 2, TILE, TILE), bf),
            pltpu.VMEM((4, 2, cap_pair, TILE, TILE), bf),
            pltpu.VMEM((cap_pair, TILE, TILE), bf),
            pltpu.VMEM((ROWS, TILE), f32),
            pltpu.VMEM((ROWS, ROWS, TILE), f32),
        ]
        + [dma((COPIES,))] * 2
        + [dma((ROWS,))] * 2
    )


def multiply(caps, collective_id, strips, cand, plan):
    jobs, f32 = caps[4], jnp.float32
    mib = 24 + jobs * TILE * TILE * 4 // (1 << 20)
    return pl.pallas_call(
        functools.partial(multiply_kernel, caps),
        out_shape=(
            jax.ShapeDtypeStruct((jobs, TILE, TILE), f32),
            jax.ShapeDtypeStruct((ROWS, TILE), f32),
        ),
        in_specs=[VMEM, VMEM, SMEM],
        out_specs=(VMEM, VMEM),
        scratch_shapes=multiply_scratch(caps),
        compiler_params=params(mib, collective_id=collective_id, has_side_effects=True),
    )(strips, cand, plan)


def vector_prep(cap_y, owner, idx, sections, r, c):
    i32 = jnp.int32
    line = lax.broadcasted_iota(i32, (ROWS, TILE), 0)
    lane = lax.broadcasted_iota(i32, (ROWS, TILE), 1)
    blocks = [jnp.broadcast_to(owner[h : h + 1, :] >> 4, (ROWS, TILE)) for h in range(2)]
    who = jnp.zeros((ROWS, 1), i32)
    own = [jnp.zeros((ROWS, 1), i32) for _ in range(2)]
    for h in range(2):
        t = lane + h * TILE
        hit = (blocks[h] == line) & ((t >> 4) == r)
        who = who + jnp.where(hit, lane & (ROWS - 1), 0).sum(axis=1, keepdims=True)
        for i in range(2):
            hit = t == r * ROWS + c * 2 + i
            own[i] = own[i] + jnp.where(hit, blocks[h], 0).sum(axis=1, keepdims=True)
    sec0, sec1 = sections[0], sections[1]
    mine = jnp.where(lane < BLOCK_COLS, own[0], own[1])
    b = (lane & (BLOCK_COLS - 1)) >> 2
    rel = jnp.broadcast_to(idx[...], (ROWS, TILE)) - b * BLOCK_COLS
    ok = (lane < 2 * BLOCK_COLS) & (rel >= 0) & (rel < SLAB) & ((mine == sec0) | (mine == sec1))
    ok = ok & ((b >> 1) == line)
    rank = mm(picked(ok), picked(iota(0) < iota(1))).astype(i32)
    rank = jnp.where(ok, rank, -1)
    plan = jnp.where(lane == TILE - 1, jnp.clip(who, 0, ROWS - 1), 0)
    for m in range(cap_y):
        at = jnp.where(rank == m, lane, 0).sum(axis=1, keepdims=True)
        at = jnp.clip(at, 0, 2 * BLOCK_COLS - 1)
        plan = jnp.where(lane == m, at, plan)
    return plan


class Row:
    def __init__(self, ref, row):
        self.ref, self.row = ref, row

    def __getitem__(self, i):
        return self.ref[self.row, i]


def whole_kernel(
    caps, values, idx, owner, sections,
    sums, totals, made, over,
    tv, strips, cand, lists, early, places_of, scalars, value_sem, plan_sem, *scratch,
):
    r, c = lax.axis_index("row"), lax.axis_index("col")
    greet(r, c)
    load = pltpu.make_async_copy(values, tv, value_sem)
    load.start()
    early[...] = vector_prep(caps[0], owner, idx, sections, r, c)
    move = pltpu.make_async_copy(early, places_of, plan_sem)
    move.start()
    move.wait()
    load.wait()
    first, second = scratch[:14], scratch[14:]
    left, right, held, other, rows, parts, send, recv, total_send, total_recv = second
    row = lambda n: Row(scalars, n)
    steps = gather_part(
        caps, row(ROW_LEFT), row(ROW_HERE), row(ROW_THERE), row(ROW_KEEP),
        strips, cand, left, right, held, other, send, recv,
    )

    def on_lists():
        found, excess = vector_plan(caps, lists, owner, sections, r, c)
        made[...] = found
        over[...] = excess
        move = pltpu.make_async_copy(made, scalars, plan_sem)
        move.start()
        move.wait()

    started = spread_part(
        caps[0], tv, idx, sections,
        lambda yd, m: places_of[yd, m], lambda t: places_of[t, TILE - 1],
        strips, cand, lists, *first,
        meet, on_lists, *[lambda: next(steps)] * 2,
    )
    started = started + next(steps)
    started += product_part(
        caps, row(ROW_JOB), row(ROW_TILE), row(ROW_LAST), row(ROW_COL),
        left, right, sums, totals, rows, parts, total_send, total_recv,
    )
    for copy in started:
        copy.wait_send()


def whole(caps, collective_id, tv, idx, owner, sections):
    bf, f32, i32 = jnp.bfloat16, jnp.float32, jnp.int32
    dma = pltpu.SemaphoreType.DMA
    return pl.pallas_call(
        functools.partial(whole_kernel, caps),
        out_shape=(
            jax.ShapeDtypeStruct((caps[4], TILE, TILE), f32),
            jax.ShapeDtypeStruct((ROWS, TILE), f32),
            jax.ShapeDtypeStruct((ROWS, TILE), i32),
            jax.ShapeDtypeStruct((TILE, TILE), f32),
        ),
        in_specs=[HBM, VMEM, VMEM, SMEM],
        out_specs=(VMEM,) * 4,
        scratch_shapes=[
            pltpu.VMEM((2 * COLS * KB, TILE, TILE), bf),
            pltpu.VMEM((ROWS, ENTRIES, STRIP, TILE), bf),
            pltpu.VMEM((4, caps[0], TILE, TILE), bf),
            pltpu.VMEM((ROWS, COLS, 1, TILE), i32),
            pltpu.VMEM((ROWS, TILE), i32),
            pltpu.SMEM((ROWS, TILE), i32),
            pltpu.SMEM((ROWS, TILE), i32),
            dma,
            dma,
        ]
        + spread_scratch(caps[0])
        + multiply_scratch(caps),
        compiler_params=params(24, collective_id=collective_id, has_side_effects=True),
    )(tv, idx, owner, sections)


def write_listed_kernel(jobs, sums, plan, totals, out, block, factor, zeros, zero_sem, out_sem):
    zeros[...] = jnp.zeros_like(zeros)
    clears = [
        pltpu.make_async_copy(zeros, out.at[pl.ds(p * TILE, TILE)], zero_sem.at[p])
        for p in range(ROWS)
    ]
    for copy in clears:
        copy.start()
    count = float(ROWS * ROWS * TILE)
    factor[...] = count / (totals[...] + 1e-06)

    def scale(n, _):
        o = plan[ROW_OUT, n]

        @pl.when(o >= 0)
        def _():
            value = sums[n]
            col = o - o // SLAB * SLAB
            block[n] = (value * value * factor[pl.ds(col, 1), :]).astype(jnp.bfloat16)

        return 0

    lax.fori_loop(0, jobs, scale, 0)
    for copy in clears:
        copy.wait()

    def place(n, o):
        p = o // SLAB
        col = o - p * SLAB
        row = pl.ds(pl.multiple_of(p * TILE, TILE), TILE)
        lanes = pl.ds(pl.multiple_of(col * TILE, TILE), TILE)
        return pltpu.make_async_copy(block.at[n], out.at[row, lanes], out_sem)

    def send(n, _):
        o = plan[ROW_OUT, n]

        @pl.when(o >= 0)
        def _():
            place(n, o).start()

        return 0

    lax.fori_loop(0, jobs, send, 0)

    def drain(n, _):
        o = plan[ROW_OUT, n]

        @pl.when(o >= 0)
        def _():
            place(n, o).wait()

        return 0

    lax.fori_loop(0, jobs, drain, 0)


def write_listed(jobs, sums, plan, totals):
    return pl.pallas_call(
        functools.partial(write_listed_kernel, jobs),
        out_shape=jax.ShapeDtypeStruct((ROWS * TILE, SLAB * TILE), jnp.bfloat16),
        in_specs=[VMEM, SMEM, VMEM],
        out_specs=ANY,
        scratch_shapes=[
            pltpu.VMEM((jobs, TILE, TILE), jnp.bfloat16),
            pltpu.VMEM((ROWS, TILE), jnp.float32),
            pltpu.VMEM((TILE, SLAB * TILE), jnp.bfloat16),
            pltpu.SemaphoreType.DMA((ROWS,)),
            pltpu.SemaphoreType.DMA,
        ],
        compiler_params=params(12),
    )(sums, plan, totals)


def write_kernel(at, sums, blank, plan, totals, out, block, factor, out_sem):
    touched = plan[at["touched"]]
    count = float(ROWS * ROWS * TILE)
    factor[...] = count / (totals[...] + 1e-06)

    def place(i):
        o = plan[at["out"] + i]
        p = o // SLAB
        col = o - p * SLAB
        row = pl.ds(pl.multiple_of(p * TILE, TILE), TILE)
        lanes = pl.ds(pl.multiple_of(col * TILE, TILE), TILE)
        return o, col, pltpu.make_async_copy(block.at[i], out.at[row, lanes], out_sem)

    def scale(i, _):
        o, col, copy = place(i)
        value = sums[plan[at["slot"] + o]]
        block[i] = (value * value * factor[pl.ds(col, 1), :]).astype(jnp.bfloat16)
        copy.start()
        return 0

    lax.fori_loop(0, touched, scale, 0)

    def drain(i, _):
        place(i)[2].wait()
        return 0

    lax.fori_loop(0, touched, drain, 0)


def write(caps, sums, blank, plan, totals):
    jobs = caps[4]
    mib = 10 + jobs * TILE * TILE * 4 // (1 << 20)
    return pl.pallas_call(
        functools.partial(write_kernel, places(caps)[0]),
        out_shape=jax.ShapeDtypeStruct((ROWS * TILE, SLAB * TILE), jnp.bfloat16),
        in_specs=[VMEM, ANY, SMEM, VMEM],
        out_specs=ANY,
        input_output_aliases={1: 0},
        scratch_shapes=[
            pltpu.VMEM((OUT_TILES, TILE, TILE), jnp.bfloat16),
            pltpu.VMEM((ROWS, TILE), jnp.float32),
            pltpu.SemaphoreType.DMA,
        ],
        compiler_params=params(mib),
    )(sums, blank, plan, totals)


def per_device(tile_values, tile_columns, owner_map, section_rows):
    flat = tile_columns.reshape(-1)
    idx = jnp.pad(flat, (0, TILE - flat.shape[0])).reshape(1, TILE)
    tv = tile_values.reshape(2 * COLS * KB, TILE, TILE)
    owner_rows = owner_map.reshape(2, TILE)

    sums, totals, made, over = whole(FAST, 0, tv, idx, owner_rows, section_rows)

    out = write_listed(FAST[4], sums, made, totals)

    def full(state):
        plan, blank = prep(FULL[0], owner_map, section_rows, flat)
        strips, cand, lists = spread(FULL[0], 2, tv, idx, section_rows, plan)
        made = make_lists(FULL, lists.reshape(ROWS * COLS, TILE), owner_map, section_rows, plan)
        sums, totals = multiply(FULL, 3, strips, cand, made)
        return jnp.float32(0), write(FULL, sums, blank, made, totals)

    return lax.while_loop(lambda state: state[0] > 0, full, (jnp.max(over), out))[1]


def solution(mesh):
    both = ("row", "col")
    in_specs = (P(both, None, None, None, None), P(both, None, None), P(), P())
    return jax.shard_map(
        per_device, mesh=mesh, in_specs=in_specs, out_specs=P("row", "col"), check_vma=False
    )
```

```python
import functools

import jax
import jax.numpy as jnp
from jax import lax
from jax.experimental import pallas as pl
from jax.experimental.pallas import tpu as pltpu
from jax.sharding import PartitionSpec as P

TILE = 128
KB = 4
SLAB = 12
SECTIONS = 2
ROWS = 16
COLS = 8
BLOCK_COLS = 32
STRIP = TILE // COLS
ENTRIES = SECTIONS * KB
PANEL = SECTIONS * ROWS
FAST = (9, 60, 7, 16, 96)
FULL = (16, 128, 8, 32, 512)
MESH = pl.DeviceIdType.MESH
VMEM = pl.BlockSpec(memory_space=pltpu.VMEM)
SMEM = pl.BlockSpec(memory_space=pltpu.SMEM)
ANY = pl.BlockSpec(memory_space=pl.ANY)
HBM = pl.BlockSpec(memory_space=pltpu.HBM)


def params(mib, **kw):
    return pltpu.CompilerParams(vmem_limit_bytes=mib << 20, **kw)


SEND, ROW_FROM, PANEL_FROM, PICKS = 0, ROWS, 2 * ROWS, 4 * ROWS


def prep_kernel(cap, owner, sections, cols, plan, blank, inverse, zeros, zero_sem):
    r, c = lax.axis_index("row"), lax.axis_index("col")
    zeros[...] = jnp.zeros_like(zeros)
    clears = [
        pltpu.make_async_copy(zeros, blank.at[pl.ds(p * TILE, TILE)], zero_sem.at[p])
        for p in range(ROWS)
    ]
    for copy in clears:
        copy.start()

    def invert(g, _):
        for j in range(ROWS):
            inverse[owner[g * ROWS + j]] = g * ROWS + j
        return 0

    lax.fori_loop(0, ROWS, invert, 0)
    secs = [sections[0], sections[1]]
    for j in range(ROWS):
        plan[SEND + (owner[r * ROWS + j] >> 4)] = j
        t = inverse[r * ROWS + j]
        plan[ROW_FROM + (t >> 4)] = t & 15
        for s in range(SECTIONS):
            t = inverse[secs[s] * ROWS + j]
            plan[PANEL_FROM + s * ROWS + (t >> 4)] = t & 15
    wanted = []
    for i in range(2):
        block = owner[r * ROWS + c * 2 + i] >> 4
        wanted.append((block == secs[0]) | (block == secs[1]))
    room = cap + 1

    def per_y(yd, _):
        for m in range(room):
            plan[PICKS + yd * room + m] = 0
        count = jnp.int32(0)
        for i in range(2):
            for z in range(2):
                b = yd * 2 + z
                for k in range(KB):
                    rel = cols[i * BLOCK_COLS + b * KB + k] - b * BLOCK_COLS
                    take = wanted[i] & (rel >= 0) & (rel < SLAB)
                    plan[PICKS + yd * room + count] = i * BLOCK_COLS + b * KB + k
                    count = jnp.minimum(count + take.astype(jnp.int32), cap)
        return 0

    lax.fori_loop(0, 4, per_y, 0)
    for copy in clears:
        copy.wait()


def prep(cap, owner, sections, cols):
    return pl.pallas_call(
        functools.partial(prep_kernel, cap),
        out_shape=(
            jax.ShapeDtypeStruct((PICKS + 4 * (cap + 1),), jnp.int32),
            jax.ShapeDtypeStruct((ROWS * TILE, SLAB * TILE), jnp.bfloat16),
        ),
        in_specs=[SMEM] * 3,
        out_specs=(SMEM, ANY),
        scratch_shapes=[
            pltpu.SMEM((ROWS * ROWS,), jnp.int32),
            pltpu.VMEM((TILE, SLAB * TILE), jnp.bfloat16),
            pltpu.SemaphoreType.DMA((ROWS,)),
        ],
        compiler_params=params(4),
    )(owner, sections, cols)


def iota(dim):
    return lax.broadcasted_iota(jnp.int32, (TILE, TILE), dim)


def picked(mask):
    return jnp.where(mask, 1.0, 0.0).astype(jnp.bfloat16)


def mm(a, b, dims=((1,), (0,))):
    return lax.dot_general(a, b, (dims, ((), ())), preferred_element_type=jnp.float32)


ROW_LEFT, ROW_HERE, ROW_THERE, ROW_KEEP = 0, 1, 2, 3
ROW_JOB, ROW_TILE, ROW_LAST, ROW_COL, ROW_OUT = 4, 5, 6, 7, 8


def vector_plan(caps, lists, owner, sections, r, c):
    cap_y, cap_left, cap_pair, cap_x, most_jobs = caps
    f32, bf, i32 = jnp.float32, jnp.bfloat16, jnp.int32
    cols = lists[...].reshape(TILE, TILE)
    line, lane = iota(0), iota(1)
    before = picked(line < lane)
    after = picked(lane < line)
    ones = jnp.ones((TILE, TILE), bf)
    same = picked(line == lane)
    nn, tn, nt = ((1,), (0,)), ((0,), (0,)), ((1,), (1,))
    small = lambda v: v.astype(f32).astype(bf)
    whole = lambda v: v.astype(i32)
    places_, blocks = [], []
    for i in range(2):
        total = jnp.zeros((TILE, TILE), f32)
        for h in range(2):
            row = jnp.broadcast_to(owner[h : h + 1, :].astype(f32), (TILE, TILE))
            total = total + mm(picked(lane + h * TILE == 2 * line + i), row.astype(bf), nt)
        places_.append(whole(total))
        blocks.append(places_[i] >> 4)
    mine = jnp.where(lane < BLOCK_COLS, blocks[0], blocks[1])
    sec0, sec1 = sections[0], sections[1]
    real = lane < 2 * BLOCK_COLS
    b = (lane & (BLOCK_COLS - 1)) >> 2
    rel = cols - b * BLOCK_COLS
    slab_mask = real & (rel >= 0) & (rel < SLAB) & ((mine == sec0) | (mine == sec1))
    slab = picked(slab_mask)
    shifted = small(jnp.where(real, cols + 1, 0))
    lane_b = (line & (BLOCK_COLS - 1)) >> 2
    row_real = line < 2 * BLOCK_COLS

    per_y = mm(slab, picked(row_real & ((lane_b >> 1) == lane)))
    per_b = small(mm(slab, picked(row_real & (lane_b == lane))))
    per_pair = mm(picked(((line >> 3) == (lane >> 3)) & ((line & 1) == (lane & 1))), per_b)
    per_x = mm(picked((line >> 5) == (lane >> 5)), per_b)
    section = lane >> 4
    target = jnp.where(section == 0, sec0, sec1) * ROWS + (lane & (ROWS - 1))
    target = jnp.where(section < SECTIONS, target, 2 * TILE + 1)
    source = jnp.where((lane >> 2) % SECTIONS == 0, sec0, sec1) >> 1
    chosen, panel_tiles = [], jnp.zeros((TILE, TILE), f32)
    for i in range(2):
        wanted = i * BLOCK_COLS + source * KB + lane % KB
        chosen.append(mm(shifted, picked((lane < ENTRIES) & (line == wanted))))
        own = (line >= i * BLOCK_COLS) & (line < (i + 1) * BLOCK_COLS)
        mine_b = small(mm(slab, picked(own & (lane_b == lane))))
        panel_tiles = panel_tiles + mm(picked(places_[i] == target), mine_b, tn)
    panel_tiles = small(panel_tiles)
    rows = jnp.zeros((TILE, TILE), f32)
    jobs = jnp.zeros((TILE, TILE), f32)
    for i in range(2):
        hits = jnp.zeros((TILE, TILE), f32)
        for e in range(ENTRIES):
            at = whole(chosen[i][:, e : e + 1]) - 1
            hits = hits + jnp.where((at == target) & (section == e // KB), 1.0, 0.0)
        hits = small(hits)
        block = picked(blocks[i] == lane)
        rows = rows + mm(block, small(mm(hits, ones)), tn)
        jobs = jobs + mm(block, small(mm(hits, panel_tiles)), tn)
    over = jnp.maximum(per_y - cap_y, rows - cap_left)
    over = jnp.maximum(over, jnp.maximum(per_pair - cap_pair, per_x - cap_x))
    over = jnp.maximum(over, jobs - most_jobs)

    got = jnp.zeros((TILE, TILE), f32)
    place = jnp.zeros((TILE, TILE), f32)
    for i in range(2):
        group = picked(((line >> 3) == lane) & (blocks[i] == r))
        got = got + mm(group, small(chosen[i]), tn)
        place = place + mm(group, small(places_[i]), tn)
    line16 = lax.broadcasted_iota(i32, (ROWS, TILE), 0)
    lane16 = lax.broadcasted_iota(i32, (ROWS, TILE), 1)
    got, place = whole(got[:ROWS]) - 1, whole(place[:ROWS]) - r * ROWS
    inner = got - jnp.where(lane16 < KB, sec0, sec1) * ROWS
    ok = (lane16 < ENTRIES) & (inner >= 0) & (inner < ROWS)
    inner = inner + (lane16 >> 2) * ROWS
    flags = picked(ok)
    spare = jnp.zeros((TILE - ROWS, TILE), bf)
    padded = jnp.concatenate([flags, spare], axis=0)
    rank = mm(padded, before) + mm(after, small(mm(padded, ones)))
    rank = jnp.where(ok, whole(rank[:ROWS]), -1)
    zero16 = jnp.zeros((ROWS, TILE), i32)
    code, left_p, left_q = zero16, zero16, zero16
    for e in range(ENTRIES):
        hit = rank[:, e : e + 1] == lane16
        code = code + jnp.where(hit, line16 * ENTRIES + e, 0)
        left_p = left_p + jnp.where(hit, place[:, e : e + 1], 0)
        left_q = left_q + jnp.where(hit, inner[:, e : e + 1] + 1, 0)
    code = code.sum(axis=0, keepdims=True)
    left_p = left_p.sum(axis=0, keepdims=True)
    left_q = left_q.sum(axis=0, keepdims=True)

    def lanes_of(column):
        wanted = (lane >> 2) * BLOCK_COLS + column * KB + lane % KB
        return picked((lane < 2 * KB) & (line == wanted))

    x, y, zl = r // 4, c // 2, c % 2
    to_here, to_there = lanes_of(c), lanes_of(c + 1 - 2 * zl)
    of_y = slab_mask & ((b >> 1) == y)
    used = small(mm(picked(of_y), before))
    spot = ((line & 7) >> 1) * cap_y
    eligible = ((line >> 3) == r) & ((line & 1) == zl)

    def packed_row(key, values):
        sums = [jnp.zeros((TILE, TILE), i32) for _ in values]
        for u in range(2 * KB):
            hit = key[:, u : u + 1] == lane
            for n, value in enumerate(values):
                sums[n] = sums[n] + jnp.where(hit, value(u), 0)
        return [v.sum(axis=0, keepdims=True) for v in sums]

    def from_y(choose):
        flag = (mm(slab, choose) > 0.5) & eligible
        number = picked(flag)
        order = whole(mm(number, before) + mm(after, small(mm(number, ones))))
        at = spot + whole(mm(used, choose))
        key = jnp.where(flag, order, -1)
        return packed_row(key, [lambda u: at[:, u : u + 1]])[0]

    here, there = from_y(to_here), from_y(to_there)

    flag = mm(slab, to_here) > 0.5
    number = picked(flag)
    ahead = mm(number, before)
    rest = small(mm(number, ones))
    in_x = whole(ahead + mm(picked((lane < line) & ((line >> 5) == (lane >> 5))), rest))
    same_pair = (lane < line) & ((line >> 3) == (lane >> 3)) & ((line & 1) == (lane & 1))
    in_pair = whole(ahead + mm(picked(same_pair), rest))
    at = ((((line >> 4) & 1) * 2 + (line & 1)) * 2 + ((line >> 3) & 1)) * cap_pair + in_pair
    key = jnp.where(flag & ((line >> 5) == x), in_x, -1)
    keep = packed_row(key, [lambda u: at[:, u : u + 1]])[0]
    key = jnp.where(flag, (line >> 5) * cap_x + in_x, -1)
    grid_col = whole(mm(shifted, to_here)) - 1 - c * BLOCK_COLS
    panel_of = []
    for i in range(2):
        q = jnp.where(blocks[i] == sec0, places_[i] - sec0 * ROWS, places_[i] - sec1 * ROWS + ROWS)
        panel_of.append(q + 1)
    right_q, right_col = packed_row(
        key, [lambda u: panel_of[u // KB], lambda u: grid_col[:, u : u + 1]]
    )

    wide = lambda row: jnp.broadcast_to(row, (TILE, TILE))
    left_q_down = whole(mm(same, small(wide(left_q)), nt))
    pair = picked((left_q_down == wide(right_q)) & (left_q_down > 0))
    number = small(mm(pair, ones))
    begin_row = whole(mm(number, before, tn))
    number_row = whole(mm(number, same, tn))
    job_of = picked((line >= begin_row) & (line < begin_row + number_row))
    begin = mm(job_of, small(mm(after, number)))
    turn = mm(job_of, small(mm(pair, before)))
    choice = (mm(job_of, pair) > 0.5) & (whole(turn) == line - whole(begin))
    choice = picked(choice)
    line8 = lax.broadcasted_iota(i32, (ROWS, TILE), 0)
    stack = jnp.where(line8 == 0, lane16, jnp.where(line8 == 1, jnp.broadcast_to(left_p, (ROWS, TILE)), 0))
    by_left = whole(mm(small(stack), job_of, nt))
    stack = jnp.where(line8 == 0, lane16, jnp.where(line8 == 1, jnp.broadcast_to(right_col, (ROWS, TILE)), 1))
    by_right = whole(mm(small(stack), choice, nt))
    job_left, job_p = by_left[0:1], by_left[1:2]
    job_tile, job_col, valid = by_right[0:1], by_right[1:2], by_right[2:3] > 0
    out = jnp.where(valid, job_p * SLAB + job_col, 255)
    out_row = wide(out)
    out_down = whole(mm(same, small(out_row), nt))
    alike = out_down == out_row
    last = jnp.where(alike & (line < lane), line, -1).max(axis=0, keepdims=True)
    later = jnp.where(alike & (line > lane), 1, 0).max(axis=0, keepdims=True)
    final = valid & (later == 0)
    made = [
        jnp.clip(code, 0, ROWS * ENTRIES - 1),
        jnp.clip(here, 0, 4 * cap_y - 1),
        jnp.clip(there, 0, 4 * cap_y - 1),
        jnp.clip(keep, 0, 8 * cap_pair - 1),
        jnp.clip(job_left, 0, cap_left - 1),
        jnp.clip(job_tile, 0, 4 * cap_x - 1),
        jnp.where(valid, jnp.clip(last, -1, most_jobs - 1), -1),
        jnp.where(final, job_col, UNUSED),
        jnp.where(final, jnp.clip(out, 0, OUT_TILES - 1), -1),
    ]
    plan = jnp.zeros((ROWS, TILE), i32)
    for n, row in enumerate(made):
        plan = jnp.where(line16 == n, jnp.broadcast_to(row, (ROWS, TILE)), plan)
    return plan, over


def spread_part(
    cap, tv, idx, sections, pick, sender,
    strips, cand, lists,
    left_out, left_in, right_out, row_out,
    s_idx, r_idx, s_left, r_left, s_right, r_right, s_list, r_list, s_row, r_row,
    meet, on_lists, on_right, on_strips,
):
    r, c = lax.axis_index("row"), lax.axis_index("col")
    y, z = c // 2, c % 2
    for i in range(2):
        for s in range(SECTIONS):
            source = sections[s] // 2
            for k in range(KB):
                for h in range(COLS):
                    left_out[h, i * ENTRIES + s * KB + k] = tv[
                        i * BLOCK_COLS + source * KB + k, h * STRIP : (h + 1) * STRIP, :
                    ]

    def pack(yd, _):
        for m in range(cap):
            right_out[yd, m] = tv[pick(yd, m)]
        return 0

    lax.fori_loop(0, 4, pack, 0)
    lists[r, c] = idx[...]
    left_in[c] = left_out[c]
    cand[y] = right_out[y]
    meet()

    idx_copies, left_copies, right_copies = [], [], []
    for d in range(1, COLS):
        to = (c + d) % COLS
        copy = pltpu.make_async_remote_copy(
            idx, lists.at[r, c], s_idx.at[d], r_idx.at[d], device_id={"col": to}, device_id_type=MESH
        )
        copy.start()
        idx_copies.append(copy)
    for d in range(1, COLS):
        to = (c + d) % COLS
        copy = pltpu.make_async_remote_copy(
            left_out.at[to], left_in.at[c], s_left.at[d], r_left.at[d],
            device_id={"col": to}, device_id_type=MESH,
        )
        copy.start()
        left_copies.append(copy)
    for d in (2, 1, 3):
        to = (y + d) % 4
        copy = pltpu.make_async_remote_copy(
            right_out.at[to], cand.at[y], s_right.at[d], r_right.at[d],
            device_id={"col": to * 2 + z}, device_id_type=MESH,
        )
        copy.start()
        right_copies.append(copy)
    for copy in idx_copies:
        copy.wait_recv()
    list_copies = []
    for d in range(1, ROWS):
        to = (r + d) % ROWS
        copy = pltpu.make_async_remote_copy(
            lists.at[r], lists.at[r], s_list.at[d], r_list.at[d],
            device_id={"row": to}, device_id_type=MESH,
        )
        copy.start()
        list_copies.append(copy)
    for copy in left_copies:
        copy.wait_recv()

    def reorder(t, _):
        j = sender(t)
        for e in range(ENTRIES):
            row_out[t, e] = left_in[j // 2, (j % 2) * ENTRIES + e]
        return 0

    lax.fori_loop(0, ROWS, reorder, 0)
    strips[r] = row_out[r]
    row_copies = []
    for d in range(1, ROWS):
        to = (r + d) % ROWS
        copy = pltpu.make_async_remote_copy(
            row_out.at[to], strips.at[r], s_row.at[d], r_row.at[d],
            device_id={"row": to}, device_id_type=MESH,
        )
        copy.start()
        row_copies.append(copy)
    for copy in list_copies:
        copy.wait_recv()
    on_lists()
    for copy in right_copies:
        copy.wait_recv()
    on_right()
    for copy in row_copies:
        copy.wait_recv()
    on_strips()
    return idx_copies + left_copies + right_copies + list_copies + row_copies


def greet(r, c):
    barrier = pltpu.get_barrier_semaphore()
    for d in range(1, COLS):
        pl.semaphore_signal(barrier, inc=1, device_id={"col": (c + d) % COLS}, device_id_type=MESH)
    for d in range(1, ROWS):
        pl.semaphore_signal(barrier, inc=1, device_id={"row": (r + d) % ROWS}, device_id_type=MESH)
    across = {"row": (r // 4) * 4 + (r + 2) % 4, "col": c + 1 - 2 * (c % 2)}
    pl.semaphore_signal(barrier, inc=1, device_id=across, device_id_type=MESH)


def meet():
    pl.semaphore_wait(pltpu.get_barrier_semaphore(), COLS - 1 + ROWS - 1 + 1)


def spread_kernel(cap, values, idx, sections, plan, strips, cand, lists, tv, value_sem, *scratch):
    greet(lax.axis_index("row"), lax.axis_index("col"))
    load = pltpu.make_async_copy(values, tv, value_sem)
    load.start()
    load.wait()
    nothing = lambda: None
    pick = lambda yd, m: plan[PICKS + yd * (cap + 1) + m]
    sender = lambda t: plan[SEND + t]
    started = spread_part(
        cap, tv, idx, sections, pick, sender, strips, cand, lists, *scratch, meet, *[nothing] * 3
    )
    for copy in started:
        copy.wait_send()


def spread_scratch(cap):
    bf = jnp.bfloat16
    dma = pltpu.SemaphoreType.DMA
    return (
        [
            pltpu.VMEM((COLS, 2 * ENTRIES, STRIP, TILE), bf),
            pltpu.VMEM((COLS, 2 * ENTRIES, STRIP, TILE), bf),
            pltpu.VMEM((4, cap, TILE, TILE), bf),
            pltpu.VMEM((ROWS, ENTRIES, STRIP, TILE), bf),
        ]
        + [dma((COLS,))] * 6
        + [dma((ROWS,))] * 4
    )


def spread(cap, collective_id, tv, idx, sections, plan):
    bf = jnp.bfloat16
    return pl.pallas_call(
        functools.partial(spread_kernel, cap),
        out_shape=(
            jax.ShapeDtypeStruct((ROWS, ENTRIES, STRIP, TILE), bf),
            jax.ShapeDtypeStruct((4, cap, TILE, TILE), bf),
            jax.ShapeDtypeStruct((ROWS, COLS, 1, TILE), jnp.int32),
        ),
        in_specs=[HBM, VMEM, SMEM, SMEM],
        out_specs=(VMEM,) * 3,
        scratch_shapes=[pltpu.VMEM((2 * COLS * KB, TILE, TILE), bf), pltpu.SemaphoreType.DMA]
        + spread_scratch(cap),
        compiler_params=params(20, collective_id=collective_id, has_side_effects=True),
    )(tv, idx, sections, plan)


OUT_TILES = ROWS * SLAB
UNUSED = ROWS - 1


def places(caps):
    cap_y, cap_left, cap_pair, cap_x, jobs = caps
    sizes = (
        ("left", cap_left + 8), ("here", cap_pair + 8), ("there", cap_pair + 8), ("keep", cap_x + 8),
        ("job_left", jobs + 8), ("job_right", jobs + 8), ("job_last", jobs + 8), ("job_col", jobs + 8),
        ("out", OUT_TILES), ("slot", OUT_TILES), ("touched", 8),
    )
    at, found = 0, {}
    for name, size in sizes:
        found[name] = at
        at += size
    return found, at


class Part:
    def __init__(self, ref, base):
        self.ref, self.base = ref, base

    def __getitem__(self, i):
        return self.ref[self.base + i]

    def __setitem__(self, i, value):
        self.ref[self.base + i] = value


def lists_kernel(
    caps, lists, owner, sections, plan, made,
    row_left, inner_left, start, count, col_right,
):
    cap_y, cap_left, cap_pair, cap_x, jobs = caps
    part = {name: Part(made, base) for name, base in places(caps)[0].items()}
    keep_left, here, there, keep = part["left"], part["here"], part["there"], part["keep"]
    job_left, job_right = part["job_left"], part["job_right"]
    job_last, job_col = part["job_last"], part["job_col"]
    out_of, slot_of = part["out"], part["slot"]
    row_from, panel_from = Part(plan, ROW_FROM), Part(plan, PANEL_FROM)
    r, c = lax.axis_index("row"), lax.axis_index("col")
    x = r >> 2
    y, zl = c >> 1, c & 1
    secs = [sections[0], sections[1]]
    for m in range(cap_pair):
        here[m] = 0
        there[m] = 0
    for m in range(cap_x):
        keep[m] = 0

    def clear(m, _):
        for u in range(8):
            keep_left[m * 8 + u] = 0
        return 0

    lax.fori_loop(0, cap_left // 8, clear, 0)

    def left(g, n):
        j = row_from[g]
        line = g * COLS + (j >> 1)
        base = (j & 1) * BLOCK_COLS
        p = owner[g * ROWS + j] - r * ROWS
        for s in range(SECTIONS):
            for k in range(KB):
                rel = lists[line, base + (secs[s] >> 1) * KB + k] - secs[s] * ROWS
                keep_left[n] = g * ENTRIES + s * KB + k
                row_left[n] = p
                inner_left[n] = s * ROWS + rel
                n = n + ((rel >= 0) & (rel < ROWS)).astype(jnp.int32)
        return n

    left_count = lax.fori_loop(0, ROWS, left, jnp.int32(0))

    def ordered(g):
        a, b = panel_from[g], panel_from[ROWS + g]
        swap = (b < a).astype(jnp.int32)
        return ((swap, jnp.minimum(a, b)), (1 - swap, jnp.maximum(a, b)))

    n_here, n_there, used, before = jnp.int32(0), jnp.int32(0), jnp.int32(0), jnp.int32(-1)
    for s, j in ordered(r):
        source = j >> 1
        used = jnp.where(source == before, used, 0)
        before = source
        line = r * COLS + source
        base = (j & 1) * BLOCK_COLS
        near = (source & 1) == zl
        for z in range(2):
            mine = zl == z
            for k in range(KB):
                b = y * 2 + z
                rel = lists[line, base + b * KB + k] - b * BLOCK_COLS
                ok = (rel >= 0) & (rel < SLAB)
                at = jnp.minimum((source >> 1) * cap_y + used, 4 * cap_y - 1)
                here[n_here] = at
                there[n_there] = at
                n_here = n_here + (ok & near & mine).astype(jnp.int32)
                n_there = n_there + (ok & near & jnp.logical_not(mine)).astype(jnp.int32)
                used = used + ok.astype(jnp.int32)

    def per_x(xs, _):
        def per_zh(zs, n):
            def per_core(k2, carry):
                n, seen0, seen1 = carry, jnp.int32(0), jnp.int32(0)
                g = xs * 4 + zs * 2 + k2
                for s, j in ordered(g):
                    source = j >> 1
                    sec = jnp.where(s == 0, secs[0], secs[1])
                    q = s * ROWS + owner[g * ROWS + j] - sec * ROWS
                    line = g * COLS + source
                    base = (j & 1) * BLOCK_COLS + c * KB
                    odd = source & 1
                    first = n
                    for k in range(KB):
                        rel = lists[line, base + k] - c * BLOCK_COLS
                        take = ((rel >= 0) & (rel < SLAB)).astype(jnp.int32)
                        seen = jnp.where(odd == 0, seen0, seen1)
                        at = ((zs * 2 + odd) * 2 + k2) * cap_pair
                        at = jnp.minimum(at + seen, 8 * cap_pair - 1)
                        col_right[xs * (cap_x + 1) + n] = rel
                        keep[jnp.where(xs == x, n, cap_x)] = at
                        n = n + take
                        seen0 = seen0 + take * (1 - odd)
                        seen1 = seen1 + take * odd
                    start[q] = xs * (cap_x + 1) + first
                    count[q] = n - first
                return n

            return lax.fori_loop(0, 2, per_core, n)

        lax.fori_loop(0, 2, per_zh, jnp.int32(0))
        return 0

    lax.fori_loop(0, 4, per_x, 0)

    def no_slot(o, _):
        for u in range(16):
            slot_of[o * 16 + u] = -1
        return 0

    lax.fori_loop(0, OUT_TILES // 16, no_slot, 0)

    def no_job(n, _):
        for u in range(8):
            job_left[n * 8 + u] = 0
            job_right[n * 8 + u] = 0
            job_last[n * 8 + u] = -1
            job_col[n * 8 + u] = UNUSED
        return 0

    lax.fori_loop(0, jobs // 8, no_job, 0)

    def per_left(m, carry):
        first = row_left[m] * SLAB
        q = inner_left[m]
        begin = start[q]

        def per_right(t, carry):
            n, touched = carry
            at = begin + t
            col = col_right[at]
            o = first + col
            last = slot_of[o]
            fresh = last < 0
            job_left[n] = m
            job_right[n] = at - at // (cap_x + 1)
            job_last[n] = last
            job_col[n] = col
            job_col[jnp.where(fresh, jobs + 1, last)] = UNUSED
            slot_of[o] = n
            out_of[jnp.where(fresh, touched, OUT_TILES - 1)] = jnp.where(
                fresh, o, out_of[OUT_TILES - 1]
            )
            return n + 1, touched + fresh.astype(jnp.int32)

        return lax.fori_loop(0, count[q], per_right, carry)

    _, touched = lax.fori_loop(0, left_count, per_left, (jnp.int32(0), jnp.int32(0)))
    part["touched"][0] = touched


def make_lists(caps, lists, owner, sections, plan):
    cap_y, cap_left, cap_pair, cap_x, jobs = caps
    smem = lambda n: pltpu.SMEM((n,), jnp.int32)
    return pl.pallas_call(
        functools.partial(lists_kernel, caps),
        out_shape=jax.ShapeDtypeStruct((places(caps)[1],), jnp.int32),
        in_specs=[SMEM] * 4,
        out_specs=SMEM,
        scratch_shapes=[
            smem(cap_left + 8), smem(cap_left + 8), smem(PANEL), smem(PANEL), smem(4 * (cap_x + 1)),
        ],
        compiler_params=params(4),
    )(lists, owner, sections, plan)


UNROLL = 8


def gather_part(caps, keep_left, here, there, keep, strips, cand, left, right, held, other, send, recv):
    cap_y, cap_left, cap_pair, cap_x, jobs = caps
    r, c = lax.axis_index("row"), lax.axis_index("col")
    k = r % 2
    x = r // 4
    me = ((r // 2) % 2) * 2 + c % 2
    cz = c + 1 - 2 * (c % 2)
    rz = (r // 4) * 4 + (r + 2) % 4
    zp, zh, zx = {"col": cz}, {"row": rz}, {"row": rz, "col": cz}
    yn, yb = {"col": (c + 2) % COLS}, {"col": (c + COLS - 2) % COLS}
    core = {"row": r + 1 - 2 * k}
    xn, xb = {"row": (r + 4) % ROWS}, {"row": (r + ROWS - 4) % ROWS}
    part = cap_x // 2
    end = cap_left
    mid = end // 2
    c_m, c_p = (c + COLS - 2) % COLS, (c + 2) % COLS
    z_m, z_p = (cz + COLS - 2) % COLS, (cz + 2) % COLS
    x_m, x_p, x_o = (x + 3) % 4, (x + 1) % 4, (x + 2) % 4
    z_of_p, z_of_h = (me // 2) * 2 + (me + 1) % 2, (me + 2) % 4
    z_of_x = (z_of_p + 2) % 4
    started, done = [], []

    def push(src, dst, to):
        n = len(started)
        copy = pltpu.make_async_remote_copy(
            src, dst, send.at[n], recv.at[n], device_id=to, device_id_type=MESH
        )
        copy.start()
        started.append(copy)
        return copy

    def go(origin, a, b, to):
        piece = left.at[origin, pl.ds(a, b - a)]
        return push(piece, piece, to)

    def gz(origin, to):
        piece = held.at[origin, k]
        return push(piece, piece, to)

    def gx(origin, a, b, to):
        piece = right.at[origin, k, pl.ds(a, b - a)]
        return push(piece, piece, to)

    def arrived(*copies):
        for copy in copies:
            copy.wait_recv()
            done.append(copy)

    for m in range(cap_pair):
        e = there[m]
        other[m] = cand[e // cap_y, e % cap_y]
        e = here[m]
        held[me, k, m] = cand[e // cap_y, e % cap_y]
    s1 = push(other, held.at[me, k], zp)
    s2 = push(other, held.at[me, k], zx)
    s3 = gz(me, zh)
    t0 = gz(me, core)
    yield started

    def pack_left(m, _):
        for u in range(4):
            e = keep_left[m * 4 + u]
            left[c, m * 4 + u] = strips[e // ENTRIES, e % ENTRIES]
        return 0

    lax.fori_loop(0, cap_left // 4, pack_left, 0)
    k1a = go(c, 0, mid, zp)
    k2a = go(c, 0, mid, yn)
    k3b = go(c, mid, end, yb)
    k1b = go(c, mid, end, zp)
    k2b = go(c, mid, end, yn)
    k3a = go(c, 0, mid, yb)
    yield started
    arrived(s1)
    t1 = gz(z_of_p, core)
    arrived(s2)
    t2 = gz(z_of_x, core)
    arrived(s3)
    t3 = gz(z_of_h, core)
    arrived(t0, t1, t2, t3)
    for m in range(cap_x):
        e = keep[m]
        right[x, m // part, m % part] = held[e // (2 * cap_pair), (e // cap_pair) % 2, e % cap_pair]
    h = part // 2
    u1a = gx(x, 0, h, xn)
    u2b = gx(x, h, part, xb)
    u1b = gx(x, h, part, xn)
    u2a = gx(x, 0, h, xb)
    arrived(k2a)
    k6 = go(c_m, 0, mid, yn)
    arrived(k3b)
    k7 = go(c_p, mid, end, yb)
    arrived(k1a)
    k4a = go(cz, 0, mid, yn)
    arrived(k1b)
    k5b = go(cz, mid, end, yb)
    k4b = go(cz, mid, end, yn)
    k5a = go(cz, 0, mid, yb)
    arrived(u1a)
    u3 = gx(x_m, 0, h, xn)
    u4a = gx(x_m, 0, h, core)
    arrived(u2b)
    u5 = gx(x_p, h, part, xb)
    u6b = gx(x_p, h, part, core)
    arrived(k4a)
    k8 = go(z_m, 0, mid, yn)
    arrived(k5b)
    k9 = go(z_p, mid, end, yb)
    arrived(u1b)
    u4b = gx(x_m, h, part, core)
    arrived(u2a)
    u6a = gx(x_p, 0, h, core)
    arrived(u3)
    u7 = gx(x_o, 0, h, core)
    arrived(u5)
    u8 = gx(x_o, h, part, core)
    for copy in started:
        if not any(copy is seen for seen in done):
            copy.wait_recv()
    yield started


def product_part(
    caps, job_left, job_right, job_last, job_col, left, right, sums, totals, rows, parts,
    total_send, total_recv,
):
    cap_y, cap_left, cap_pair, cap_x, jobs = caps
    r = lax.axis_index("row")
    part = cap_x // 2
    rows[...] = jnp.zeros_like(rows)
    line = lax.broadcasted_iota(jnp.int32, (ROWS, TILE), 0)

    def multiply(g, _):
        results = []
        for u in range(UNROLL):
            n = g * UNROLL + u
            a = left[:, job_left[n]].reshape(TILE, TILE)
            e = job_right[n]
            b = right[e // cap_x, (e // part) % 2, e % part]
            results.append(jnp.dot(a, b, preferred_element_type=jnp.float32))
        added = jnp.zeros((ROWS, TILE), jnp.float32)
        for u in range(UNROLL):
            n = g * UNROLL + u
            last = job_last[n]
            old = sums[jnp.maximum(last, 0)]
            value = results[u] + jnp.where(last >= 0, old, 0.0)
            sums[n] = value
            square = (value * value).reshape(TILE // 8, 8, TILE).sum(axis=0)
            square = square.sum(axis=0, keepdims=True)
            added = added + jnp.where(line == job_col[n], square, 0.0)
        rows[...] += added
        return 0

    lax.fori_loop(0, jobs // UNROLL, multiply, 0)
    parts[r] = rows[...]
    copies = []
    for d in range(1, ROWS):
        copy = pltpu.make_async_remote_copy(
            rows, parts.at[r], total_send.at[d], total_recv.at[d],
            device_id={"row": (r + d) % ROWS}, device_id_type=MESH,
        )
        copy.start()
        copies.append(copy)
    for copy in copies:
        copy.wait_recv()
    totals[...] = parts[...].sum(axis=0)
    return copies


def multiply_kernel(
    caps, strips, cand, plan, sums, totals,
    left, right, held, other, rows, parts, send, recv, total_send, total_recv,
):
    greet(lax.axis_index("row"), lax.axis_index("col"))
    found = {name: Part(plan, base) for name, base in places(caps)[0].items()}
    meet()
    steps = gather_part(
        caps, found["left"], found["here"], found["there"], found["keep"],
        strips, cand, left, right, held, other, send, recv,
    )
    for _ in range(2):
        next(steps)
    started = next(steps)
    started += product_part(
        caps, found["job_left"], found["job_right"], found["job_last"], found["job_col"],
        left, right, sums, totals, rows, parts, total_send, total_recv,
    )
    for copy in started:
        copy.wait_send()


COPIES = 33


def multiply_scratch(caps):
    cap_y, cap_left, cap_pair, cap_x, jobs = caps
    bf, f32 = jnp.bfloat16, jnp.float32
    dma = pltpu.SemaphoreType.DMA
    return (
        [
            pltpu.VMEM((COLS, cap_left, STRIP, TILE), bf),
            pltpu.VMEM((4, 2, cap_x // 2, TILE, TILE), bf),
            pltpu.VMEM((4, 2, cap_pair, TILE, TILE), bf),
            pltpu.VMEM((cap_pair, TILE, TILE), bf),
            pltpu.VMEM((ROWS, TILE), f32),
            pltpu.VMEM((ROWS, ROWS, TILE), f32),
        ]
        + [dma((COPIES,))] * 2
        + [dma((ROWS,))] * 2
    )


def multiply(caps, collective_id, strips, cand, plan):
    jobs, f32 = caps[4], jnp.float32
    mib = 24 + jobs * TILE * TILE * 4 // (1 << 20)
    return pl.pallas_call(
        functools.partial(multiply_kernel, caps),
        out_shape=(
            jax.ShapeDtypeStruct((jobs, TILE, TILE), f32),
            jax.ShapeDtypeStruct((ROWS, TILE), f32),
        ),
        in_specs=[VMEM, VMEM, SMEM],
        out_specs=(VMEM, VMEM),
        scratch_shapes=multiply_scratch(caps),
        compiler_params=params(mib, collective_id=collective_id, has_side_effects=True),
    )(strips, cand, plan)


def vector_prep(cap_y, owner, idx, sections, r, c):
    i32 = jnp.int32
    line = lax.broadcasted_iota(i32, (ROWS, TILE), 0)
    lane = lax.broadcasted_iota(i32, (ROWS, TILE), 1)
    blocks = [jnp.broadcast_to(owner[h : h + 1, :] >> 4, (ROWS, TILE)) for h in range(2)]
    who = jnp.zeros((ROWS, 1), i32)
    own = [jnp.zeros((ROWS, 1), i32) for _ in range(2)]
    for h in range(2):
        t = lane + h * TILE
        hit = (blocks[h] == line) & ((t >> 4) == r)
        who = who + jnp.where(hit, lane & (ROWS - 1), 0).sum(axis=1, keepdims=True)
        for i in range(2):
            hit = t == r * ROWS + c * 2 + i
            own[i] = own[i] + jnp.where(hit, blocks[h], 0).sum(axis=1, keepdims=True)
    sec0, sec1 = sections[0], sections[1]
    mine = jnp.where(lane < BLOCK_COLS, own[0], own[1])
    b = (lane & (BLOCK_COLS - 1)) >> 2
    rel = jnp.broadcast_to(idx[...], (ROWS, TILE)) - b * BLOCK_COLS
    ok = (lane < 2 * BLOCK_COLS) & (rel >= 0) & (rel < SLAB) & ((mine == sec0) | (mine == sec1))
    ok = ok & ((b >> 1) == line)
    rank = mm(picked(ok), picked(iota(0) < iota(1))).astype(i32)
    rank = jnp.where(ok, rank, -1)
    plan = jnp.where(lane == TILE - 1, jnp.clip(who, 0, ROWS - 1), 0)
    for m in range(cap_y):
        at = jnp.where(rank == m, lane, 0).sum(axis=1, keepdims=True)
        at = jnp.clip(at, 0, 2 * BLOCK_COLS - 1)
        plan = jnp.where(lane == m, at, plan)
    return plan


class Row:
    def __init__(self, ref, row):
        self.ref, self.row = ref, row

    def __getitem__(self, i):
        return self.ref[self.row, i]


def whole_kernel(
    caps, values, idx, owner, sections,
    sums, totals, made, over,
    tv, strips, cand, lists, early, places_of, scalars, value_sem, plan_sem, *scratch,
):
    r, c = lax.axis_index("row"), lax.axis_index("col")
    greet(r, c)
    load = pltpu.make_async_copy(values, tv, value_sem)
    load.start()
    early[...] = vector_prep(caps[0], owner, idx, sections, r, c)
    move = pltpu.make_async_copy(early, places_of, plan_sem)
    move.start()
    move.wait()
    load.wait()
    first, second = scratch[:14], scratch[14:]
    left, right, held, other, rows, parts, send, recv, total_send, total_recv = second
    row = lambda n: Row(scalars, n)
    steps = gather_part(
        caps, row(ROW_LEFT), row(ROW_HERE), row(ROW_THERE), row(ROW_KEEP),
        strips, cand, left, right, held, other, send, recv,
    )

    def on_lists():
        found, excess = vector_plan(caps, lists, owner, sections, r, c)
        made[...] = found
        over[...] = jnp.broadcast_to(excess.max(axis=0, keepdims=True), (8, TILE))
        move = pltpu.make_async_copy(made, scalars, plan_sem)
        move.start()
        move.wait()

    started = spread_part(
        caps[0], tv, idx, sections,
        lambda yd, m: places_of[yd, m], lambda t: places_of[t, TILE - 1],
        strips, cand, lists, *first,
        meet, on_lists, *[lambda: next(steps)] * 2,
    )
    started = started + next(steps)
    started += product_part(
        caps, row(ROW_JOB), row(ROW_TILE), row(ROW_LAST), row(ROW_COL),
        left, right, sums, totals, rows, parts, total_send, total_recv,
    )
    for copy in started:
        copy.wait_send()


def whole(caps, collective_id, tv, idx, owner, sections):
    bf, f32, i32 = jnp.bfloat16, jnp.float32, jnp.int32
    dma = pltpu.SemaphoreType.DMA
    return pl.pallas_call(
        functools.partial(whole_kernel, caps),
        out_shape=(
            jax.ShapeDtypeStruct((caps[4], TILE, TILE), f32),
            jax.ShapeDtypeStruct((ROWS, TILE), f32),
            jax.ShapeDtypeStruct((ROWS, TILE), i32),
            jax.ShapeDtypeStruct((8, TILE), f32),
        ),
        in_specs=[HBM, VMEM, VMEM, SMEM],
        out_specs=(VMEM,) * 4,
        scratch_shapes=[
            pltpu.VMEM((2 * COLS * KB, TILE, TILE), bf),
            pltpu.VMEM((ROWS, ENTRIES, STRIP, TILE), bf),
            pltpu.VMEM((4, caps[0], TILE, TILE), bf),
            pltpu.VMEM((ROWS, COLS, 1, TILE), i32),
            pltpu.VMEM((ROWS, TILE), i32),
            pltpu.SMEM((ROWS, TILE), i32),
            pltpu.SMEM((ROWS, TILE), i32),
            dma,
            dma,
        ]
        + spread_scratch(caps[0])
        + multiply_scratch(caps),
        compiler_params=params(24, collective_id=collective_id, has_side_effects=True),
    )(tv, idx, owner, sections)


def write_listed_kernel(jobs, sums, plan, totals, out, block, factor, zeros, zero_sem, out_sem):
    zeros[...] = jnp.zeros_like(zeros)
    clears = [
        pltpu.make_async_copy(zeros, out.at[pl.ds(p * TILE, TILE)], zero_sem.at[p])
        for p in range(ROWS)
    ]
    for copy in clears:
        copy.start()
    count = float(ROWS * ROWS * TILE)
    factor[...] = count / (totals[...] + 1e-06)

    def scale(n, _):
        o = plan[ROW_OUT, n]

        @pl.when(o >= 0)
        def _():
            value = sums[n]
            col = o - o // SLAB * SLAB
            block[n] = (value * value * factor[pl.ds(col, 1), :]).astype(jnp.bfloat16)

        return 0

    lax.fori_loop(0, jobs, scale, 0)
    for copy in clears:
        copy.wait()

    def place(n, o):
        p = o // SLAB
        col = o - p * SLAB
        row = pl.ds(pl.multiple_of(p * TILE, TILE), TILE)
        lanes = pl.ds(pl.multiple_of(col * TILE, TILE), TILE)
        return pltpu.make_async_copy(block.at[n], out.at[row, lanes], out_sem)

    def send(n, _):
        o = plan[ROW_OUT, n]

        @pl.when(o >= 0)
        def _():
            place(n, o).start()

        return 0

    lax.fori_loop(0, jobs, send, 0)

    def drain(n, _):
        o = plan[ROW_OUT, n]

        @pl.when(o >= 0)
        def _():
            place(n, o).wait()

        return 0

    lax.fori_loop(0, jobs, drain, 0)


def write_listed(jobs, sums, plan, totals):
    return pl.pallas_call(
        functools.partial(write_listed_kernel, jobs),
        out_shape=jax.ShapeDtypeStruct((ROWS * TILE, SLAB * TILE), jnp.bfloat16),
        in_specs=[VMEM, SMEM, VMEM],
        out_specs=ANY,
        scratch_shapes=[
            pltpu.VMEM((jobs, TILE, TILE), jnp.bfloat16),
            pltpu.VMEM((ROWS, TILE), jnp.float32),
            pltpu.VMEM((TILE, SLAB * TILE), jnp.bfloat16),
            pltpu.SemaphoreType.DMA((ROWS,)),
            pltpu.SemaphoreType.DMA,
        ],
        compiler_params=params(12),
    )(sums, plan, totals)


def write_kernel(at, sums, blank, plan, totals, out, block, factor, out_sem):
    touched = plan[at["touched"]]
    count = float(ROWS * ROWS * TILE)
    factor[...] = count / (totals[...] + 1e-06)

    def place(i):
        o = plan[at["out"] + i]
        p = o // SLAB
        col = o - p * SLAB
        row = pl.ds(pl.multiple_of(p * TILE, TILE), TILE)
        lanes = pl.ds(pl.multiple_of(col * TILE, TILE), TILE)
        return o, col, pltpu.make_async_copy(block.at[i], out.at[row, lanes], out_sem)

    def scale(i, _):
        o, col, copy = place(i)
        value = sums[plan[at["slot"] + o]]
        block[i] = (value * value * factor[pl.ds(col, 1), :]).astype(jnp.bfloat16)
        copy.start()
        return 0

    lax.fori_loop(0, touched, scale, 0)

    def drain(i, _):
        place(i)[2].wait()
        return 0

    lax.fori_loop(0, touched, drain, 0)


def write(caps, sums, blank, plan, totals):
    jobs = caps[4]
    mib = 10 + jobs * TILE * TILE * 4 // (1 << 20)
    return pl.pallas_call(
        functools.partial(write_kernel, places(caps)[0]),
        out_shape=jax.ShapeDtypeStruct((ROWS * TILE, SLAB * TILE), jnp.bfloat16),
        in_specs=[VMEM, ANY, SMEM, VMEM],
        out_specs=ANY,
        input_output_aliases={1: 0},
        scratch_shapes=[
            pltpu.VMEM((OUT_TILES, TILE, TILE), jnp.bfloat16),
            pltpu.VMEM((ROWS, TILE), jnp.float32),
            pltpu.SemaphoreType.DMA,
        ],
        compiler_params=params(mib),
    )(sums, blank, plan, totals)


def per_device(tile_values, tile_columns, owner_map, section_rows):
    flat = tile_columns.reshape(-1)
    idx = jnp.pad(flat, (0, TILE - flat.shape[0])).reshape(1, TILE)
    tv = tile_values.reshape(2 * COLS * KB, TILE, TILE)
    owner_rows = owner_map.reshape(2, TILE)

    sums, totals, made, over = whole(FAST, 0, tv, idx, owner_rows, section_rows)

    out = write_listed(FAST[4], sums, made, totals)

    def full(state):
        plan, blank = prep(FULL[0], owner_map, section_rows, flat)
        strips, cand, lists = spread(FULL[0], 2, tv, idx, section_rows, plan)
        made = make_lists(FULL, lists.reshape(ROWS * COLS, TILE), owner_map, section_rows, plan)
        sums, totals = multiply(FULL, 3, strips, cand, made)
        return jnp.float32(0), write(FULL, sums, blank, made, totals)

    return lax.while_loop(lambda state: state[0] > 0, full, (jnp.max(over), out))[1]


def solution(mesh):
    both = ("row", "col")
    in_specs = (P(both, None, None, None, None), P(both, None, None), P(), P())
    return jax.shard_map(
        per_device, mesh=mesh, in_specs=in_specs, out_specs=P("row", "col"), check_vma=False
    )
```
